32 devices in a mesh: groups: 2 (over x), row: 4 (over y, core), col: 4 (over z).
Axes of the slice: x: 2, y: 2, z: 4, core: 2. Of those that a mesh axis runs over, the one named last changes fastest.
Arguments:
- noise_field: float32 [3, 2, 4096], P(None, None, ('groups', 'row', 'col')), parts along dimension 2, may hold values from -6 to 6
- offsets: int32 [3, 4096], P(None, ('groups', 'row', 'col')), parts along dimension 1, may hold values from 0 to 7
- tile_list: int32 [8, 4, 2, 2], P(('groups', 'row'), 'col'), parts along dimension 0, may hold values from -1 to 3, as said below
- send_cells: int32 [8, 4, 16, 16], P(('groups', 'row'), 'col'), parts along dimension 0, may hold values from 0 to 131071, as said below
- bead_slot: int32 [4096], P(('groups', 'row', 'col')), parts along dimension 0, may hold values from 0 to 255, as said below
- spectral: float32 [2, 3, 2, 256, 128, 128], P(None, None, None, ('groups', 'row'), 'col'), parts along dimension 3, may hold values from -6 to 6
Outputs:
- velocity: float32 [3, 2, 4096], P(None, None, ('groups', 'row', 'col')), parts along dimension 2
The draws below stay inside these ranges and needn't reach their ends.
There are 2 independent parts, one for each index of `groups`. The reference program is written for one: setup_inputs(seed, part) draws one part's arguments, and reference() takes and returns one part's arrays. A program takes and returns all parts, laid end to end along the dimension named above; each array names one. Nothing has to cross between parts.
Inputs may be any that keep to these rules, and one draw needn't show every extreme that they name: `tile_list`: for each device the first slots name distinct (row tile, column tile) pairs with row tile below 4 and column tile below 4; the remaining slots hold -1 in both entries. Some device uses all 2 slots, some device fewer. `send_cells`: entries are local cell indices of the holder's block of 128 x 32 x 32 cells, first dimension slowest. `bead_slot`: within one owner's 128 beads no value repeats, so a holder serves one owner through at most 16 slots; every owner takes all 16 slots of one holder.
All inputs are finite; a program needn't handle non-finite values.
Results may differ from the reference program's by a relative error of at most 0.0039.
Values may be sent and summed in bfloat16 or wider, within the bound.
A program may use at most 128 MiB of HBM per device.

```python
import math
import jax
import jax.numpy as jnp
from jax import lax

MONOMER_PER_UNIT = 128
NVEC = 2
TB = 128
G = 128
PERIOD = 8
SHARING_UNITS = 16
NB = 2048
RT = 4
CT = 4
SLOTS = 2
CAP = 16
YSLAB = 32
ZSLAB = 32
N_ROW = 4
N_COL = 4


def draw_tile_list(key, part):
    divided_seeds = jax.random.split(jax.random.fold_in(key, 11), 4)
    device_ids = jnp.arange(SHARING_UNITS, dtype=jnp.int32)
    message_batches = jax.random.randint(divided_seeds[0], (SHARING_UNITS,), 0, 8)
    coarsest_tier = jax.random.randint(divided_seeds[1], (SHARING_UNITS,), 1, 4)
    tier_sequence = jnp.where(message_batches == 0, 8, coarsest_tier)
    full_device = jax.random.randint(divided_seeds[2], (), 0, SHARING_UNITS)
    tier_sequence = jnp.where(device_ids == full_device, 8, tier_sequence)
    tier_sequence = jnp.where(device_ids == (full_device + 1) % SHARING_UNITS, 1, tier_sequence)
    counts = jnp.maximum(1, SLOTS * tier_sequence // 8)
    pair_ids = jnp.arange(RT * CT, dtype=jnp.int32)
    slot_ids = jnp.arange(SLOTS, dtype=jnp.int32)

    def per_device(subkey, device, limit):
        scores = jax.random.permutation(subkey, RT * CT)
        scores = jnp.where((device == full_device) & (pair_ids == RT * CT - 1), -1, scores)
        ranked = jnp.argsort(scores)[:SLOTS]
        active = slot_ids < limit
        return jnp.stack([jnp.where(active, ranked // CT, -1), jnp.where(active, ranked % CT, -1)])
    final_output = jax.vmap(per_device)(jax.random.split(divided_seeds[3], SHARING_UNITS), device_ids, counts)
    return final_output.reshape(N_ROW, N_COL, 2, SLOTS).astype(jnp.int32)


def draw_send_cells(key, part):
    cell_count = G * YSLAB * ZSLAB
    values = jax.random.randint(jax.random.fold_in(key, 23), (N_ROW, N_COL, CAP, SHARING_UNITS), 0, cell_count)
    position = jnp.arange(N_ROW * N_COL * CAP * SHARING_UNITS, dtype=jnp.int32).reshape(N_ROW, N_COL, CAP, SHARING_UNITS)
    values = jnp.where(position == 0, cell_count - 1, jnp.where(position == 1, 0, values))
    return values.astype(jnp.int32)


def draw_bead_slot(key, part):
    divided_seeds = jax.random.split(jax.random.fold_in(key, 37), 2)
    rotate = jax.random.randint(divided_seeds[0], (), 0, SHARING_UNITS)
    owners = jnp.arange(SHARING_UNITS, dtype=jnp.int32)
    full_holder = (owners + rotate) % SHARING_UNITS
    code_ids = jnp.arange(SHARING_UNITS * CAP, dtype=jnp.int32)

    def by_holding_unit(subkey, holder):
        scores = jax.random.permutation(subkey, SHARING_UNITS * CAP)
        scores = jnp.where(code_ids % SHARING_UNITS == holder, code_ids // SHARING_UNITS - CAP, scores)
        return jnp.argsort(scores)[:MONOMER_PER_UNIT]
    final_output = jax.vmap(by_holding_unit)(jax.random.split(divided_seeds[1], SHARING_UNITS), full_holder)
    return final_output.reshape(-1).astype(jnp.int32)


def place_ends(result, stream_key, smallest, high):
    dims = result.shape
    place = [jax.random.randint(jax.random.fold_in(stream_key, axis), (), 0, dims[axis]) for axis in range(len(dims))]
    result = result.at[tuple(place)].set(smallest)
    longest = dims.index(max(dims))
    place[longest] = (place[longest] + 1) % dims[longest]
    return result.at[tuple(place)].set(high)


def block_levels(stream_key, dims, cuts, smallest, high):
    gain = 1.0
    for axis_at, shards_of in cuts:
        steps = jax.random.uniform(jax.random.fold_in(jax.random.fold_in(stream_key, 6), axis_at), (shards_of,), jnp.float32, smallest / len(cuts), high / len(cuts))
        gain = gain * jnp.repeat(jnp.exp(steps), dims[axis_at] // shards_of).reshape((-1,) + (1,) * (len(dims) - 1 - axis_at))
    return gain


def centred(rng, dims, scale, most, shards=(), kind=jnp.bfloat16):
    values = scale * jax.random.normal(rng, dims, jnp.float32)
    if shards:
        values = values * block_levels(rng, dims, shards, -0.22, 0.18)
    return jnp.clip(values, -most, most).astype(kind)


def setup_inputs(seed: int = 0, part: int = 0) -> dict:
    arg_keys = jax.random.split(jax.random.key(seed), 7)
    part_splits = jax.random.split(jax.random.fold_in(arg_keys[6], part), 7)
    noise_field = centred(part_splits[0], (3, NVEC, NB), 1.0, 6.0, ((2, 16),), jnp.float32)
    offsets = place_ends(jax.random.randint(part_splits[1], (3, NB), 0, PERIOD), jax.random.fold_in(part_splits[1], 1), 0, PERIOD - 1).astype(jnp.int32)
    tile_list = draw_tile_list(jax.random.fold_in(jax.random.fold_in(arg_keys[6], part), 71), part)
    send_cells = draw_send_cells(jax.random.fold_in(jax.random.fold_in(arg_keys[6], part), 71), part)
    bead_slot = draw_bead_slot(jax.random.fold_in(jax.random.fold_in(arg_keys[6], part), 71), part)
    spectral = centred(part_splits[5], (2, 3, NVEC, G, G, G), 1.0, 6.0, ((3, 4), (4, 4)), jnp.float32)
    return dict(noise_field=noise_field, offsets=offsets, tile_list=tile_list, send_cells=send_cells, bead_slot=bead_slot, spectral=spectral)


cheb_coef = (1.0, 0.45, -0.2, 0.12, -0.08)
kernel_range = 1.5

def kernel_parts(displace):
    squares = displace[0] * displace[0] + displace[1] * displace[1] + displace[2] * displace[2]
    scale_sq = kernel_range * kernel_range
    envelope = jnp.exp(squares * (-0.5 / scale_sq)) / scale_sq
    entries = []
    for left_comp in range(3):
        for right_comp in range(3):
            element = displace[left_comp] * displace[right_comp]
            if left_comp == right_comp:
                element = element - squares / 3.0
            entries.append(envelope * element)
    return jnp.stack(entries)

def kernel_lookup():
    half_period = PERIOD // 2
    code_ids = jnp.arange(PERIOD ** 3, dtype=jnp.int32)
    shifted = jnp.stack([code_ids // (PERIOD * PERIOD), code_ids // PERIOD % PERIOD, code_ids % PERIOD])
    return kernel_parts((shifted - half_period).astype(jnp.float32)).astype(jnp.bfloat16)

def device_tiles(device, offsets, tile_list, lookup):
    row_idx = device // N_COL
    col_idx = device % N_COL
    tile_rows = tile_list[row_idx, col_idx, 0]
    tile_cols = tile_list[row_idx, col_idx, 1]
    active = tile_rows >= 0
    safe_rows = jnp.maximum(tile_rows, 0)
    safe_cols = jnp.maximum(tile_cols, 0)
    lane_ids = jnp.arange(TB, dtype=jnp.int32)
    row_beads = row_idx * N_COL * MONOMER_PER_UNIT + safe_rows[:, None] * TB + lane_ids[None, :]
    local_cols = safe_cols[:, None] * TB + lane_ids[None, :]
    col_beads = local_cols // MONOMER_PER_UNIT * N_COL * MONOMER_PER_UNIT + col_idx * MONOMER_PER_UNIT + local_cols % MONOMER_PER_UNIT
    half_period = PERIOD // 2
    shifted = (offsets[:, row_beads][:, :, :, None] - offsets[:, col_beads][:, :, None, :] + half_period) % PERIOD
    code_ids = (shifted[0] * PERIOD + shifted[1]) * PERIOD + shifted[2]
    kernel_tiles = lookup[:, code_ids].reshape(3, 3, SLOTS, TB, TB)
    selector = ((tile_rows[:, None] == jnp.arange(RT, dtype=jnp.int32)[None, :]) & active[:, None]).astype(jnp.float32)
    return (kernel_tiles, selector, col_beads)

def combine(partials):
    lead_shape = partials.shape[1:-1]
    grouped = partials.reshape((N_ROW, N_COL) + lead_shape + (N_COL * MONOMER_PER_UNIT,)).sum(axis=1)
    regrouped = jnp.moveaxis(grouped, 0, -2)
    return regrouped.reshape(lead_shape + (NB,))

def row_energy(offsets, tile_list, lookup):

    def per_device(device):
        kernel_tiles, selector, col_beads = device_tiles(device, offsets, tile_list, lookup)
        squared = lax.optimization_barrier(jnp.sum(jnp.square(kernel_tiles.astype(jnp.float32)), axis=(1, 4)))
        return jnp.einsum('asp,si->aip', squared, selector, precision=lax.Precision.HIGHEST).reshape(3, RT * TB)
    return combine(lax.map(per_device, jnp.arange(SHARING_UNITS, dtype=jnp.int32)))

def near_apply(vector, offsets, tile_list, lookup):
    rounded = vector.astype(jnp.bfloat16)

    def per_device(device):
        kernel_tiles, selector, col_beads = device_tiles(device, offsets, tile_list, lookup)
        pieces = rounded[:, :, col_beads].astype(jnp.float32)
        blocks = jnp.einsum('abspq,bksq->aksp', kernel_tiles.astype(jnp.float32), pieces, precision=lax.Precision.HIGHEST)
        return jnp.einsum('aksp,si->akip', blocks, selector, precision=lax.Precision.HIGHEST).reshape(3, NVEC, RT * TB)
    return combine(lax.map(per_device, jnp.arange(SHARING_UNITS, dtype=jnp.int32)))

def far_grid(spectral):
    wave_ids = jnp.arange(G, dtype=jnp.int32)
    signed = jnp.where(wave_ids < G // 2, wave_ids, wave_ids - G).astype(jnp.float32)
    wave_x = signed[:, None, None]
    wave_y = signed[None, :, None]
    wave_z = signed[None, None, :]
    wave_sq = wave_x * wave_x + wave_y * wave_y + wave_z * wave_z
    width_sq = (G / 8.0) ** 2
    amplitude = jnp.where(wave_sq > 0, math.sqrt(1.5) / (2.0 * math.pi * width_sq) ** 0.75 * jnp.exp(wave_sq * (-0.25 / width_sq)), 0.0)

    def project(source_field):
        along_k = wave_x * source_field[0] + wave_y * source_field[1] + wave_z * source_field[2]
        factor = along_k / jnp.maximum(wave_sq, 1.0)
        return jnp.stack([amplitude * (source_field[0] - wave_x * factor), amplitude * (source_field[1] - wave_y * factor), amplitude * (source_field[2] - wave_z * factor)])
    real_part = project(spectral[0])
    imag_part = project(spectral[1])
    inverse = jnp.fft.ifftn(real_part + 1j * imag_part, axes=(-3, -2, -1))
    return jnp.real(inverse) * G ** 3

def reference(noise_field, offsets, tile_list, send_cells, bead_slot, spectral):
    lookup = kernel_lookup()
    energy = row_energy(offsets, tile_list, lookup)
    scaling = 1.0 / jnp.sqrt(jnp.max(energy) + 1e-06)
    previous = noise_field
    current = scaling * near_apply(noise_field, offsets, tile_list, lookup)
    near_field = cheb_coef[0] * previous + cheb_coef[1] * current
    for degree in range(2, 5):
        following = 2.0 * (scaling * near_apply(current, offsets, tile_list, lookup)) - previous
        near_field = near_field + cheb_coef[degree] * following
        previous, current = (current, following)
    grid_field = far_grid(spectral)
    owner_ids = jnp.arange(NB, dtype=jnp.int32) // MONOMER_PER_UNIT
    source = bead_slot % SHARING_UNITS
    slot_idx = bead_slot // SHARING_UNITS
    src_row = source // N_COL
    src_col = source % N_COL
    cell_ids = send_cells[src_row, src_col, slot_idx, owner_ids]
    pos_x = cell_ids // (YSLAB * ZSLAB)
    pos_y = src_row * YSLAB + cell_ids // ZSLAB % YSLAB
    pos_z = src_col * ZSLAB + cell_ids % ZSLAB
    far_field = grid_field[:, :, pos_x, pos_y, pos_z]
    return near_field + far_field
```

```python
import functools
import math

import jax
import jax.numpy as jnp
import ml_dtypes
import numpy as np
from jax import lax
from jax.experimental import pallas as pl
from jax.experimental.pallas import tpu as pltpu
from jax.sharding import PartitionSpec as P

TB = 128
LANES = 128
PERIOD = 8
DEGREES = 4

cheb_coef = (1.0, 0.45, -0.2, 0.12, -0.08)
kernel_range = 1.5

f32 = jnp.float32
bf16 = jnp.bfloat16


def iota(shape, dim):
    return lax.broadcasted_iota(jnp.int32, shape, dim)


def over(n, d):
    return lax.shift_right_logical(n, jnp.full(n.shape, d.bit_length() - 1, jnp.int32))


def dot(a, b):
    return jnp.dot(a, b, preferred_element_type=f32)


def dot_nt(a, b):
    return lax.dot_general(a, b, (((1,), (1,)), ((), ())), preferred_element_type=f32)


def cos_turn(turns):
    x = jnp.abs(turns - jnp.floor(turns) - 0.5) * 4.0 - 1.0
    x2 = x * x
    p = 0.00015148419
    for c in (-0.00467376557, 0.07968967928, -0.64596371106, 1.57079631847):
        p = p * x2 + c
    return p * x


def kernel(
    dims,
    tiles_ref, noise_ref, off_ref, slot_ref, cells_ref, spec_hbm,
    out_ref,
    spec, pre, hat, phase, ang, wang, tabf, tab, kmat,
    a_send, a_recv, b_send, row_b, col_b,
    e_send, e_recv, y_send, y_recv, far_send, far_recv,
    cur, prev, acc, scale,
    spec_sem, a_ss, a_rs, b_ss, b_rs, e_ss, e_rs, y_ss, y_rs, far_ss, far_rs,
):
    n_row, n_col, slots, xs, ys, glen, cap = dims
    nd = n_row * n_col
    xy = xs * ys
    cr = cap * nd // LANES
    kq = tab.shape[0]
    beads = n_col * TB
    me_r = lax.axis_index("row")
    me_c = lax.axis_index("col")
    me = me_r * n_col + me_c
    chunks = spec_sem.shape[0]
    part = xy // chunks
    per_row = LANES // nd

    def spec_copy(i):
        rows = pl.ds(i * part, part)
        return pltpu.make_async_copy(
            spec_hbm.at[:, rows, :], spec.at[:, rows, :], spec_sem.at[i]
        )

    for i in range(chunks):
        spec_copy(i).start()

    straight = nd <= 32
    if straight:
        rows_of = [me_r] + [lax.rem(me_r + d, n_row) for d in range(1, n_row)]
        cols_of = [me_c] + [lax.rem(me_c + d, n_col) for d in range(1, n_col)]
        order = sorted(
            [(i, j) for i in range(n_row) for j in range(n_col) if i + j],
            key=lambda t: (abs(t[1] - n_col // 2), abs(t[0] - n_row // 2)),
        )

    def each(body):
        if straight:
            for i, j in order:
                body(rows_of[i], cols_of[j])
            return

        def turn(d, carry):
            body(lax.rem(me_r + d // n_col, n_row), lax.rem(me_c + lax.rem(d, n_col), n_col))
            return carry

        lax.fori_loop(1, nd, turn, 0)

    def each_row(body):
        if straight:
            for d in range(1, n_row):
                body(rows_of[d])
        else:
            lax.fori_loop(1, n_row, lambda d, t: (body(lax.rem(me_r + d, n_row)), t)[1], 0)

    def each_col(body):
        if straight:
            for d in range(1, n_col):
                body(cols_of[d])
        else:
            lax.fori_loop(1, n_col, lambda d, t: (body(lax.rem(me_c + d, n_col)), t)[1], 0)

    barrier = pltpu.get_barrier_semaphore()

    def greet(r, c):
        pl.semaphore_signal(
            barrier, inc=1, device_id={"row": r, "col": c},
            device_id_type=pl.DeviceIdType.MESH,
        )

    each(greet)

    def remote(src, dst, ss, rs, r, c):
        return pltpu.make_async_remote_copy(
            src_ref=src, dst_ref=dst, send_sem=ss, recv_sem=rs,
            device_id={"row": r, "col": c}, device_id_type=pl.DeviceIdType.MESH,
        )

    def packed_cells():
        flat = cells_ref[...].astype(f32)
        if per_row == 1:
            return flat
        spread = (iota((nd, LANES), 1) & (nd - 1)) == iota((nd, LANES), 0)
        wide = jnp.dot(
            flat, spread.astype(f32), precision=lax.Precision.HIGHEST,
            preferred_element_type=f32,
        )
        mine = over(iota((cap, LANES), 1), nd) == (iota((cap, LANES), 0) & (per_row - 1))
        return jnp.sum(jnp.where(mine, wide, 0.0).reshape(cr, per_row, LANES), axis=1)

    a_send[0:1, :] = slot_ref[...].astype(f32)
    cells = packed_cells()
    a_send[1 : 1 + cr, :] = cells
    a_recv[me, 0:1, :] = slot_ref[...].astype(f32)
    a_recv[me, 1 : 1 + cr, :] = cells
    own_noise = jnp.concatenate([noise_ref[0], noise_ref[1], noise_ref[2]], axis=1)
    off = off_ref[...].astype(f32)
    own_off = jnp.concatenate([off[0:1], off[1:2], off[2:3]], axis=1)
    b_send[0:2, :] = own_noise
    b_send[2:3, :] = own_off
    row_b[me_c, 0:2, :] = own_noise
    row_b[me_c, 2:3, :] = own_off
    col_b[me_r, 0:2, :] = own_noise
    col_b[me_r, 2:3, :] = own_off
    tabf[...] = jnp.zeros_like(tabf)

    pl.semaphore_wait(barrier, nd - 1)

    def b_row_copy(c):
        return remote(b_send, row_b.at[me_c], b_ss.at[c], b_rs.at[me_c], me_r, c)

    def b_col_copy(r):
        return remote(
            b_send, col_b.at[me_r], b_ss.at[n_col + r], b_rs.at[n_col + me_r], r, me_c
        )

    each_col(lambda c: b_row_copy(c).start())
    each_row(lambda r: b_col_copy(r).start())

    def a_copy(r, c):
        p = r * n_col + c
        return remote(a_send, a_recv.at[me], a_ss.at[p], a_rs.at[me], r, c)

    each(lambda r, c: a_copy(r, c).start())

    gi = iota((2 * glen, 2 * glen), 0)
    gj = iota((2 * glen, 2 * glen), 1)
    zi, zj = gi & (glen - 1), gj & (glen - 1)
    in_im, out_im = gi >= glen, gj >= glen
    half = glen // 2
    same = zi == zj
    mirror = (zi + zj == glen) & (zi != zj)
    even = zj <= half
    plain = in_im == out_im
    fold = jnp.where(
        even,
        jnp.where(plain & (same | mirror), 1.0, 0.0),
        jnp.where(
            plain,
            0.0,
            jnp.where(same, 1.0, 0.0) - jnp.where(mirror, 1.0, 0.0),
        )
        * jnp.where(out_im, -1.0, 1.0),
    ).astype(bf16)

    width_sq = (glen / 8.0) ** 2
    front = math.sqrt(1.5) / (2.0 * math.pi * width_sq) ** 0.75
    def signed(n):
        return jnp.where(n < half, n, n - glen).astype(f32)

    ky = signed(me_c * ys + iota((ys, glen), 0))
    kz = signed(iota((ys, glen), 1))
    kyz_sq = ky * ky + kz * kz

    def hat_block(i, first):
        kx = signed(me_r * xs + i)
        q = kx * kx + kyz_sq
        amp = jnp.where(q > 0, front * jnp.exp(q * (-0.25 / width_sq)), 0.0)
        damp = amp / jnp.maximum(q, 1.0)
        rows = pl.ds(pl.multiple_of(i * ys, ys), ys)
        at = pl.multiple_of((i - first) * ys, ys)
        waves = (kx, ky, kz)
        for v in range(2):
            for p in range(2):
                s = [spec[(p * 3 + a) * 2 + v, rows, :] for a in range(3)]
                along = (kx * s[0] + ky * s[1] + kz * s[2]) * damp
                for a in range(3):
                    pre[pl.ds((a * 2 + v) * part + at, ys), p * glen : (p + 1) * glen] = (
                        amp * s[a] - waves[a] * along
                    ).astype(bf16)
        return first

    per = part // ys
    for i in range(chunks):
        spec_copy(i).wait()
        lax.fori_loop(i * per, (i + 1) * per, hat_block, i * per)
        folded = dot(pre[...], fold)
        for k in range(6):
            for p in range(2):
                hat[
                    p * xy + i * part : p * xy + (i + 1) * part, k * glen : (k + 1) * glen
                ] = folded[
                    k * part : (k + 1) * part, p * glen : (p + 1) * glen
                ].astype(bf16)

    def b_col_arrive(r):
        remote(b_send, col_b.at[r], b_ss.at[n_col + r], b_rs.at[n_col + r], r, me_c).wait_recv()

    def b_row_arrive(c):
        remote(b_send, row_b.at[c], b_ss.at[c], b_rs.at[c], me_r, c).wait_recv()

    each_row(b_col_arrive)
    each_col(b_row_arrive)

    eye = (iota((TB, TB), 0) == iota((TB, TB), 1)).astype(f32)
    ones = jnp.ones((TB, TB), bf16)
    scale_sq = kernel_range * kernel_range

    def pick(values, into, s):
        tr = tiles_ref[0, s]
        return tuple(
            into[i] + values * jnp.where(tr == i, 1.0, 0.0).astype(f32) for i in range(n_col)
        )

    def build(s, energies):
        tr = jnp.maximum(tiles_ref[0, s], 0)
        tc = jnp.maximum(tiles_ref[1, s], 0)
        row_off = row_b[tr][2:3, :]
        col_off = col_b[tc][2:3, :]
        disp = []
        for a in range(3):
            lanes = slice(a * TB, (a + 1) * TB)
            rp = dot((eye * row_off[:, lanes]).astype(bf16), ones)
            gap = (rp - col_off[:, lanes]).astype(jnp.int32) + PERIOD // 2
            disp.append(((gap & (PERIOD - 1)) - PERIOD // 2).astype(f32))
        squares = disp[0] * disp[0] + disp[1] * disp[1] + disp[2] * disp[2]
        envelope = jnp.exp(squares * (-0.5 / scale_sq)) / scale_sq
        third = squares / 3.0
        for a in range(3):
            for b in range(a, 3):
                element = disp[a] * disp[b]
                if a == b:
                    element = element - third
                entry = (envelope * element).astype(bf16)
                kmat[s, a * TB : (a + 1) * TB, b * TB : (b + 1) * TB] = entry
                if a != b:
                    kmat[s, b * TB : (b + 1) * TB, a * TB : (a + 1) * TB] = entry
        wide = kmat[s].astype(f32)
        sq = wide * wide
        high = sq.astype(bf16)
        low = (sq - high.astype(f32)).astype(bf16)
        one_row = jnp.ones((8, 3 * TB), bf16)
        energy = dot_nt(one_row, high) + dot_nt(one_row, low)
        return pick(energy[0:1], energies, s)

    energies = lax.fori_loop(
        0, slots, build, tuple(jnp.zeros((1, 3 * TB), f32) for _ in range(n_col)),
        unroll=slots <= 4,
    )
    for i in range(n_col):
        e_send[i : i + 1, :] = energies[i]
        e_recv[me, i : i + 1, :] = energies[i]

    def e_copy(r, c):
        p = r * n_col + c
        return remote(e_send, e_recv.at[me], e_ss.at[p], e_rs.at[me], r, c)

    for r in range(n_row):
        cur[r] = col_b[r, 0:2, :]
    acc[...] = cheb_coef[0] * own_noise

    def a_arrive(r, c):
        p = r * n_col + c
        remote(a_send, a_recv.at[p], a_ss.at[p], a_rs.at[p], r, c).wait_recv()

    def prepare_table():
        each(a_arrive)

        def spread(h, carry):
            tabf[pl.ds(h * cr, cr), :] = a_recv[h, 1 : 1 + cr, :]
            return carry

        lax.fori_loop(0, nd, spread, 0)
        cell = tabf[...].astype(jnp.int32)
        y_slab, z_slab = glen // n_row, glen // n_col
        holder = over(iota((kq, LANES), 0), cr)
        pos_x = over(cell, y_slab * z_slab)
        pos_y = over(holder, n_col) * y_slab + (over(cell, z_slab) & (y_slab - 1))
        pos_z = (holder & (n_col - 1)) * z_slab + (cell & (z_slab - 1))
        for at, pos in enumerate((pos_x, pos_y, pos_z)):
            tab[:, at * LANES : (at + 1) * LANES] = pos.astype(f32).astype(bf16)

    x_step = LANES // ys
    lane = iota((LANES, LANES), 1)
    scaled = 1.0 / glen
    along_x = ((me_r * xs + over(lane, ys)).astype(f32) * scaled).astype(bf16)
    along_y = ((me_c * ys + (lane & (ys - 1))).astype(f32) * scaled).astype(bf16)
    wang[...] = jnp.zeros_like(wang)
    wang[0:LANES, 0:LANES] = along_x
    wang[LANES : 2 * LANES, 0:LANES] = along_y
    wang[0:LANES, LANES : 2 * LANES] = jnp.full((LANES, LANES), x_step * scaled, bf16)
    wang[2 * LANES :, 2 * LANES :] = (lane.astype(f32) * scaled).astype(bf16)
    rep = over(iota((8, 6 * glen), 1), glen) == iota((8, 6 * glen), 0)
    rep = rep.astype(f32).astype(bf16)
    wide_ones = jnp.ones((TB, kq), bf16)
    step_rows = 32

    def far_copy(i, c):
        return remote(
            far_send.at[i * n_col + c], far_recv.at[me],
            far_ss.at[i * n_col + c], far_rs.at[me], i, c,
        )

    def far_chunk(i, carry):
        spots = jnp.concatenate(
            [eye * a_recv[i * n_col + c, 0:1, :] for c in range(n_col)], axis=0
        ).astype(bf16)
        code = dot(spots, wide_ones).astype(jnp.int32)
        s_idx = over(code, nd)
        row_idx = (code & (nd - 1)) * cr + over(s_idx, per_row)
        hot = (row_idx == iota((beads, kq), 1)).astype(f32).astype(bf16)
        found = dot(hot, tab[...])
        owner_of = i * n_col + over(iota((beads, LANES), 0), TB)
        want = (s_idx[:, :LANES] & (per_row - 1)) * nd + owner_of
        keep = want == iota((beads, LANES), 1)
        places = jnp.concatenate(
            [jnp.where(keep, found[:, k * LANES : (k + 1) * LANES], 0.0) for k in range(3)],
            axis=1,
        ).astype(bf16)
        ang[...] = dot(places, wang[...])

        def phase_block(j, carry):
            rows = pl.ds(pl.multiple_of(j * step_rows, step_rows), step_rows)
            at_lane = iota((step_rows, LANES), 1)
            start = ang[rows, 0:LANES]
            co = cos_turn(start)
            ns = cos_turn(start + 0.25)
            turn_x = cos_turn(
                ang[rows, LANES : 2 * LANES] - jnp.where(at_lane == 1, 0.25, 0.0)
            )
            cd = jnp.broadcast_to(turn_x[:, 0:1], co.shape)
            sd = jnp.broadcast_to(turn_x[:, 1:2], co.shape)
            ang[rows, 2 * LANES :] = cos_turn(
                ang[rows, 2 * LANES :] + jnp.where(at_lane > half, 0.25, 0.0)
            )
            for g in range(xy // LANES):
                phase[rows, g * LANES : (g + 1) * LANES] = co.astype(bf16)
                phase[rows, xy + g * LANES : xy + (g + 1) * LANES] = ns.astype(bf16)
                co, ns = co * cd + ns * sd, ns * cd - co * sd
            return carry

        lax.fori_loop(0, beads // step_rows, phase_block, 0)
        sums = dot(phase[...], hat[...])
        tz = ang[:, 2 * LANES :]
        weighted = jnp.concatenate(
            [(sums[:, k * glen : (k + 1) * glen] * tz).astype(bf16) for k in range(6)], axis=1
        )
        res = dot_nt(rep, weighted)
        for c in range(n_col):
            owner = i * n_col + c
            far_send[owner] = res[:, c * TB : (c + 1) * TB]

            @pl.when(owner == me)
            def _():
                far_recv[me] = res[:, c * TB : (c + 1) * TB]

            @pl.when(owner != me)
            def _():
                far_copy(i, c).start()

        return carry

    def y_copy(r, c, par):
        p = r * n_col + c
        return remote(
            y_send.at[par, c], y_recv.at[par, me], y_ss.at[par, p], y_rs.at[par, me], r, c
        )

    def y_arrive(r, c, par):
        p = r * n_col + c
        remote(
            y_send.at[par, 0], y_recv.at[par, p], y_ss.at[par, p], y_rs.at[par, p], r, c
        ).wait_recv()

    each(lambda r, c: e_copy(r, c).start())

    def degree_step(m, carry):
        par = lax.rem(m, 2)

        def apply(s, sums):
            tc = jnp.maximum(tiles_ref[1, s], 0)
            w = cur[tc]
            w = jnp.concatenate([w, jnp.zeros((6, 3 * TB), f32)], axis=0).astype(bf16)
            return pick(dot_nt(w, kmat[s])[0:2], sums, s)

        sums = lax.fori_loop(
            0, slots, apply, tuple(jnp.zeros((2, 3 * TB), f32) for _ in range(n_col)),
            unroll=slots <= 4,
        )
        own = jnp.zeros((2, 3 * TB), f32)
        for i in range(n_col):
            y_send[par, i] = sums[i]
            own = own + sums[i] * jnp.where(me_c == i, 1.0, 0.0).astype(f32)
        y_recv[par, me] = own
        each(lambda r, c: y_copy(r, c, par).start())

        @pl.when(m == 0)
        def _():
            prepare_table()

        lax.fori_loop(m * n_row // DEGREES, (m + 1) * n_row // DEGREES, far_chunk, 0)

        @pl.when(m == 0)
        def _():
            def e_arrive(r, c):
                p = r * n_col + c
                remote(e_send, e_recv.at[p], e_ss.at[p], e_rs.at[p], r, c).wait_recv()

            each(e_arrive)
            top = jnp.zeros((n_col, 3 * TB), f32)
            for r in range(n_row):
                total = e_recv[r * n_col]
                for c in range(1, n_col):
                    total = total + e_recv[r * n_col + c]
                top = jnp.maximum(top, total)
            largest = jnp.max(jnp.max(top, axis=1, keepdims=True), axis=0, keepdims=True)
            scale[...] = jnp.broadcast_to(1.0 / jnp.sqrt(largest + 1e-06), scale.shape)

        each(lambda r, c: y_arrive(r, c, par))
        each(lambda r, c: y_copy(r, c, par).wait_send())
        first = jnp.where(m == 0, 1.0, 0.0).astype(f32)
        coef = jnp.where(
            m == 0, cheb_coef[1],
            jnp.where(m == 1, cheb_coef[2], jnp.where(m == 2, cheb_coef[3], cheb_coef[4])),
        ).astype(f32)
        sc = jnp.concatenate([scale[0:2, :]] * 3, axis=1)

        def advance(r, carry):
            total = y_recv[par, r * n_col]
            for c in range(1, n_col):
                total = total + y_recv[par, r * n_col + c]
            now = sc * total
            following = jnp.where(m == 0, now, 2.0 * now - prev[r])
            prev[r] = cur[r]
            cur[r] = following
            return carry

        lax.fori_loop(0, n_row, advance, 0)
        acc[...] = acc[...] + coef * cur[me_r]
        return carry

    prev[...] = jnp.zeros_like(prev)
    lax.fori_loop(0, DEGREES, degree_step, 0)

    each_row(lambda r: b_col_copy(r).wait_send())
    each_col(lambda c: b_row_copy(c).wait_send())
    each(lambda r, c: a_copy(r, c).wait_send())
    each(lambda r, c: e_copy(r, c).wait_send())

    def far_arrive(r, c):
        p = r * n_col + c
        remote(
            far_send.at[p], far_recv.at[p], far_ss.at[p], far_rs.at[p], r, c
        ).wait_recv()

    each(far_arrive)
    each(lambda r, c: far_copy(r, c).wait_send())
    far = lax.fori_loop(
        1, nd, lambda p, t: t + far_recv[p], far_recv[0]
    )
    near = acc[...]
    for a in range(3):
        out_ref[a] = near[:, a * TB : (a + 1) * TB] + far[2 * a : 2 * a + 2, :]


def spread_device(noise_field, offsets, tile_list, send_cells, bead_slot, spectral):
    n_row = lax.axis_size("row")
    n_col = lax.axis_size("col")
    nd = n_row * n_col
    xs, ys, glen = spectral.shape[3:]
    slots = tile_list.shape[3]
    cap = send_cells.shape[2]
    cr = cap * nd // LANES
    xy = xs * ys
    kq = max(LANES, nd * cr)
    beads = n_col * TB
    a_rows = -(-(1 + cr) // 4) * 4
    chunks = 4 if xy % 256 == 0 else 1
    dims = (n_row, n_col, slots, xs, ys, glen, cap)
    vmem = pl.BlockSpec(memory_space=pltpu.VMEM)
    dma = pltpu.SemaphoreType.DMA
    wide = 3 * TB
    return pl.pallas_call(
        functools.partial(kernel, dims),
        out_shape=jax.ShapeDtypeStruct(noise_field.shape, f32),
        in_specs=[pl.BlockSpec(memory_space=pltpu.SMEM), vmem, vmem, vmem, vmem,
                  pl.BlockSpec(memory_space=pl.ANY)],
        out_specs=vmem,
        scratch_shapes=[
            pltpu.VMEM((12, xy, glen), f32),
            pltpu.VMEM((6 * (xy // chunks), 2 * glen), bf16),
            pltpu.VMEM((2 * xy, 6 * glen), bf16),
            pltpu.VMEM((beads, 2 * xy), bf16),
            pltpu.VMEM((beads, 3 * LANES), f32),
            pltpu.VMEM((3 * LANES, 3 * LANES), bf16),
            pltpu.VMEM((kq, LANES), f32),
            pltpu.VMEM((kq, 3 * LANES), bf16),
            pltpu.VMEM((slots, wide, wide), bf16),
            pltpu.VMEM((a_rows, LANES), f32),
            pltpu.VMEM((nd, a_rows, LANES), f32),
            pltpu.VMEM((4, wide), f32),
            pltpu.VMEM((n_col, 4, wide), f32),
            pltpu.VMEM((n_row, 4, wide), f32),
            pltpu.VMEM((n_col, wide), f32),
            pltpu.VMEM((nd, n_col, wide), f32),
            pltpu.VMEM((2, n_col, 2, wide), f32),
            pltpu.VMEM((2, nd, 2, wide), f32),
            pltpu.VMEM((nd, 8, TB), f32),
            pltpu.VMEM((nd, 8, TB), f32),
            pltpu.VMEM((n_row, 2, wide), f32),
            pltpu.VMEM((n_row, 2, wide), f32),
            pltpu.VMEM((2, wide), f32),
            pltpu.VMEM((8, LANES), f32),
            dma((chunks,)),
            dma((nd,)), dma((nd,)),
            dma((n_row + n_col,)), dma((n_row + n_col,)),
            dma((nd,)), dma((nd,)),
            dma((2, nd)), dma((2, nd)),
            dma((nd,)), dma((nd,)),
        ],
        compiler_params=pltpu.CompilerParams(
            collective_id=0, has_side_effects=True, vmem_limit_bytes=56 * 1024 * 1024
        ),
    )(
        tile_list.reshape(2, slots),
        noise_field,
        offsets,
        bead_slot.reshape(1, TB),
        send_cells.reshape(cap, nd),
        spectral.reshape(12, xy, glen),
    )


PLANES = PERIOD // 2 + 1
FLAT = PERIOD * PERIOD
MODES = PLANES * 2 * FLAT
PAIRS = ((0, 0), (1, 1), (2, 2), (0, 1), (0, 2), (1, 2))


def lattice_spectrum():
    code = np.arange(PERIOD**3)
    site = np.stack([code // FLAT, code // PERIOD % PERIOD, code % PERIOD])
    disp = (site + PERIOD // 2) % PERIOD - PERIOD // 2
    d = disp.astype(np.float32)
    squares = d[0] * d[0] + d[1] * d[1] + d[2] * d[2]
    scale_sq = np.float32(kernel_range * kernel_range)
    envelope = np.exp(squares * np.float32(-0.5 / scale_sq)) / scale_sq
    table = np.zeros((3, 3, PERIOD**3))
    for a, b in PAIRS:
        element = d[a] * d[b]
        if a == b:
            element = element - squares / np.float32(3.0)
        table[a, b] = (envelope * element).astype(ml_dtypes.bfloat16).astype(np.float64)
        table[b, a] = table[a, b]
    energy = (table * table).sum(axis=1)
    qz = np.arange(PLANES)[:, None, None, None]
    part = np.arange(2)[None, :, None, None]
    qx = np.arange(PERIOD)[None, None, :, None]
    qy = np.arange(PERIOD)[None, None, None, :]
    qx, qy, qz, part = (t.reshape(-1) for t in np.broadcast_arrays(qx, qy, qz, part))
    angle = 2.0 * np.pi / PERIOD * ((np.stack([qx, qy, qz], 1) @ site) % PERIOD)
    weight = np.where((qz == 0) | (qz == PERIOD // 2), 1.0, 2.0) / PERIOD**3
    turn = np.where(part == 0, 1.0, -1.0)
    rows = [weight * (np.cos(angle) @ table[p]) for p in PAIRS]
    rows += [-turn * weight * (np.sin(angle) @ table[p]) for p in PAIRS[3:]]
    rows += [weight * (np.cos(angle) @ energy[a]) for a in range(3)]
    rows += [np.zeros(MODES)] * (-len(rows) % 8)
    return np.stack(rows).astype(np.float32)


def shared_kernel(
    dims,
    tiles_ref, noise_ref, off_ref, slot_ref, cells_ref, spectrum_hbm, spec_hbm,
    out_ref,
    spec, pre, hat, phase_a, phase_b, phi, wide, cheb_a, cheb_b, mixer, mixed,
    msg_f, msg, inbox, table, offs, spectrum, last,
    far_send, far_recv,
    spec_sem, spectrum_sem, m_ss, m_rs, far_ss, far_rs,
):
    n_row, n_col, slots, xs, ys, glen, cap = dims
    nd = n_row * n_col
    xy = xs * ys
    per_row = LANES // nd
    cr = cap // per_row
    cells_at = 10
    tile_at = cells_at + 2 * cr
    beads = nd * TB
    me_r = lax.axis_index("row")
    me_c = lax.axis_index("col")
    me = me_r * n_col + me_c
    chunks = spec_sem.shape[0]
    part = xy // chunks
    nb = 2 * nd
    rows_t = 3 * nb
    rows_e = rows_t + nd

    def spec_copy(i):
        rows = pl.ds(i * part, part)
        return pltpu.make_async_copy(
            spec_hbm.at[:, rows, :], spec.at[:, rows, :], spec_sem.at[i]
        )

    for i in range(chunks):
        spec_copy(i).start()
    spectrum_copy = pltpu.make_async_copy(spectrum_hbm, spectrum, spectrum_sem)
    spectrum_copy.start()

    peers = sorted(
        [(i, j) for i in range(n_row) for j in range(n_col)], key=lambda t: (-t[1], -t[0])
    )
    others = peers[:-1]

    def place(i, j):
        return jnp.bitwise_xor(me_r, i), jnp.bitwise_xor(me_c, j)

    barrier = pltpu.get_barrier_semaphore()
    for i, j in others:
        r, c = place(i, j)
        pl.semaphore_signal(
            barrier, inc=1, device_id={"row": r, "col": c},
            device_id_type=pl.DeviceIdType.MESH,
        )

    def remote(src, dst, ss, rs, r, c):
        return pltpu.make_async_remote_copy(
            src_ref=src, dst_ref=dst, send_sem=ss, recv_sem=rs,
            device_id={"row": r, "col": c}, device_id_type=pl.DeviceIdType.MESH,
        )

    for a in range(3):
        msg_f[2 * a : 2 * a + 2, :] = noise_ref[a]
    msg_f[6:9, :] = off_ref[...].astype(f32)
    msg_f[9:10, :] = slot_ref[...].astype(f32)
    spread = over(iota((nd, LANES), 1), per_row) == iota((nd, LANES), 0)
    spread = spread.astype(f32).astype(bf16)
    keep = (iota((cap, LANES), 1) & (per_row - 1)) == (iota((cap, LANES), 0) & (per_row - 1))
    cells = cells_ref[...]
    for h, half_cell in enumerate((over(cells, 512), (cells & 511) - 256)):
        out = dot(half_cell.astype(f32).astype(bf16), spread)
        out = jnp.sum(jnp.where(keep, out, 0.0).reshape(cr, per_row, LANES), axis=1)
        msg_f[cells_at + h * cr : cells_at + (h + 1) * cr, :] = out
    lane_row = iota((1, LANES), 1)
    row_list = jnp.zeros((1, LANES), jnp.int32)
    col_list = jnp.zeros((1, LANES), jnp.int32)
    for s in range(slots):
        here = lane_row == me * slots + s
        tr, tc = tiles_ref[0, s], tiles_ref[1, s]
        row_list = jnp.where(
            here & (jnp.full((1, LANES), tr) >= 0), me_r * n_col + tr + 1, row_list
        )
        col_list = jnp.where(here, tc * n_col + me_c + 1, col_list)
    msg_f[tile_at : tile_at + 1, :] = row_list.astype(f32)
    msg_f[tile_at + 1 : tile_at + 2, :] = col_list.astype(f32)
    if tile_at + 2 < msg_f.shape[0]:
        msg_f[tile_at + 2 :, :] = jnp.zeros((msg_f.shape[0] - tile_at - 2, LANES), f32)
    msg[...] = msg_f[...].astype(bf16)
    inbox[me] = msg_f[...].astype(bf16)

    pl.semaphore_wait(barrier, nd - 1)

    def msg_copy(i, j):
        r, c = place(i, j)
        p = i * n_col + j
        return remote(msg, inbox.at[me], m_ss.at[p], m_rs.at[me], r, c)

    def msg_arrive(i, j):
        r, c = place(i, j)
        p = r * n_col + c
        remote(msg, inbox.at[p], m_ss.at[0], m_rs.at[p], r, c).wait_recv()

    for i, j in others:
        msg_copy(i, j).start()

    wide[...] = jnp.zeros_like(wide)
    mixed[...] = jnp.zeros_like(mixed)
    cheb_a[...] = jnp.zeros_like(cheb_a)
    for o in range(nd):
        ones = (iota((nd, TB), 0) == o).astype(f32)
        wide[rows_t:rows_e, o * TB : (o + 1) * TB] = ones.astype(bf16)

    gj = iota((2 * glen, 2 * glen), 0)
    gi = iota((2 * glen, 2 * glen), 1)
    zi, zj = gi & (glen - 1), gj & (glen - 1)
    in_im, out_im = gi >= glen, gj >= glen
    half = glen // 2
    same = zi == zj
    mirror = (zi + zj == glen) & (zi != zj)
    even = zj <= half
    plain = in_im == out_im
    fold = jnp.where(
        even,
        jnp.where(plain & (same | mirror), 1.0, 0.0),
        jnp.where(
            plain,
            0.0,
            jnp.where(same, 1.0, 0.0) - jnp.where(mirror, 1.0, 0.0),
        )
        * jnp.where(out_im, -1.0, 1.0),
    ).astype(bf16)

    width_sq = (glen / 8.0) ** 2
    front = math.sqrt(1.5) / (2.0 * math.pi * width_sq) ** 0.75

    def signed(n):
        return jnp.where(n < half, n, n - glen).astype(f32)

    ky = signed(me_c * ys + iota((ys, glen), 0))
    kz = signed(iota((ys, glen), 1))
    kyz_sq = ky * ky + kz * kz

    def hat_block(i, first):
        kx = signed(me_r * xs + i)
        q = kx * kx + kyz_sq
        amp = jnp.where(q > 0, front * jnp.exp(q * (-0.25 / width_sq)), 0.0)
        damp = amp / jnp.maximum(q, 1.0)
        rows = pl.ds(pl.multiple_of(i * ys, ys), ys)
        at = pl.multiple_of((i - first) * ys, ys)
        waves = (kx, ky, kz)
        for v in range(2):
            for p in range(2):
                s = [spec[(p * 3 + a) * 2 + v, rows, :] for a in range(3)]
                along = (kx * s[0] + ky * s[1] + kz * s[2]) * damp
                for a in range(3):
                    pre[pl.ds((a * 2 + v) * part + at, ys), p * glen : (p + 1) * glen] = (
                        amp * s[a] - waves[a] * along
                    ).astype(bf16)
        return first

    per = part // ys
    for i in range(chunks):
        spec_copy(i).wait()
        lax.fori_loop(i * per, (i + 1) * per, hat_block, i * per)
        for k in range(6):
            folded = dot_nt(fold, pre[k * part : (k + 1) * part, :]).astype(bf16)
            for p in range(2):
                hat[
                    k * glen : (k + 1) * glen, p * xy + i * part : p * xy + (i + 1) * part
                ] = folded[p * glen : (p + 1) * glen, :]

    spectrum_copy.wait()
    for i, j in others[::-1]:
        msg_arrive(i, j)

    row_list = jnp.zeros((1, LANES), f32)
    col_list = jnp.zeros((1, LANES), f32)
    slot_rows = nb // 2 * cr
    for o in range(nd):
        got = inbox[o].astype(f32)
        row_list = row_list + got[tile_at : tile_at + 1]
        col_list = col_list + got[tile_at + 1 : tile_at + 2]
        for h in range(2):
            table[h, o * cr : (o + 1) * cr, :] = got[
                cells_at + h * cr : cells_at + (h + 1) * cr
            ]
        offs[:, o * TB : (o + 1) * TB] = got[6:9]
        first = 2 * o % 16
        base = 2 * o // 16 * 16
        for a in range(3):
            cheb_a[a, o, first : first + 2, :] = got[2 * a : 2 * a + 2]
            wide[a * nb + base : a * nb + base + 16, o * TB : (o + 1) * TB] = (
                cheb_a[a, o].astype(bf16)
            )
    tables = []
    for h in range(2):
        tables.append(jnp.transpose(table[h])[:, :slot_rows])
    for h in range(2):
        table[2 + h, :, :slot_rows] = tables[h]

    def kind_of(n):
        return jnp.where(n < rows_t, over(n, nb) * 2 + (n & 1), 6)

    def owner_of(n):
        return jnp.where(n < rows_t, over(n & (nb - 1), 2), n - rows_t)

    mix_rows = iota((rows_e, LANES), 0)
    mix_lanes = iota((rows_e, LANES), 1)
    all_rows = iota((LANES, LANES), 0)
    to = ((owner_of(mix_rows) + 1).astype(f32) == row_list).astype(f32).astype(bf16)
    frm = ((owner_of(all_rows) + 1).astype(f32) == col_list).astype(f32).astype(bf16)
    joined = jnp.where(
        (kind_of(mix_rows) == kind_of(mix_lanes)) & (mix_lanes < rows_e), dot_nt(to, frm), 0.0
    ).astype(bf16)
    mixer[:, :LANES] = joined
    mixer[:, LANES:] = joined

    def build_phi(o):
        lanes = slice(o * TB, (o + 1) * TB)
        q = iota((PERIOD, TB), 0).astype(f32) * (1.0 / PERIOD)
        co, si = [], []
        for a in range(3):
            turn = q * offs[a : a + 1, lanes]
            co.append(cos_turn(turn))
            si.append(cos_turn(turn - 0.25))
        flat_c, flat_s = [], []
        for x in range(PERIOD):
            cx, sx = co[0][x : x + 1], si[0][x : x + 1]
            flat_c.append(cx * co[1] - sx * si[1])
            flat_s.append(sx * co[1] + cx * si[1])
        flat_c = jnp.concatenate(flat_c, axis=0)
        flat_s = jnp.concatenate(flat_s, axis=0)
        for z in range(PLANES):
            cz, sz = co[2][z : z + 1], si[2][z : z + 1]
            at = z * 2 * FLAT
            phi[at : at + FLAT, lanes] = (flat_c * cz - flat_s * sz).astype(bf16)
            phi[at + FLAT : at + 2 * FLAT, lanes] = (flat_s * cz + flat_c * sz).astype(bf16)

    y_slab, z_slab = glen // n_row, glen // n_col
    scaled = 1.0 / glen

    def locate(r, c):
        o = r * n_col + c
        code = inbox[o].astype(f32)[9:10].astype(jnp.int32)
        slot = over(code, nd)
        holder = code & (nd - 1)
        row_at = holder * cr + over(slot, per_row)
        hot = (iota((slot_rows, TB), 0) == row_at).astype(f32).astype(bf16)
        at = pl.ds(pl.multiple_of(o * per_row, per_row), per_row)
        lists = jnp.concatenate(
            [table[2, at, :slot_rows], table[3, at, :slot_rows]], axis=0
        ).astype(bf16)
        found = dot(lists, hot)
        mine = iota((per_row, TB), 0) == (slot & (per_row - 1))
        high = jnp.sum(jnp.where(mine, found[:per_row], 0.0), axis=0, keepdims=True)
        low = jnp.sum(jnp.where(mine, found[per_row:], 0.0), axis=0, keepdims=True)
        cell = high.astype(jnp.int32) * 512 + low.astype(jnp.int32) + 256
        pos_x = over(cell, y_slab * z_slab)
        pos_y = over(holder, n_col) * y_slab + (over(cell, z_slab) & (y_slab - 1))
        pos_z = (holder & (n_col - 1)) * z_slab + (cell & (z_slab - 1))
        return [p.astype(f32) * scaled for p in (pos_x, pos_y, pos_z)]

    kx_col = (me_r * xs + iota((xs, 2 * TB), 0)).astype(f32)
    ky_col = (me_c * ys + iota((ys, 2 * TB), 0)).astype(f32)
    kz_col = iota((glen, 2 * TB), 0)

    def build_phase(pair, phase):
        spots = [locate(*place(i, j)) for i, j in pair]
        px, py, pz = (
            jnp.concatenate([spots[0][t], spots[1][t]], axis=1) for t in range(3)
        )
        turn = kx_col * px
        cx, nx = cos_turn(turn), cos_turn(turn + 0.25)
        turn = ky_col * py
        cy, ny = cos_turn(turn), cos_turn(turn + 0.25)
        for i in range(xs):
            a, b = cx[i : i + 1], nx[i : i + 1]
            phase[i * ys : (i + 1) * ys, :] = (a * cy - b * ny).astype(bf16)
            phase[xy + i * ys : xy + (i + 1) * ys, :] = (b * cy + a * ny).astype(bf16)
        return cos_turn(kz_col.astype(f32) * pz + jnp.where(kz_col > half, 0.25, 0.0))

    def far_copy(i, j):
        r, c = place(i, j)
        p = r * n_col + c
        q = i * n_col + j
        return remote(far_send.at[q], far_recv.at[me], far_ss.at[q], far_rs.at[me], r, c)

    def far_sums(pair, phase, tz):
        sums = dot(hat[...], phase[...])
        for k in range(6):
            line = jnp.sum(sums[k * glen : (k + 1) * glen] * tz, axis=0, keepdims=True)
            for t, (i, j) in enumerate(pair):
                half_line = line[:, t * TB : (t + 1) * TB]
                if i + j:
                    far_send[i * n_col + j, k : k + 1, :] = half_line
                else:
                    far_recv[me, k : k + 1, :] = half_line
        for i, j in pair:
            if i + j:
                far_copy(i, j).start()

    pairs = [peers[t : t + 2] for t in range(0, nd, 2)]
    phases = (phase_a, phase_b)
    tz = build_phase(pairs[0], phase_a)
    for n, pair in enumerate(pairs):
        nxt = None
        if n + 1 < len(pairs):
            nxt = build_phase(pairs[n + 1], phases[(n + 1) % 2])
        far_sums(pair, phases[n % 2], tz)
        tz = nxt
        for o in range(n * nd // len(pairs), (n + 1) * nd // len(pairs)):
            build_phi(o)

    near = [cheb_coef[0] * noise_ref[a] for a in range(3)]
    own_rows = pl.ds(lax.rem(2 * me, 16), 2)
    scale = None
    for m in range(DEGREES):
        rows = rows_e if m == 0 else rows_t
        sums = dot_nt(wide[0:rows, :], phi[...])
        high = sums.astype(bf16)
        mixed[0:rows, :] = high
        mixed[LANES : LANES + rows, :] = (sums - high.astype(f32)).astype(bf16)
        sums = dot(mixer[0:rows, :], mixed[...])
        turned = jnp.concatenate(
            [
                pltpu.roll(sums[0:rows_t, g * LANES : (g + 1) * LANES], FLAT, 1)
                for g in range(PLANES)
            ],
            axis=1,
        )
        blocks = []
        for a in range(3):
            total = spectrum[a : a + 1, :] * sums[a * nb : (a + 1) * nb]
            for b in range(3):
                if a != b:
                    e = PAIRS.index((min(a, b), max(a, b)))
                    total = total + spectrum[e : e + 1, :] * sums[b * nb : (b + 1) * nb]
                    total = total + spectrum[e + 3 : e + 4, :] * turned[b * nb : (b + 1) * nb]
            blocks.append(total)
        if m == 0:
            for a in range(3):
                blocks.append(spectrum[9 + a : 10 + a, :] * sums[rows_t:rows_e])
            stacked = jnp.concatenate(blocks, axis=0)
            high = stacked.astype(bf16)
            low = (stacked[rows_t:] - high[rows_t:].astype(f32)).astype(bf16)
            out = dot(jnp.concatenate([high, low], axis=0), phi[...])
            energy = out[rows_t : rows_t + 3 * nd] + out[rows_t + 3 * nd :]
            top = jnp.zeros((3 * nd, TB), f32)
            owner = iota((3 * nd, TB), 0) & (nd - 1)
            for o in range(nd):
                top = jnp.maximum(
                    top, jnp.where(owner == o, energy[:, o * TB : (o + 1) * TB], 0.0)
                )
            top = jnp.max(jnp.max(top, axis=1, keepdims=True), axis=0, keepdims=True)
            scale = jnp.broadcast_to(1.0 / jnp.sqrt(top + 1e-06), (16, TB))
        else:
            stacked = jnp.concatenate(blocks, axis=0).astype(bf16)
            if m < DEGREES - 1:
                out = dot(stacked, phi[...])
        now, before = (cheb_a, cheb_b) if m % 2 == 0 else (cheb_b, cheb_a)
        if m < DEGREES - 1:
            line = iota((16, TB), 0)
            for o in range(nd):
                first = 2 * o % 16
                base = 2 * o // 16 * 16
                mine = (line >= first) & (line < first + 2)
                for a in range(3):
                    got = out[a * nb + base : a * nb + base + 16, o * TB : (o + 1) * TB]
                    got = jnp.where(mine, scale * got, 0.0)
                    if m > 0:
                        got = 2.0 * got - before[a, o]
                    before[a, o] = got
                    wide[a * nb + base : a * nb + base + 16, o * TB : (o + 1) * TB] = (
                        got.astype(bf16)
                    )
            for a in range(3):
                near[a] = near[a] + cheb_coef[m + 1] * before[a, me, own_rows, :]
        else:
            last[...] = dot(stacked, phi[:, pl.ds(pl.multiple_of(me * TB, TB), TB)])
            for a in range(3):
                got = 2.0 * (scale[0:2] * last[pl.ds(a * nb + 2 * me, 2), :])
                near[a] = near[a] + cheb_coef[m + 1] * (got - before[a, me, own_rows, :])

    for i, j in others:
        msg_copy(i, j).wait_send()

    def far_arrive(i, j):
        r, c = place(i, j)
        p = r * n_col + c
        remote(far_send.at[0], far_recv.at[p], far_ss.at[0], far_rs.at[p], r, c).wait_recv()

    for i, j in others:
        far_arrive(i, j)
    for i, j in others:
        far_copy(i, j).wait_send()
    far = far_recv[0]
    for p in range(1, nd):
        far = far + far_recv[p]
    for a in range(3):
        out_ref[a] = near[a] + far[2 * a : 2 * a + 2, :]


def shared_device(noise_field, offsets, tile_list, send_cells, bead_slot, spectral):
    n_row = lax.axis_size("row")
    n_col = lax.axis_size("col")
    nd = n_row * n_col
    xs, ys, glen = spectral.shape[3:]
    slots = tile_list.shape[3]
    cap = send_cells.shape[2]
    xy = xs * ys
    cr = cap * nd // LANES
    msg_rows = -(-(12 + 2 * cr) // 16) * 16
    chunks = 4 if xy % 256 == 0 else 1
    dims = (n_row, n_col, slots, xs, ys, glen, cap)
    vmem = pl.BlockSpec(memory_space=pltpu.VMEM)
    hbm = pl.BlockSpec(memory_space=pl.ANY)
    dma = pltpu.SemaphoreType.DMA
    rows_t = 6 * nd
    spectrum = lattice_spectrum()
    return pl.pallas_call(
        functools.partial(shared_kernel, dims),
        out_shape=jax.ShapeDtypeStruct(noise_field.shape, f32),
        in_specs=[pl.BlockSpec(memory_space=pltpu.SMEM), vmem, vmem, vmem, vmem, hbm, hbm],
        out_specs=vmem,
        scratch_shapes=[
            pltpu.VMEM((12, xy, glen), f32),
            pltpu.VMEM((6 * (xy // chunks), 2 * glen), bf16),
            pltpu.VMEM((6 * glen, 2 * xy), bf16),
            pltpu.VMEM((2 * xy, 2 * TB), bf16),
            pltpu.VMEM((2 * xy, 2 * TB), bf16),
            pltpu.VMEM((MODES, nd * TB), bf16),
            pltpu.VMEM((rows_t + nd, nd * TB), bf16),
            pltpu.VMEM((3, nd, 16, TB), f32),
            pltpu.VMEM((3, nd, 16, TB), f32),
            pltpu.VMEM((rows_t + nd, 2 * LANES), bf16),
            pltpu.VMEM((2 * LANES, MODES), bf16),
            pltpu.VMEM((msg_rows, LANES), f32),
            pltpu.VMEM((msg_rows, LANES), bf16),
            pltpu.VMEM((nd, msg_rows, LANES), bf16),
            pltpu.VMEM((4, LANES, LANES), f32),
            pltpu.VMEM((3, nd * TB), f32),
            pltpu.VMEM(spectrum.shape, f32),
            pltpu.VMEM((rows_t, TB), f32),
            pltpu.VMEM((nd, 8, TB), f32),
            pltpu.VMEM((nd, 8, TB), f32),
            dma((chunks,)), dma,
            dma((nd,)), dma((nd,)),
            dma((nd,)), dma((nd,)),
        ],
        compiler_params=pltpu.CompilerParams(
            collective_id=1, has_side_effects=True, vmem_limit_bytes=56 * 1024 * 1024
        ),
    )(
        tile_list.reshape(2, slots),
        noise_field,
        offsets,
        bead_slot.reshape(1, TB),
        send_cells.reshape(cap, nd),
        jnp.asarray(spectrum),
        spectral.reshape(12, xy, glen),
    )


def power_of_two(n):
    return n & (n - 1) == 0


def per_device(noise_field, offsets, tile_list, send_cells, bead_slot, spectral):
    n_row = lax.axis_size("row")
    n_col = lax.axis_size("col")
    nd = n_row * n_col
    xs, ys, glen = spectral.shape[3:]
    cap = send_cells.shape[2]
    fits = (
        8 <= nd <= 16
        and power_of_two(n_row)
        and power_of_two(n_col)
        and power_of_two(glen)
        and nd * tile_list.shape[3] <= LANES
        and cap % (LANES // nd) == 0
        and cap * nd <= 256
        and glen * (glen // n_row) * (glen // n_col) <= 1 << 17
        and ys % 16 == 0
    )
    run = shared_device if fits else spread_device
    return run(noise_field, offsets, tile_list, send_cells, bead_slot, spectral)


def solution(mesh):
    return jax.shard_map(
        per_device,
        mesh=mesh,
        in_specs=(
            P(None, None, ("groups", "row", "col")),
            P(None, ("groups", "row", "col")),
            P(("groups", "row"), "col", None, None),
            P(("groups", "row"), "col", None, None),
            P(("groups", "row", "col")),
            P(None, None, None, ("groups", "row"), "col", None),
        ),
        out_specs=P(None, None, ("groups", "row", "col")),
        check_vma=False,
    )
```

```python
import functools
import math

import jax
import jax.numpy as jnp
import ml_dtypes
import numpy as np
from jax import lax
from jax.experimental import pallas as pl
from jax.experimental.pallas import tpu as pltpu
from jax.sharding import PartitionSpec as P

TB = 128
LANES = 128
PERIOD = 8
DEGREES = 4

cheb_coef = (1.0, 0.45, -0.2, 0.12, -0.08)
kernel_range = 1.5

f32 = jnp.float32
bf16 = jnp.bfloat16


def iota(shape, dim):
    return lax.broadcasted_iota(jnp.int32, shape, dim)


def over(n, d):
    return lax.shift_right_logical(n, jnp.full(n.shape, d.bit_length() - 1, jnp.int32))


def dot(a, b):
    return jnp.dot(a, b, preferred_element_type=f32)


def dot_nt(a, b):
    return lax.dot_general(a, b, (((1,), (1,)), ((), ())), preferred_element_type=f32)


def cos_turn(turns):
    x = jnp.abs(turns - jnp.floor(turns) - 0.5) * 4.0 - 1.0
    x2 = x * x
    p = 0.00015148419
    for c in (-0.00467376557, 0.07968967928, -0.64596371106, 1.57079631847):
        p = p * x2 + c
    return p * x


def kernel(
    dims,
    tiles_ref, noise_ref, off_ref, slot_ref, cells_ref, spec_hbm,
    out_ref,
    spec, pre, hat, phase, ang, wang, tabf, tab, kmat,
    a_send, a_recv, b_send, row_b, col_b,
    e_send, e_recv, y_send, y_recv, far_send, far_recv,
    cur, prev, acc, scale,
    spec_sem, a_ss, a_rs, b_ss, b_rs, e_ss, e_rs, y_ss, y_rs, far_ss, far_rs,
):
    n_row, n_col, slots, xs, ys, glen, cap = dims
    nd = n_row * n_col
    xy = xs * ys
    cr = cap * nd // LANES
    kq = tab.shape[0]
    beads = n_col * TB
    me_r = lax.axis_index("row")
    me_c = lax.axis_index("col")
    me = me_r * n_col + me_c
    chunks = spec_sem.shape[0]
    part = xy // chunks
    per_row = LANES // nd

    def spec_copy(i):
        rows = pl.ds(i * part, part)
        return pltpu.make_async_copy(
            spec_hbm.at[:, rows, :], spec.at[:, rows, :], spec_sem.at[i]
        )

    for i in range(chunks):
        spec_copy(i).start()

    straight = nd <= 32
    if straight:
        rows_of = [me_r] + [lax.rem(me_r + d, n_row) for d in range(1, n_row)]
        cols_of = [me_c] + [lax.rem(me_c + d, n_col) for d in range(1, n_col)]
        order = sorted(
            [(i, j) for i in range(n_row) for j in range(n_col) if i + j],
            key=lambda t: (abs(t[1] - n_col // 2), abs(t[0] - n_row // 2)),
        )

    def each(body):
        if straight:
            for i, j in order:
                body(rows_of[i], cols_of[j])
            return

        def turn(d, carry):
            body(lax.rem(me_r + d // n_col, n_row), lax.rem(me_c + lax.rem(d, n_col), n_col))
            return carry

        lax.fori_loop(1, nd, turn, 0)

    def each_row(body):
        if straight:
            for d in range(1, n_row):
                body(rows_of[d])
        else:
            lax.fori_loop(1, n_row, lambda d, t: (body(lax.rem(me_r + d, n_row)), t)[1], 0)

    def each_col(body):
        if straight:
            for d in range(1, n_col):
                body(cols_of[d])
        else:
            lax.fori_loop(1, n_col, lambda d, t: (body(lax.rem(me_c + d, n_col)), t)[1], 0)

    barrier = pltpu.get_barrier_semaphore()

    def greet(r, c):
        pl.semaphore_signal(
            barrier, inc=1, device_id={"row": r, "col": c},
            device_id_type=pl.DeviceIdType.MESH,
        )

    each(greet)

    def remote(src, dst, ss, rs, r, c):
        return pltpu.make_async_remote_copy(
            src_ref=src, dst_ref=dst, send_sem=ss, recv_sem=rs,
            device_id={"row": r, "col": c}, device_id_type=pl.DeviceIdType.MESH,
        )

    def packed_cells():
        flat = cells_ref[...].astype(f32)
        if per_row == 1:
            return flat
        spread = (iota((nd, LANES), 1) & (nd - 1)) == iota((nd, LANES), 0)
        wide = jnp.dot(
            flat, spread.astype(f32), precision=lax.Precision.HIGHEST,
            preferred_element_type=f32,
        )
        mine = over(iota((cap, LANES), 1), nd) == (iota((cap, LANES), 0) & (per_row - 1))
        return jnp.sum(jnp.where(mine, wide, 0.0).reshape(cr, per_row, LANES), axis=1)

    a_send[0:1, :] = slot_ref[...].astype(f32)
    cells = packed_cells()
    a_send[1 : 1 + cr, :] = cells
    a_recv[me, 0:1, :] = slot_ref[...].astype(f32)
    a_recv[me, 1 : 1 + cr, :] = cells
    own_noise = jnp.concatenate([noise_ref[0], noise_ref[1], noise_ref[2]], axis=1)
    off = off_ref[...].astype(f32)
    own_off = jnp.concatenate([off[0:1], off[1:2], off[2:3]], axis=1)
    b_send[0:2, :] = own_noise
    b_send[2:3, :] = own_off
    row_b[me_c, 0:2, :] = own_noise
    row_b[me_c, 2:3, :] = own_off
    col_b[me_r, 0:2, :] = own_noise
    col_b[me_r, 2:3, :] = own_off
    tabf[...] = jnp.zeros_like(tabf)

    pl.semaphore_wait(barrier, nd - 1)

    def b_row_copy(c):
        return remote(b_send, row_b.at[me_c], b_ss.at[c], b_rs.at[me_c], me_r, c)

    def b_col_copy(r):
        return remote(
            b_send, col_b.at[me_r], b_ss.at[n_col + r], b_rs.at[n_col + me_r], r, me_c
        )

    each_col(lambda c: b_row_copy(c).start())
    each_row(lambda r: b_col_copy(r).start())

    def a_copy(r, c):
        p = r * n_col + c
        return remote(a_send, a_recv.at[me], a_ss.at[p], a_rs.at[me], r, c)

    each(lambda r, c: a_copy(r, c).start())

    gi = iota((2 * glen, 2 * glen), 0)
    gj = iota((2 * glen, 2 * glen), 1)
    zi, zj = gi & (glen - 1), gj & (glen - 1)
    in_im, out_im = gi >= glen, gj >= glen
    half = glen // 2
    same = zi == zj
    mirror = (zi + zj == glen) & (zi != zj)
    even = zj <= half
    plain = in_im == out_im
    fold = jnp.where(
        even,
        jnp.where(plain & (same | mirror), 1.0, 0.0),
        jnp.where(
            plain,
            0.0,
            jnp.where(same, 1.0, 0.0) - jnp.where(mirror, 1.0, 0.0),
        )
        * jnp.where(out_im, -1.0, 1.0),
    ).astype(bf16)

    width_sq = (glen / 8.0) ** 2
    front = math.sqrt(1.5) / (2.0 * math.pi * width_sq) ** 0.75
    def signed(n):
        return jnp.where(n < half, n, n - glen).astype(f32)

    ky = signed(me_c * ys + iota((ys, glen), 0))
    kz = signed(iota((ys, glen), 1))
    kyz_sq = ky * ky + kz * kz

    def hat_block(i, first):
        kx = signed(me_r * xs + i)
        q = kx * kx + kyz_sq
        amp = jnp.where(q > 0, front * jnp.exp(q * (-0.25 / width_sq)), 0.0)
        damp = amp / jnp.maximum(q, 1.0)
        rows = pl.ds(pl.multiple_of(i * ys, ys), ys)
        at = pl.multiple_of((i - first) * ys, ys)
        waves = (kx, ky, kz)
        for v in range(2):
            for p in range(2):
                s = [spec[(p * 3 + a) * 2 + v, rows, :] for a in range(3)]
                along = (kx * s[0] + ky * s[1] + kz * s[2]) * damp
                for a in range(3):
                    pre[pl.ds((a * 2 + v) * part + at, ys), p * glen : (p + 1) * glen] = (
                        amp * s[a] - waves[a] * along
                    ).astype(bf16)
        return first

    per = part // ys
    for i in range(chunks):
        spec_copy(i).wait()
        lax.fori_loop(i * per, (i + 1) * per, hat_block, i * per)
        folded = dot(pre[...], fold)
        for k in range(6):
            for p in range(2):
                hat[
                    p * xy + i * part : p * xy + (i + 1) * part, k * glen : (k + 1) * glen
                ] = folded[
                    k * part : (k + 1) * part, p * glen : (p + 1) * glen
                ].astype(bf16)

    def b_col_arrive(r):
        remote(b_send, col_b.at[r], b_ss.at[n_col + r], b_rs.at[n_col + r], r, me_c).wait_recv()

    def b_row_arrive(c):
        remote(b_send, row_b.at[c], b_ss.at[c], b_rs.at[c], me_r, c).wait_recv()

    each_row(b_col_arrive)
    each_col(b_row_arrive)

    eye = (iota((TB, TB), 0) == iota((TB, TB), 1)).astype(f32)
    ones = jnp.ones((TB, TB), bf16)
    scale_sq = kernel_range * kernel_range

    def pick(values, into, s):
        tr = tiles_ref[0, s]
        return tuple(
            into[i] + values * jnp.where(tr == i, 1.0, 0.0).astype(f32) for i in range(n_col)
        )

    def build(s, energies):
        tr = jnp.maximum(tiles_ref[0, s], 0)
        tc = jnp.maximum(tiles_ref[1, s], 0)
        row_off = row_b[tr][2:3, :]
        col_off = col_b[tc][2:3, :]
        disp = []
        for a in range(3):
            lanes = slice(a * TB, (a + 1) * TB)
            rp = dot((eye * row_off[:, lanes]).astype(bf16), ones)
            gap = (rp - col_off[:, lanes]).astype(jnp.int32) + PERIOD // 2
            disp.append(((gap & (PERIOD - 1)) - PERIOD // 2).astype(f32))
        squares = disp[0] * disp[0] + disp[1] * disp[1] + disp[2] * disp[2]
        envelope = jnp.exp(squares * (-0.5 / scale_sq)) / scale_sq
        third = squares / 3.0
        for a in range(3):
            for b in range(a, 3):
                element = disp[a] * disp[b]
                if a == b:
                    element = element - third
                entry = (envelope * element).astype(bf16)
                kmat[s, a * TB : (a + 1) * TB, b * TB : (b + 1) * TB] = entry
                if a != b:
                    kmat[s, b * TB : (b + 1) * TB, a * TB : (a + 1) * TB] = entry
        wide = kmat[s].astype(f32)
        sq = wide * wide
        high = sq.astype(bf16)
        low = (sq - high.astype(f32)).astype(bf16)
        one_row = jnp.ones((8, 3 * TB), bf16)
        energy = dot_nt(one_row, high) + dot_nt(one_row, low)
        return pick(energy[0:1], energies, s)

    energies = lax.fori_loop(
        0, slots, build, tuple(jnp.zeros((1, 3 * TB), f32) for _ in range(n_col)),
        unroll=slots <= 4,
    )
    for i in range(n_col):
        e_send[i : i + 1, :] = energies[i]
        e_recv[me, i : i + 1, :] = energies[i]

    def e_copy(r, c):
        p = r * n_col + c
        return remote(e_send, e_recv.at[me], e_ss.at[p], e_rs.at[me], r, c)

    for r in range(n_row):
        cur[r] = col_b[r, 0:2, :]
    acc[...] = cheb_coef[0] * own_noise

    def a_arrive(r, c):
        p = r * n_col + c
        remote(a_send, a_recv.at[p], a_ss.at[p], a_rs.at[p], r, c).wait_recv()

    def prepare_table():
        each(a_arrive)

        def spread(h, carry):
            tabf[pl.ds(h * cr, cr), :] = a_recv[h, 1 : 1 + cr, :]
            return carry

        lax.fori_loop(0, nd, spread, 0)
        cell = tabf[...].astype(jnp.int32)
        y_slab, z_slab = glen // n_row, glen // n_col
        holder = over(iota((kq, LANES), 0), cr)
        pos_x = over(cell, y_slab * z_slab)
        pos_y = over(holder, n_col) * y_slab + (over(cell, z_slab) & (y_slab - 1))
        pos_z = (holder & (n_col - 1)) * z_slab + (cell & (z_slab - 1))
        for at, pos in enumerate((pos_x, pos_y, pos_z)):
            tab[:, at * LANES : (at + 1) * LANES] = pos.astype(f32).astype(bf16)

    x_step = LANES // ys
    lane = iota((LANES, LANES), 1)
    scaled = 1.0 / glen
    along_x = ((me_r * xs + over(lane, ys)).astype(f32) * scaled).astype(bf16)
    along_y = ((me_c * ys + (lane & (ys - 1))).astype(f32) * scaled).astype(bf16)
    wang[...] = jnp.zeros_like(wang)
    wang[0:LANES, 0:LANES] = along_x
    wang[LANES : 2 * LANES, 0:LANES] = along_y
    wang[0:LANES, LANES : 2 * LANES] = jnp.full((LANES, LANES), x_step * scaled, bf16)
    wang[2 * LANES :, 2 * LANES :] = (lane.astype(f32) * scaled).astype(bf16)
    rep = over(iota((8, 6 * glen), 1), glen) == iota((8, 6 * glen), 0)
    rep = rep.astype(f32).astype(bf16)
    wide_ones = jnp.ones((TB, kq), bf16)
    step_rows = 32

    def far_copy(i, c):
        return remote(
            far_send.at[i * n_col + c], far_recv.at[me],
            far_ss.at[i * n_col + c], far_rs.at[me], i, c,
        )

    def far_chunk(i, carry):
        spots = jnp.concatenate(
            [eye * a_recv[i * n_col + c, 0:1, :] for c in range(n_col)], axis=0
        ).astype(bf16)
        code = dot(spots, wide_ones).astype(jnp.int32)
        s_idx = over(code, nd)
        row_idx = (code & (nd - 1)) * cr + over(s_idx, per_row)
        hot = (row_idx == iota((beads, kq), 1)).astype(f32).astype(bf16)
        found = dot(hot, tab[...])
        owner_of = i * n_col + over(iota((beads, LANES), 0), TB)
        want = (s_idx[:, :LANES] & (per_row - 1)) * nd + owner_of
        keep = want == iota((beads, LANES), 1)
        places = jnp.concatenate(
            [jnp.where(keep, found[:, k * LANES : (k + 1) * LANES], 0.0) for k in range(3)],
            axis=1,
        ).astype(bf16)
        ang[...] = dot(places, wang[...])

        def phase_block(j, carry):
            rows = pl.ds(pl.multiple_of(j * step_rows, step_rows), step_rows)
            at_lane = iota((step_rows, LANES), 1)
            start = ang[rows, 0:LANES]
            co = cos_turn(start)
            ns = cos_turn(start + 0.25)
            turn_x = cos_turn(
                ang[rows, LANES : 2 * LANES] - jnp.where(at_lane == 1, 0.25, 0.0)
            )
            cd = jnp.broadcast_to(turn_x[:, 0:1], co.shape)
            sd = jnp.broadcast_to(turn_x[:, 1:2], co.shape)
            ang[rows, 2 * LANES :] = cos_turn(
                ang[rows, 2 * LANES :] + jnp.where(at_lane > half, 0.25, 0.0)
            )
            for g in range(xy // LANES):
                phase[rows, g * LANES : (g + 1) * LANES] = co.astype(bf16)
                phase[rows, xy + g * LANES : xy + (g + 1) * LANES] = ns.astype(bf16)
                co, ns = co * cd + ns * sd, ns * cd - co * sd
            return carry

        lax.fori_loop(0, beads // step_rows, phase_block, 0)
        sums = dot(phase[...], hat[...])
        tz = ang[:, 2 * LANES :]
        weighted = jnp.concatenate(
            [(sums[:, k * glen : (k + 1) * glen] * tz).astype(bf16) for k in range(6)], axis=1
        )
        res = dot_nt(rep, weighted)
        for c in range(n_col):
            owner = i * n_col + c
            far_send[owner] = res[:, c * TB : (c + 1) * TB]

            @pl.when(owner == me)
            def _():
                far_recv[me] = res[:, c * TB : (c + 1) * TB]

            @pl.when(owner != me)
            def _():
                far_copy(i, c).start()

        return carry

    def y_copy(r, c, par):
        p = r * n_col + c
        return remote(
            y_send.at[par, c], y_recv.at[par, me], y_ss.at[par, p], y_rs.at[par, me], r, c
        )

    def y_arrive(r, c, par):
        p = r * n_col + c
        remote(
            y_send.at[par, 0], y_recv.at[par, p], y_ss.at[par, p], y_rs.at[par, p], r, c
        ).wait_recv()

    each(lambda r, c: e_copy(r, c).start())

    def degree_step(m, carry):
        par = lax.rem(m, 2)

        def apply(s, sums):
            tc = jnp.maximum(tiles_ref[1, s], 0)
            w = cur[tc]
            w = jnp.concatenate([w, jnp.zeros((6, 3 * TB), f32)], axis=0).astype(bf16)
            return pick(dot_nt(w, kmat[s])[0:2], sums, s)

        sums = lax.fori_loop(
            0, slots, apply, tuple(jnp.zeros((2, 3 * TB), f32) for _ in range(n_col)),
            unroll=slots <= 4,
        )
        own = jnp.zeros((2, 3 * TB), f32)
        for i in range(n_col):
            y_send[par, i] = sums[i]
            own = own + sums[i] * jnp.where(me_c == i, 1.0, 0.0).astype(f32)
        y_recv[par, me] = own
        each(lambda r, c: y_copy(r, c, par).start())

        @pl.when(m == 0)
        def _():
            prepare_table()

        lax.fori_loop(m * n_row // DEGREES, (m + 1) * n_row // DEGREES, far_chunk, 0)

        @pl.when(m == 0)
        def _():
            def e_arrive(r, c):
                p = r * n_col + c
                remote(e_send, e_recv.at[p], e_ss.at[p], e_rs.at[p], r, c).wait_recv()

            each(e_arrive)
            top = jnp.zeros((n_col, 3 * TB), f32)
            for r in range(n_row):
                total = e_recv[r * n_col]
                for c in range(1, n_col):
                    total = total + e_recv[r * n_col + c]
                top = jnp.maximum(top, total)
            largest = jnp.max(jnp.max(top, axis=1, keepdims=True), axis=0, keepdims=True)
            scale[...] = jnp.broadcast_to(1.0 / jnp.sqrt(largest + 1e-06), scale.shape)

        each(lambda r, c: y_arrive(r, c, par))
        each(lambda r, c: y_copy(r, c, par).wait_send())
        first = jnp.where(m == 0, 1.0, 0.0).astype(f32)
        coef = jnp.where(
            m == 0, cheb_coef[1],
            jnp.where(m == 1, cheb_coef[2], jnp.where(m == 2, cheb_coef[3], cheb_coef[4])),
        ).astype(f32)
        sc = jnp.concatenate([scale[0:2, :]] * 3, axis=1)

        def advance(r, carry):
            total = y_recv[par, r * n_col]
            for c in range(1, n_col):
                total = total + y_recv[par, r * n_col + c]
            now = sc * total
            following = jnp.where(m == 0, now, 2.0 * now - prev[r])
            prev[r] = cur[r]
            cur[r] = following
            return carry

        lax.fori_loop(0, n_row, advance, 0)
        acc[...] = acc[...] + coef * cur[me_r]
        return carry

    prev[...] = jnp.zeros_like(prev)
    lax.fori_loop(0, DEGREES, degree_step, 0)

    each_row(lambda r: b_col_copy(r).wait_send())
    each_col(lambda c: b_row_copy(c).wait_send())
    each(lambda r, c: a_copy(r, c).wait_send())
    each(lambda r, c: e_copy(r, c).wait_send())

    def far_arrive(r, c):
        p = r * n_col + c
        remote(
            far_send.at[p], far_recv.at[p], far_ss.at[p], far_rs.at[p], r, c
        ).wait_recv()

    each(far_arrive)
    each(lambda r, c: far_copy(r, c).wait_send())
    far = lax.fori_loop(
        1, nd, lambda p, t: t + far_recv[p], far_recv[0]
    )
    near = acc[...]
    for a in range(3):
        out_ref[a] = near[:, a * TB : (a + 1) * TB] + far[2 * a : 2 * a + 2, :]


def spread_device(noise_field, offsets, tile_list, send_cells, bead_slot, spectral):
    n_row = lax.axis_size("row")
    n_col = lax.axis_size("col")
    nd = n_row * n_col
    xs, ys, glen = spectral.shape[3:]
    slots = tile_list.shape[3]
    cap = send_cells.shape[2]
    cr = cap * nd // LANES
    xy = xs * ys
    kq = max(LANES, nd * cr)
    beads = n_col * TB
    a_rows = -(-(1 + cr) // 4) * 4
    chunks = 4 if xy % 256 == 0 else 1
    dims = (n_row, n_col, slots, xs, ys, glen, cap)
    vmem = pl.BlockSpec(memory_space=pltpu.VMEM)
    dma = pltpu.SemaphoreType.DMA
    wide = 3 * TB
    return pl.pallas_call(
        functools.partial(kernel, dims),
        out_shape=jax.ShapeDtypeStruct(noise_field.shape, f32),
        in_specs=[pl.BlockSpec(memory_space=pltpu.SMEM), vmem, vmem, vmem, vmem,
                  pl.BlockSpec(memory_space=pl.ANY)],
        out_specs=vmem,
        scratch_shapes=[
            pltpu.VMEM((12, xy, glen), f32),
            pltpu.VMEM((6 * (xy // chunks), 2 * glen), bf16),
            pltpu.VMEM((2 * xy, 6 * glen), bf16),
            pltpu.VMEM((beads, 2 * xy), bf16),
            pltpu.VMEM((beads, 3 * LANES), f32),
            pltpu.VMEM((3 * LANES, 3 * LANES), bf16),
            pltpu.VMEM((kq, LANES), f32),
            pltpu.VMEM((kq, 3 * LANES), bf16),
            pltpu.VMEM((slots, wide, wide), bf16),
            pltpu.VMEM((a_rows, LANES), f32),
            pltpu.VMEM((nd, a_rows, LANES), f32),
            pltpu.VMEM((4, wide), f32),
            pltpu.VMEM((n_col, 4, wide), f32),
            pltpu.VMEM((n_row, 4, wide), f32),
            pltpu.VMEM((n_col, wide), f32),
            pltpu.VMEM((nd, n_col, wide), f32),
            pltpu.VMEM((2, n_col, 2, wide), f32),
            pltpu.VMEM((2, nd, 2, wide), f32),
            pltpu.VMEM((nd, 8, TB), f32),
            pltpu.VMEM((nd, 8, TB), f32),
            pltpu.VMEM((n_row, 2, wide), f32),
            pltpu.VMEM((n_row, 2, wide), f32),
            pltpu.VMEM((2, wide), f32),
            pltpu.VMEM((8, LANES), f32),
            dma((chunks,)),
            dma((nd,)), dma((nd,)),
            dma((n_row + n_col,)), dma((n_row + n_col,)),
            dma((nd,)), dma((nd,)),
            dma((2, nd)), dma((2, nd)),
            dma((nd,)), dma((nd,)),
        ],
        compiler_params=pltpu.CompilerParams(
            collective_id=0, has_side_effects=True, vmem_limit_bytes=56 * 1024 * 1024
        ),
    )(
        tile_list.reshape(2, slots),
        noise_field,
        offsets,
        bead_slot.reshape(1, TB),
        send_cells.reshape(cap, nd),
        spectral.reshape(12, xy, glen),
    )


PLANES = PERIOD // 2 + 1
FLAT = PERIOD * PERIOD
MODES = PLANES * 2 * FLAT
PAIRS = ((0, 0), (1, 1), (2, 2), (0, 1), (0, 2), (1, 2))


def lattice_spectrum():
    code = np.arange(PERIOD**3)
    site = np.stack([code // FLAT, code // PERIOD % PERIOD, code % PERIOD])
    disp = (site + PERIOD // 2) % PERIOD - PERIOD // 2
    d = disp.astype(np.float32)
    squares = d[0] * d[0] + d[1] * d[1] + d[2] * d[2]
    scale_sq = np.float32(kernel_range * kernel_range)
    envelope = np.exp(squares * np.float32(-0.5 / scale_sq)) / scale_sq
    table = np.zeros((3, 3, PERIOD**3))
    for a, b in PAIRS:
        element = d[a] * d[b]
        if a == b:
            element = element - squares / np.float32(3.0)
        table[a, b] = (envelope * element).astype(ml_dtypes.bfloat16).astype(np.float64)
        table[b, a] = table[a, b]
    energy = (table * table).sum(axis=1)
    qz = np.arange(PLANES)[:, None, None, None]
    part = np.arange(2)[None, :, None, None]
    qx = np.arange(PERIOD)[None, None, :, None]
    qy = np.arange(PERIOD)[None, None, None, :]
    qx, qy, qz, part = (t.reshape(-1) for t in np.broadcast_arrays(qx, qy, qz, part))
    angle = 2.0 * np.pi / PERIOD * ((np.stack([qx, qy, qz], 1) @ site) % PERIOD)
    weight = np.where((qz == 0) | (qz == PERIOD // 2), 1.0, 2.0) / PERIOD**3
    turn = np.where(part == 0, 1.0, -1.0)
    rows = [weight * (np.cos(angle) @ table[p]) for p in PAIRS]
    rows += [-turn * weight * (np.sin(angle) @ table[p]) for p in PAIRS[3:]]
    rows += [weight * (np.cos(angle) @ energy[a]) for a in range(3)]
    rows += [np.zeros(MODES)] * (-len(rows) % 8)
    return np.stack(rows).astype(np.float32)


def shared_kernel(
    dims,
    tiles_hbm, noise_hbm, off_hbm, slot_hbm, cells_hbm, spectrum_hbm, spec_hbm,
    out_ref,
    tiles_ref, noise_ref, off_ref, slot_ref, cells_ref,
    spec, pre, hat, phase_a, phase_b, phi, modes, wide, cheb_a, cheb_b, mixer, mixed, lattice,
    msg_f, msg, inbox, table, offs, spectrum, last,
    far_send, far_recv,
    load_sem, spec_sem, spectrum_sem, m_ss, m_rs, far_ss, far_rs,
):
    n_row, n_col, slots, xs, ys, glen, cap = dims
    nd = n_row * n_col
    xy = xs * ys
    per_row = LANES // nd
    cr = cap // per_row
    cells_at = 10
    tile_at = cells_at + 2 * cr
    beads = nd * TB
    me_r = lax.axis_index("row")
    me_c = lax.axis_index("col")
    me = me_r * n_col + me_c
    chunks = spec_sem.shape[0]
    part = xy // chunks
    nb = 2 * nd
    rows_t = 3 * nb
    rows_e = rows_t + nd

    def spec_copy(i):
        rows = pl.ds(i * part, part)
        return pltpu.make_async_copy(
            spec_hbm.at[:, rows, :], spec.at[:, rows, :], spec_sem.at[i]
        )

    loads = [
        pltpu.make_async_copy(src, dst, load_sem.at[k])
        for k, (src, dst) in enumerate((
            (cells_hbm, cells_ref), (tiles_hbm, tiles_ref), (noise_hbm, noise_ref),
            (off_hbm, off_ref), (slot_hbm, slot_ref),
        ))
    ]

    peers = sorted(
        [(i, j) for i in range(n_row) for j in range(n_col)], key=lambda t: (-t[1], -t[0])
    )
    others = peers[:-1]

    def place(i, j):
        return jnp.bitwise_xor(me_r, i), jnp.bitwise_xor(me_c, j)

    barrier = pltpu.get_barrier_semaphore()
    for i, j in others:
        r, c = place(i, j)
        pl.semaphore_signal(
            barrier, inc=1, device_id={"row": r, "col": c},
            device_id_type=pl.DeviceIdType.MESH,
        )
    for load in loads:
        load.start()
    for i in range(chunks):
        spec_copy(i).start()
    spectrum_copy = pltpu.make_async_copy(spectrum_hbm, spectrum, spectrum_sem)
    spectrum_copy.start()

    def remote(src, dst, ss, rs, r, c):
        return pltpu.make_async_remote_copy(
            src_ref=src, dst_ref=dst, send_sem=ss, recv_sem=rs,
            device_id={"row": r, "col": c}, device_id_type=pl.DeviceIdType.MESH,
        )

    for load in loads:
        load.wait()
    for a in range(3):
        msg_f[2 * a : 2 * a + 2, :] = noise_ref[a]
    msg_f[6:9, :] = off_ref[...].astype(f32)
    msg_f[9:10, :] = slot_ref[...].astype(f32)
    spread = over(iota((nd, LANES), 1), per_row) == iota((nd, LANES), 0)
    spread = spread.astype(f32).astype(bf16)
    keep = (iota((cap, LANES), 1) & (per_row - 1)) == (iota((cap, LANES), 0) & (per_row - 1))
    cells = cells_ref[...]
    for h, half_cell in enumerate((over(cells, 512), (cells & 511) - 256)):
        out = dot(half_cell.astype(f32).astype(bf16), spread)
        out = jnp.sum(jnp.where(keep, out, 0.0).reshape(cr, per_row, LANES), axis=1)
        msg_f[cells_at + h * cr : cells_at + (h + 1) * cr, :] = out
    lane_row = iota((1, LANES), 1)
    row_list = jnp.zeros((1, LANES), jnp.int32)
    col_list = jnp.zeros((1, LANES), jnp.int32)
    for s in range(slots):
        here = lane_row == me * slots + s
        tr, tc = tiles_ref[0, s], tiles_ref[1, s]
        row_list = jnp.where(
            here & (jnp.full((1, LANES), tr) >= 0), me_r * n_col + tr + 1, row_list
        )
        col_list = jnp.where(here, tc * n_col + me_c + 1, col_list)
    msg_f[tile_at : tile_at + 1, :] = row_list.astype(f32)
    msg_f[tile_at + 1 : tile_at + 2, :] = col_list.astype(f32)
    if tile_at + 2 < msg_f.shape[0]:
        msg_f[tile_at + 2 :, :] = jnp.zeros((msg_f.shape[0] - tile_at - 2, LANES), f32)
    msg[...] = msg_f[...].astype(bf16)
    inbox[me] = msg_f[...].astype(bf16)

    pl.semaphore_wait(barrier, nd - 1)

    def msg_copy(i, j):
        r, c = place(i, j)
        p = i * n_col + j
        return remote(msg, inbox.at[me], m_ss.at[p], m_rs.at[me], r, c)

    def msg_arrive(i, j):
        r, c = place(i, j)
        p = r * n_col + c
        remote(msg, inbox.at[p], m_ss.at[0], m_rs.at[p], r, c).wait_recv()

    for i, j in others:
        msg_copy(i, j).start()

    wide[...] = jnp.zeros_like(wide)
    mixed[...] = jnp.zeros_like(mixed)
    cheb_a[...] = jnp.zeros_like(cheb_a)
    for o in range(nd):
        ones = (iota((nd, TB), 0) == o).astype(f32)
        wide[rows_t:rows_e, o * TB : (o + 1) * TB] = ones.astype(bf16)

    gj = iota((2 * glen, 2 * glen), 0)
    gi = iota((2 * glen, 2 * glen), 1)
    zi, zj = gi & (glen - 1), gj & (glen - 1)
    in_im, out_im = gi >= glen, gj >= glen
    half = glen // 2
    same = zi == zj
    mirror = (zi + zj == glen) & (zi != zj)
    even = zj <= half
    plain = in_im == out_im
    fold = jnp.where(
        even,
        jnp.where(plain & (same | mirror), 1.0, 0.0),
        jnp.where(
            plain,
            0.0,
            jnp.where(same, 1.0, 0.0) - jnp.where(mirror, 1.0, 0.0),
        )
        * jnp.where(out_im, -1.0, 1.0),
    ).astype(bf16)

    width_sq = (glen / 8.0) ** 2
    front = math.sqrt(1.5) / (2.0 * math.pi * width_sq) ** 0.75

    def signed(n):
        return jnp.where(n < half, n, n - glen).astype(f32)

    ky = signed(me_c * ys + iota((ys, glen), 0))
    kz = signed(iota((ys, glen), 1))
    kyz_sq = ky * ky + kz * kz

    def hat_block(i, first):
        kx = signed(me_r * xs + i)
        q = kx * kx + kyz_sq
        amp = jnp.where(q > 0, front * jnp.exp(q * (-0.25 / width_sq)), 0.0)
        damp = amp / jnp.maximum(q, 1.0)
        rows = pl.ds(pl.multiple_of(i * ys, ys), ys)
        at = pl.multiple_of((i - first) * ys, ys)
        waves = (kx, ky, kz)
        for v in range(2):
            for p in range(2):
                s = [spec[(p * 3 + a) * 2 + v, rows, :] for a in range(3)]
                along = (kx * s[0] + ky * s[1] + kz * s[2]) * damp
                for a in range(3):
                    pre[pl.ds((a * 2 + v) * part + at, ys), p * glen : (p + 1) * glen] = (
                        amp * s[a] - waves[a] * along
                    ).astype(bf16)
        return first

    per = part // ys
    for i in range(chunks):
        spec_copy(i).wait()
        lax.fori_loop(i * per, (i + 1) * per, hat_block, i * per)
        for k in range(6):
            folded = dot_nt(fold, pre[k * part : (k + 1) * part, :]).astype(bf16)
            for p in range(2):
                hat[
                    k * glen : (k + 1) * glen, p * xy + i * part : p * xy + (i + 1) * part
                ] = folded[p * glen : (p + 1) * glen, :]

    spectrum_copy.wait()
    for i, j in others[::-1]:
        msg_arrive(i, j)

    row_list = jnp.zeros((1, LANES), f32)
    col_list = jnp.zeros((1, LANES), f32)
    slot_rows = nb // 2 * cr
    for o in range(nd):
        got = inbox[o].astype(f32)
        row_list = row_list + got[tile_at : tile_at + 1]
        col_list = col_list + got[tile_at + 1 : tile_at + 2]
        for h in range(2):
            table[h, o * cr : (o + 1) * cr, :] = got[
                cells_at + h * cr : cells_at + (h + 1) * cr
            ]
        offs[:, o * TB : (o + 1) * TB] = got[6:9]
        first = 2 * o % 16
        base = 2 * o // 16 * 16
        for a in range(3):
            cheb_a[a, o, first : first + 2, :] = got[2 * a : 2 * a + 2]
            wide[a * nb + base : a * nb + base + 16, o * TB : (o + 1) * TB] = (
                cheb_a[a, o].astype(bf16)
            )
    tables = []
    for h in range(2):
        tables.append(jnp.transpose(table[h])[:, :slot_rows])
    for h in range(2):
        table[2 + h, :, :slot_rows] = tables[h]

    def kind_of(n):
        return jnp.where(n < rows_t, over(n, nb) * 2 + (n & 1), 6)

    def owner_of(n):
        return jnp.where(n < rows_t, over(n & (nb - 1), 2), n - rows_t)

    mix_rows = iota((rows_e, LANES), 0)
    mix_lanes = iota((rows_e, LANES), 1)
    all_rows = iota((LANES, LANES), 0)
    to = ((owner_of(mix_rows) + 1).astype(f32) == row_list).astype(f32).astype(bf16)
    frm = ((owner_of(all_rows) + 1).astype(f32) == col_list).astype(f32).astype(bf16)
    joined = jnp.where(
        (kind_of(mix_rows) == kind_of(mix_lanes)) & (mix_lanes < rows_e), dot_nt(to, frm), 0.0
    ).astype(bf16)
    mixer[:, :LANES] = joined
    mixer[:, LANES:] = joined

    def build_phi(o):
        lanes = slice(o * TB, (o + 1) * TB)
        q = iota((PERIOD, TB), 0).astype(f32) * (1.0 / PERIOD)
        co, si = [], []
        for a in range(3):
            turn = q * offs[a : a + 1, lanes]
            co.append(cos_turn(turn))
            si.append(cos_turn(turn - 0.25))
        flat_c, flat_s = [], []
        for x in range(PERIOD):
            cx, sx = co[0][x : x + 1], si[0][x : x + 1]
            flat_c.append(cx * co[1] - sx * si[1])
            flat_s.append(sx * co[1] + cx * si[1])
        flat_c = jnp.concatenate(flat_c, axis=0)
        flat_s = jnp.concatenate(flat_s, axis=0)
        for z in range(PLANES):
            cz, sz = co[2][z : z + 1], si[2][z : z + 1]
            at = z * 2 * FLAT
            block = jnp.concatenate([flat_c * cz - flat_s * sz, flat_s * cz + flat_c * sz], axis=0)
            phi[at : at + 2 * FLAT, lanes] = block.astype(bf16)
            modes[lanes, at : at + 2 * FLAT] = jnp.transpose(block).astype(bf16)

    y_slab, z_slab = glen // n_row, glen // n_col
    scaled = 1.0 / glen

    def locate(r, c):
        o = r * n_col + c
        code = inbox[o].astype(f32)[9:10].astype(jnp.int32)
        slot = over(code, nd)
        holder = code & (nd - 1)
        row_at = holder * cr + over(slot, per_row)
        hot = (iota((slot_rows, TB), 0) == row_at).astype(f32).astype(bf16)
        at = pl.ds(pl.multiple_of(o * per_row, per_row), per_row)
        lists = jnp.concatenate(
            [table[2, at, :slot_rows], table[3, at, :slot_rows]], axis=0
        ).astype(bf16)
        found = dot(lists, hot)
        mine = iota((per_row, TB), 0) == (slot & (per_row - 1))
        high = jnp.sum(jnp.where(mine, found[:per_row], 0.0), axis=0, keepdims=True)
        low = jnp.sum(jnp.where(mine, found[per_row:], 0.0), axis=0, keepdims=True)
        cell = high.astype(jnp.int32) * 512 + low.astype(jnp.int32) + 256
        pos_x = over(cell, y_slab * z_slab)
        pos_y = over(holder, n_col) * y_slab + (over(cell, z_slab) & (y_slab - 1))
        pos_z = (holder & (n_col - 1)) * z_slab + (cell & (z_slab - 1))
        return [p.astype(f32) * scaled for p in (pos_x, pos_y, pos_z)]

    kx_col = (me_r * xs + iota((xs, 2 * TB), 0)).astype(f32)
    ky_col = (me_c * ys + iota((ys, 2 * TB), 0)).astype(f32)
    kz_col = iota((glen, 2 * TB), 0)

    def build_phase(pair, phase):
        spots = [locate(*place(i, j)) for i, j in pair]
        px, py, pz = (
            jnp.concatenate([spots[0][t], spots[1][t]], axis=1) for t in range(3)
        )
        turn = kx_col * px
        cx, nx = cos_turn(turn), cos_turn(turn + 0.25)
        turn = ky_col * py
        cy, ny = cos_turn(turn), cos_turn(turn + 0.25)
        for i in range(xs):
            a, b = cx[i : i + 1], nx[i : i + 1]
            phase[i * ys : (i + 1) * ys, :] = (a * cy - b * ny).astype(bf16)
            phase[xy + i * ys : xy + (i + 1) * ys, :] = (b * cy + a * ny).astype(bf16)
        return cos_turn(kz_col.astype(f32) * pz + jnp.where(kz_col > half, 0.25, 0.0))

    def far_copy(i, j):
        r, c = place(i, j)
        p = r * n_col + c
        q = i * n_col + j
        return remote(far_send.at[q], far_recv.at[me], far_ss.at[q], far_rs.at[me], r, c)

    def far_sums(pair, phase, tz):
        sums = dot(hat[...], phase[...])
        for k in range(6):
            line = jnp.sum(sums[k * glen : (k + 1) * glen] * tz, axis=0, keepdims=True)
            for t, (i, j) in enumerate(pair):
                half_line = line[:, t * TB : (t + 1) * TB]
                if i + j:
                    far_send[i * n_col + j, k : k + 1, :] = half_line
                else:
                    far_recv[me, k : k + 1, :] = half_line
        for i, j in pair:
            if i + j:
                far_copy(i, j).start()

    near = [cheb_coef[0] * noise_ref[a] for a in range(3)]
    own_rows = pl.ds(lax.rem(2 * me, 16), 2)
    scales = []

    def to_modes(m):
        rows = rows_e if m == 0 else rows_t
        sums = dot(wide[0:rows, :], modes[...])
        high = sums.astype(bf16)
        mixed[0:rows, :] = high
        mixed[LANES : LANES + rows, :] = (sums - high.astype(f32)).astype(bf16)

    def convolve(m):
        rows = rows_e if m == 0 else rows_t
        sums = dot(mixer[0:rows, :], mixed[...])
        turned = jnp.concatenate(
            [
                pltpu.roll(sums[0:rows_t, g * LANES : (g + 1) * LANES], FLAT, 1)
                for g in range(PLANES)
            ],
            axis=1,
        )
        for a in range(3):
            total = spectrum[a : a + 1, :] * sums[a * nb : (a + 1) * nb]
            for b in range(3):
                if a != b:
                    e = PAIRS.index((min(a, b), max(a, b)))
                    total = total + spectrum[e : e + 1, :] * sums[b * nb : (b + 1) * nb]
                    total = total + spectrum[e + 3 : e + 4, :] * turned[b * nb : (b + 1) * nb]
            lattice[a * nb : (a + 1) * nb, :] = total.astype(bf16)
        if m == 0:
            for a in range(3):
                total = spectrum[9 + a : 10 + a, :] * sums[rows_t:rows_e]
                high = total.astype(bf16)
                at = rows_t + a * nd
                lattice[at : at + nd, :] = high
                lattice[at + 3 * nd : at + 4 * nd, :] = (total - high.astype(f32)).astype(bf16)

    def to_beads(m):
        if m == 0:
            out = dot(lattice[...], phi[...])
            energy = out[rows_t : rows_t + 3 * nd] + out[rows_t + 3 * nd :]
            top = jnp.zeros((3 * nd, TB), f32)
            owner = iota((3 * nd, TB), 0) & (nd - 1)
            for o in range(nd):
                top = jnp.maximum(
                    top, jnp.where(owner == o, energy[:, o * TB : (o + 1) * TB], 0.0)
                )
            top = jnp.max(jnp.max(top, axis=1, keepdims=True), axis=0, keepdims=True)
            scales.append(jnp.broadcast_to(1.0 / jnp.sqrt(top + 1e-06), (16, TB)))
        elif m < DEGREES - 1:
            out = dot(lattice[0:rows_t, :], phi[...])
        scale = scales[0]
        before = cheb_b if m % 2 == 0 else cheb_a
        if m < DEGREES - 1:
            line = iota((16, TB), 0)
            for o in range(nd):
                first = 2 * o % 16
                base = 2 * o // 16 * 16
                mine = (line >= first) & (line < first + 2)
                for a in range(3):
                    got = out[a * nb + base : a * nb + base + 16, o * TB : (o + 1) * TB]
                    got = jnp.where(mine, scale * got, 0.0)
                    if m > 0:
                        got = 2.0 * got - before[a, o]
                    before[a, o] = got
                    wide[a * nb + base : a * nb + base + 16, o * TB : (o + 1) * TB] = (
                        got.astype(bf16)
                    )
            for a in range(3):
                near[a] = near[a] + cheb_coef[m + 1] * before[a, me, own_rows, :]
        else:
            last[...] = dot(
                lattice[0:rows_t, :], phi[:, pl.ds(pl.multiple_of(me * TB, TB), TB)]
            )
            for a in range(3):
                got = 2.0 * (scale[0:2] * last[pl.ds(a * nb + 2 * me, 2), :])
                near[a] = near[a] + cheb_coef[m + 1] * (got - before[a, me, own_rows, :])

    stages = [
        functools.partial(stage, m)
        for m in range(DEGREES) for stage in (to_modes, convolve, to_beads)
    ]
    pairs = [peers[t : t + 2] for t in range(0, nd, 2)]
    phases = (phase_a, phase_b)
    built = -(-3 * len(pairs) // 8)
    tz = build_phase(pairs[0], phase_a)
    for n, pair in enumerate(pairs):
        nxt = None
        if n + 1 < len(pairs):
            nxt = build_phase(pairs[n + 1], phases[(n + 1) % 2])
        if n >= built:
            stages.pop(0)()
        far_sums(pair, phases[n % 2], tz)
        tz = nxt
        if n < built:
            for o in range(n * nd // built, (n + 1) * nd // built):
                build_phi(o)
    for stage in stages:
        stage()

    for i, j in others:
        msg_copy(i, j).wait_send()

    def far_arrive(i, j):
        r, c = place(i, j)
        p = r * n_col + c
        remote(far_send.at[0], far_recv.at[p], far_ss.at[0], far_rs.at[p], r, c).wait_recv()

    for i, j in others:
        far_arrive(i, j)
    for i, j in others:
        far_copy(i, j).wait_send()
    far = far_recv[0]
    for p in range(1, nd):
        far = far + far_recv[p]
    for a in range(3):
        out_ref[a] = near[a] + far[2 * a : 2 * a + 2, :]


def shared_device(noise_field, offsets, tile_list, send_cells, bead_slot, spectral):
    n_row = lax.axis_size("row")
    n_col = lax.axis_size("col")
    nd = n_row * n_col
    xs, ys, glen = spectral.shape[3:]
    slots = tile_list.shape[3]
    cap = send_cells.shape[2]
    xy = xs * ys
    cr = cap * nd // LANES
    msg_rows = -(-(12 + 2 * cr) // 16) * 16
    chunks = 4 if xy % 256 == 0 else 1
    dims = (n_row, n_col, slots, xs, ys, glen, cap)
    vmem = pl.BlockSpec(memory_space=pltpu.VMEM)
    hbm = pl.BlockSpec(memory_space=pl.ANY)
    dma = pltpu.SemaphoreType.DMA
    rows_t = 6 * nd
    spectrum = lattice_spectrum()
    return pl.pallas_call(
        functools.partial(shared_kernel, dims),
        out_shape=pltpu.VMEM(noise_field.shape, f32),
        in_specs=[hbm] * 7,
        out_specs=vmem,
        scratch_shapes=[
            pltpu.SMEM((2, slots), jnp.int32),
            pltpu.VMEM(noise_field.shape, f32),
            pltpu.VMEM(offsets.shape, jnp.int32),
            pltpu.VMEM((1, TB), jnp.int32),
            pltpu.VMEM((cap, nd), jnp.int32),
            pltpu.VMEM((12, xy, glen), f32),
            pltpu.VMEM((6 * (xy // chunks), 2 * glen), bf16),
            pltpu.VMEM((6 * glen, 2 * xy), bf16),
            pltpu.VMEM((2 * xy, 2 * TB), bf16),
            pltpu.VMEM((2 * xy, 2 * TB), bf16),
            pltpu.VMEM((MODES, nd * TB), bf16),
            pltpu.VMEM((nd * TB, MODES), bf16),
            pltpu.VMEM((rows_t + nd, nd * TB), bf16),
            pltpu.VMEM((3, nd, 16, TB), f32),
            pltpu.VMEM((3, nd, 16, TB), f32),
            pltpu.VMEM((rows_t + nd, 2 * LANES), bf16),
            pltpu.VMEM((2 * LANES, MODES), bf16),
            pltpu.VMEM((rows_t + 6 * nd, MODES), bf16),
            pltpu.VMEM((msg_rows, LANES), f32),
            pltpu.VMEM((msg_rows, LANES), bf16),
            pltpu.VMEM((nd, msg_rows, LANES), bf16),
            pltpu.VMEM((4, LANES, LANES), f32),
            pltpu.VMEM((3, nd * TB), f32),
            pltpu.VMEM(spectrum.shape, f32),
            pltpu.VMEM((rows_t, TB), f32),
            pltpu.VMEM((nd, 8, TB), f32),
            pltpu.VMEM((nd, 8, TB), f32),
            dma((5,)), dma((chunks,)), dma,
            dma((nd,)), dma((nd,)),
            dma((nd,)), dma((nd,)),
        ],
        compiler_params=pltpu.CompilerParams(
            collective_id=1, has_side_effects=True, vmem_limit_bytes=56 * 1024 * 1024
        ),
    )(
        tile_list.reshape(2, slots),
        noise_field,
        offsets,
        bead_slot.reshape(1, TB),
        send_cells.reshape(cap, nd),
        jnp.asarray(spectrum),
        spectral.reshape(12, xy, glen),
    )


def power_of_two(n):
    return n & (n - 1) == 0


def per_device(noise_field, offsets, tile_list, send_cells, bead_slot, spectral):
    n_row = lax.axis_size("row")
    n_col = lax.axis_size("col")
    nd = n_row * n_col
    xs, ys, glen = spectral.shape[3:]
    cap = send_cells.shape[2]
    fits = (
        8 <= nd <= 16
        and power_of_two(n_row)
        and power_of_two(n_col)
        and power_of_two(glen)
        and nd * tile_list.shape[3] <= LANES
        and cap % (LANES // nd) == 0
        and cap * nd <= 256
        and glen * (glen // n_row) * (glen // n_col) <= 1 << 17
        and ys % 16 == 0
    )
    run = shared_device if fits else spread_device
    return run(noise_field, offsets, tile_list, send_cells, bead_slot, spectral)


def solution(mesh):
    return jax.shard_map(
        per_device,
        mesh=mesh,
        in_specs=(
            P(None, None, ("groups", "row", "col")),
            P(None, ("groups", "row", "col")),
            P(("groups", "row"), "col", None, None),
            P(("groups", "row"), "col", None, None),
            P(("groups", "row", "col")),
            P(None, None, None, ("groups", "row"), "col", None),
        ),
        out_specs=P(None, None, ("groups", "row", "col")),
        check_vma=False,
    )
```

```python
import functools
import math

import jax
import jax.numpy as jnp
import ml_dtypes
import numpy as np
from jax import lax
from jax.experimental import pallas as pl
from jax.experimental.pallas import tpu as pltpu
from jax.sharding import PartitionSpec as P

TB = 128
LANES = 128
PERIOD = 8
DEGREES = 4

cheb_coef = (1.0, 0.45, -0.2, 0.12, -0.08)
kernel_range = 1.5

f32 = jnp.float32
bf16 = jnp.bfloat16


def iota(shape, dim):
    return lax.broadcasted_iota(jnp.int32, shape, dim)


def over(n, d):
    return lax.shift_right_logical(n, jnp.full(n.shape, d.bit_length() - 1, jnp.int32))


def dot(a, b):
    return jnp.dot(a, b, preferred_element_type=f32)


def dot_nt(a, b):
    return lax.dot_general(a, b, (((1,), (1,)), ((), ())), preferred_element_type=f32)


def cos_turn(turns):
    x = jnp.abs(turns - jnp.floor(turns) - 0.5) * 4.0 - 1.0
    x2 = x * x
    p = 0.00015148419
    for c in (-0.00467376557, 0.07968967928, -0.64596371106, 1.57079631847):
        p = p * x2 + c
    return p * x


def kernel(
    dims,
    tiles_ref, noise_ref, off_ref, slot_ref, cells_ref, spec_hbm,
    out_ref,
    spec, pre, hat, phase, ang, wang, tabf, tab, kmat,
    a_send, a_recv, b_send, row_b, col_b,
    e_send, e_recv, y_send, y_recv, far_send, far_recv,
    cur, prev, acc, scale,
    spec_sem, a_ss, a_rs, b_ss, b_rs, e_ss, e_rs, y_ss, y_rs, far_ss, far_rs,
):
    n_row, n_col, slots, xs, ys, glen, cap = dims
    nd = n_row * n_col
    xy = xs * ys
    cr = cap * nd // LANES
    kq = tab.shape[0]
    beads = n_col * TB
    me_r = lax.axis_index("row")
    me_c = lax.axis_index("col")
    me = me_r * n_col + me_c
    chunks = spec_sem.shape[0]
    part = xy // chunks
    per_row = LANES // nd

    def spec_copy(i):
        rows = pl.ds(i * part, part)
        return pltpu.make_async_copy(
            spec_hbm.at[:, rows, :], spec.at[:, rows, :], spec_sem.at[i]
        )

    for i in range(chunks):
        spec_copy(i).start()

    straight = nd <= 32
    if straight:
        rows_of = [me_r] + [lax.rem(me_r + d, n_row) for d in range(1, n_row)]
        cols_of = [me_c] + [lax.rem(me_c + d, n_col) for d in range(1, n_col)]
        order = sorted(
            [(i, j) for i in range(n_row) for j in range(n_col) if i + j],
            key=lambda t: (abs(t[1] - n_col // 2), abs(t[0] - n_row // 2)),
        )

    def each(body):
        if straight:
            for i, j in order:
                body(rows_of[i], cols_of[j])
            return

        def turn(d, carry):
            body(lax.rem(me_r + d // n_col, n_row), lax.rem(me_c + lax.rem(d, n_col), n_col))
            return carry

        lax.fori_loop(1, nd, turn, 0)

    def each_row(body):
        if straight:
            for d in range(1, n_row):
                body(rows_of[d])
        else:
            lax.fori_loop(1, n_row, lambda d, t: (body(lax.rem(me_r + d, n_row)), t)[1], 0)

    def each_col(body):
        if straight:
            for d in range(1, n_col):
                body(cols_of[d])
        else:
            lax.fori_loop(1, n_col, lambda d, t: (body(lax.rem(me_c + d, n_col)), t)[1], 0)

    barrier = pltpu.get_barrier_semaphore()

    def greet(r, c):
        pl.semaphore_signal(
            barrier, inc=1, device_id={"row": r, "col": c},
            device_id_type=pl.DeviceIdType.MESH,
        )

    each(greet)

    def remote(src, dst, ss, rs, r, c):
        return pltpu.make_async_remote_copy(
            src_ref=src, dst_ref=dst, send_sem=ss, recv_sem=rs,
            device_id={"row": r, "col": c}, device_id_type=pl.DeviceIdType.MESH,
        )

    def packed_cells():
        flat = cells_ref[...].astype(f32)
        if per_row == 1:
            return flat
        spread = (iota((nd, LANES), 1) & (nd - 1)) == iota((nd, LANES), 0)
        wide = jnp.dot(
            flat, spread.astype(f32), precision=lax.Precision.HIGHEST,
            preferred_element_type=f32,
        )
        mine = over(iota((cap, LANES), 1), nd) == (iota((cap, LANES), 0) & (per_row - 1))
        return jnp.sum(jnp.where(mine, wide, 0.0).reshape(cr, per_row, LANES), axis=1)

    a_send[0:1, :] = slot_ref[...].astype(f32)
    cells = packed_cells()
    a_send[1 : 1 + cr, :] = cells
    a_recv[me, 0:1, :] = slot_ref[...].astype(f32)
    a_recv[me, 1 : 1 + cr, :] = cells
    own_noise = jnp.concatenate([noise_ref[0], noise_ref[1], noise_ref[2]], axis=1)
    off = off_ref[...].astype(f32)
    own_off = jnp.concatenate([off[0:1], off[1:2], off[2:3]], axis=1)
    b_send[0:2, :] = own_noise
    b_send[2:3, :] = own_off
    row_b[me_c, 0:2, :] = own_noise
    row_b[me_c, 2:3, :] = own_off
    col_b[me_r, 0:2, :] = own_noise
    col_b[me_r, 2:3, :] = own_off
    tabf[...] = jnp.zeros_like(tabf)

    pl.semaphore_wait(barrier, nd - 1)

    def b_row_copy(c):
        return remote(b_send, row_b.at[me_c], b_ss.at[c], b_rs.at[me_c], me_r, c)

    def b_col_copy(r):
        return remote(
            b_send, col_b.at[me_r], b_ss.at[n_col + r], b_rs.at[n_col + me_r], r, me_c
        )

    each_col(lambda c: b_row_copy(c).start())
    each_row(lambda r: b_col_copy(r).start())

    def a_copy(r, c):
        p = r * n_col + c
        return remote(a_send, a_recv.at[me], a_ss.at[p], a_rs.at[me], r, c)

    each(lambda r, c: a_copy(r, c).start())

    gi = iota((2 * glen, 2 * glen), 0)
    gj = iota((2 * glen, 2 * glen), 1)
    zi, zj = gi & (glen - 1), gj & (glen - 1)
    in_im, out_im = gi >= glen, gj >= glen
    half = glen // 2
    same = zi == zj
    mirror = (zi + zj == glen) & (zi != zj)
    even = zj <= half
    plain = in_im == out_im
    fold = jnp.where(
        even,
        jnp.where(plain & (same | mirror), 1.0, 0.0),
        jnp.where(
            plain,
            0.0,
            jnp.where(same, 1.0, 0.0) - jnp.where(mirror, 1.0, 0.0),
        )
        * jnp.where(out_im, -1.0, 1.0),
    ).astype(bf16)

    width_sq = (glen / 8.0) ** 2
    front = math.sqrt(1.5) / (2.0 * math.pi * width_sq) ** 0.75
    def signed(n):
        return jnp.where(n < half, n, n - glen).astype(f32)

    ky = signed(me_c * ys + iota((ys, glen), 0))
    kz = signed(iota((ys, glen), 1))
    kyz_sq = ky * ky + kz * kz

    def hat_block(i, first):
        kx = signed(me_r * xs + i)
        q = kx * kx + kyz_sq
        amp = jnp.where(q > 0, front * jnp.exp(q * (-0.25 / width_sq)), 0.0)
        damp = amp / jnp.maximum(q, 1.0)
        rows = pl.ds(pl.multiple_of(i * ys, ys), ys)
        at = pl.multiple_of((i - first) * ys, ys)
        waves = (kx, ky, kz)
        for v in range(2):
            for p in range(2):
                s = [spec[(p * 3 + a) * 2 + v, rows, :] for a in range(3)]
                along = (kx * s[0] + ky * s[1] + kz * s[2]) * damp
                for a in range(3):
                    pre[pl.ds((a * 2 + v) * part + at, ys), p * glen : (p + 1) * glen] = (
                        amp * s[a] - waves[a] * along
                    ).astype(bf16)
        return first

    per = part // ys
    for i in range(chunks):
        spec_copy(i).wait()
        lax.fori_loop(i * per, (i + 1) * per, hat_block, i * per)
        folded = dot(pre[...], fold)
        for k in range(6):
            for p in range(2):
                hat[
                    p * xy + i * part : p * xy + (i + 1) * part, k * glen : (k + 1) * glen
                ] = folded[
                    k * part : (k + 1) * part, p * glen : (p + 1) * glen
                ].astype(bf16)

    def b_col_arrive(r):
        remote(b_send, col_b.at[r], b_ss.at[n_col + r], b_rs.at[n_col + r], r, me_c).wait_recv()

    def b_row_arrive(c):
        remote(b_send, row_b.at[c], b_ss.at[c], b_rs.at[c], me_r, c).wait_recv()

    each_row(b_col_arrive)
    each_col(b_row_arrive)

    eye = (iota((TB, TB), 0) == iota((TB, TB), 1)).astype(f32)
    ones = jnp.ones((TB, TB), bf16)
    scale_sq = kernel_range * kernel_range

    def pick(values, into, s):
        tr = tiles_ref[0, s]
        return tuple(
            into[i] + values * jnp.where(tr == i, 1.0, 0.0).astype(f32) for i in range(n_col)
        )

    def build(s, energies):
        tr = jnp.maximum(tiles_ref[0, s], 0)
        tc = jnp.maximum(tiles_ref[1, s], 0)
        row_off = row_b[tr][2:3, :]
        col_off = col_b[tc][2:3, :]
        disp = []
        for a in range(3):
            lanes = slice(a * TB, (a + 1) * TB)
            rp = dot((eye * row_off[:, lanes]).astype(bf16), ones)
            gap = (rp - col_off[:, lanes]).astype(jnp.int32) + PERIOD // 2
            disp.append(((gap & (PERIOD - 1)) - PERIOD // 2).astype(f32))
        squares = disp[0] * disp[0] + disp[1] * disp[1] + disp[2] * disp[2]
        envelope = jnp.exp(squares * (-0.5 / scale_sq)) / scale_sq
        third = squares / 3.0
        for a in range(3):
            for b in range(a, 3):
                element = disp[a] * disp[b]
                if a == b:
                    element = element - third
                entry = (envelope * element).astype(bf16)
                kmat[s, a * TB : (a + 1) * TB, b * TB : (b + 1) * TB] = entry
                if a != b:
                    kmat[s, b * TB : (b + 1) * TB, a * TB : (a + 1) * TB] = entry
        wide = kmat[s].astype(f32)
        sq = wide * wide
        high = sq.astype(bf16)
        low = (sq - high.astype(f32)).astype(bf16)
        one_row = jnp.ones((8, 3 * TB), bf16)
        energy = dot_nt(one_row, high) + dot_nt(one_row, low)
        return pick(energy[0:1], energies, s)

    energies = lax.fori_loop(
        0, slots, build, tuple(jnp.zeros((1, 3 * TB), f32) for _ in range(n_col)),
        unroll=slots <= 4,
    )
    for i in range(n_col):
        e_send[i : i + 1, :] = energies[i]
        e_recv[me, i : i + 1, :] = energies[i]

    def e_copy(r, c):
        p = r * n_col + c
        return remote(e_send, e_recv.at[me], e_ss.at[p], e_rs.at[me], r, c)

    for r in range(n_row):
        cur[r] = col_b[r, 0:2, :]
    acc[...] = cheb_coef[0] * own_noise

    def a_arrive(r, c):
        p = r * n_col + c
        remote(a_send, a_recv.at[p], a_ss.at[p], a_rs.at[p], r, c).wait_recv()

    def prepare_table():
        each(a_arrive)

        def spread(h, carry):
            tabf[pl.ds(h * cr, cr), :] = a_recv[h, 1 : 1 + cr, :]
            return carry

        lax.fori_loop(0, nd, spread, 0)
        cell = tabf[...].astype(jnp.int32)
        y_slab, z_slab = glen // n_row, glen // n_col
        holder = over(iota((kq, LANES), 0), cr)
        pos_x = over(cell, y_slab * z_slab)
        pos_y = over(holder, n_col) * y_slab + (over(cell, z_slab) & (y_slab - 1))
        pos_z = (holder & (n_col - 1)) * z_slab + (cell & (z_slab - 1))
        for at, pos in enumerate((pos_x, pos_y, pos_z)):
            tab[:, at * LANES : (at + 1) * LANES] = pos.astype(f32).astype(bf16)

    x_step = LANES // ys
    lane = iota((LANES, LANES), 1)
    scaled = 1.0 / glen
    along_x = ((me_r * xs + over(lane, ys)).astype(f32) * scaled).astype(bf16)
    along_y = ((me_c * ys + (lane & (ys - 1))).astype(f32) * scaled).astype(bf16)
    wang[...] = jnp.zeros_like(wang)
    wang[0:LANES, 0:LANES] = along_x
    wang[LANES : 2 * LANES, 0:LANES] = along_y
    wang[0:LANES, LANES : 2 * LANES] = jnp.full((LANES, LANES), x_step * scaled, bf16)
    wang[2 * LANES :, 2 * LANES :] = (lane.astype(f32) * scaled).astype(bf16)
    rep = over(iota((8, 6 * glen), 1), glen) == iota((8, 6 * glen), 0)
    rep = rep.astype(f32).astype(bf16)
    wide_ones = jnp.ones((TB, kq), bf16)
    step_rows = 32

    def far_copy(i, c):
        return remote(
            far_send.at[i * n_col + c], far_recv.at[me],
            far_ss.at[i * n_col + c], far_rs.at[me], i, c,
        )

    def far_chunk(i, carry):
        spots = jnp.concatenate(
            [eye * a_recv[i * n_col + c, 0:1, :] for c in range(n_col)], axis=0
        ).astype(bf16)
        code = dot(spots, wide_ones).astype(jnp.int32)
        s_idx = over(code, nd)
        row_idx = (code & (nd - 1)) * cr + over(s_idx, per_row)
        hot = (row_idx == iota((beads, kq), 1)).astype(f32).astype(bf16)
        found = dot(hot, tab[...])
        owner_of = i * n_col + over(iota((beads, LANES), 0), TB)
        want = (s_idx[:, :LANES] & (per_row - 1)) * nd + owner_of
        keep = want == iota((beads, LANES), 1)
        places = jnp.concatenate(
            [jnp.where(keep, found[:, k * LANES : (k + 1) * LANES], 0.0) for k in range(3)],
            axis=1,
        ).astype(bf16)
        ang[...] = dot(places, wang[...])

        def phase_block(j, carry):
            rows = pl.ds(pl.multiple_of(j * step_rows, step_rows), step_rows)
            at_lane = iota((step_rows, LANES), 1)
            start = ang[rows, 0:LANES]
            co = cos_turn(start)
            ns = cos_turn(start + 0.25)
            turn_x = cos_turn(
                ang[rows, LANES : 2 * LANES] - jnp.where(at_lane == 1, 0.25, 0.0)
            )
            cd = jnp.broadcast_to(turn_x[:, 0:1], co.shape)
            sd = jnp.broadcast_to(turn_x[:, 1:2], co.shape)
            ang[rows, 2 * LANES :] = cos_turn(
                ang[rows, 2 * LANES :] + jnp.where(at_lane > half, 0.25, 0.0)
            )
            for g in range(xy // LANES):
                phase[rows, g * LANES : (g + 1) * LANES] = co.astype(bf16)
                phase[rows, xy + g * LANES : xy + (g + 1) * LANES] = ns.astype(bf16)
                co, ns = co * cd + ns * sd, ns * cd - co * sd
            return carry

        lax.fori_loop(0, beads // step_rows, phase_block, 0)
        sums = dot(phase[...], hat[...])
        tz = ang[:, 2 * LANES :]
        weighted = jnp.concatenate(
            [(sums[:, k * glen : (k + 1) * glen] * tz).astype(bf16) for k in range(6)], axis=1
        )
        res = dot_nt(rep, weighted)
        for c in range(n_col):
            owner = i * n_col + c
            far_send[owner] = res[:, c * TB : (c + 1) * TB]

            @pl.when(owner == me)
            def _():
                far_recv[me] = res[:, c * TB : (c + 1) * TB]

            @pl.when(owner != me)
            def _():
                far_copy(i, c).start()

        return carry

    def y_copy(r, c, par):
        p = r * n_col + c
        return remote(
            y_send.at[par, c], y_recv.at[par, me], y_ss.at[par, p], y_rs.at[par, me], r, c
        )

    def y_arrive(r, c, par):
        p = r * n_col + c
        remote(
            y_send.at[par, 0], y_recv.at[par, p], y_ss.at[par, p], y_rs.at[par, p], r, c
        ).wait_recv()

    each(lambda r, c: e_copy(r, c).start())

    def degree_step(m, carry):
        par = lax.rem(m, 2)

        def apply(s, sums):
            tc = jnp.maximum(tiles_ref[1, s], 0)
            w = cur[tc]
            w = jnp.concatenate([w, jnp.zeros((6, 3 * TB), f32)], axis=0).astype(bf16)
            return pick(dot_nt(w, kmat[s])[0:2], sums, s)

        sums = lax.fori_loop(
            0, slots, apply, tuple(jnp.zeros((2, 3 * TB), f32) for _ in range(n_col)),
            unroll=slots <= 4,
        )
        own = jnp.zeros((2, 3 * TB), f32)
        for i in range(n_col):
            y_send[par, i] = sums[i]
            own = own + sums[i] * jnp.where(me_c == i, 1.0, 0.0).astype(f32)
        y_recv[par, me] = own
        each(lambda r, c: y_copy(r, c, par).start())

        @pl.when(m == 0)
        def _():
            prepare_table()

        lax.fori_loop(m * n_row // DEGREES, (m + 1) * n_row // DEGREES, far_chunk, 0)

        @pl.when(m == 0)
        def _():
            def e_arrive(r, c):
                p = r * n_col + c
                remote(e_send, e_recv.at[p], e_ss.at[p], e_rs.at[p], r, c).wait_recv()

            each(e_arrive)
            top = jnp.zeros((n_col, 3 * TB), f32)
            for r in range(n_row):
                total = e_recv[r * n_col]
                for c in range(1, n_col):
                    total = total + e_recv[r * n_col + c]
                top = jnp.maximum(top, total)
            largest = jnp.max(jnp.max(top, axis=1, keepdims=True), axis=0, keepdims=True)
            scale[...] = jnp.broadcast_to(1.0 / jnp.sqrt(largest + 1e-06), scale.shape)

        each(lambda r, c: y_arrive(r, c, par))
        each(lambda r, c: y_copy(r, c, par).wait_send())
        first = jnp.where(m == 0, 1.0, 0.0).astype(f32)
        coef = jnp.where(
            m == 0, cheb_coef[1],
            jnp.where(m == 1, cheb_coef[2], jnp.where(m == 2, cheb_coef[3], cheb_coef[4])),
        ).astype(f32)
        sc = jnp.concatenate([scale[0:2, :]] * 3, axis=1)

        def advance(r, carry):
            total = y_recv[par, r * n_col]
            for c in range(1, n_col):
                total = total + y_recv[par, r * n_col + c]
            now = sc * total
            following = jnp.where(m == 0, now, 2.0 * now - prev[r])
            prev[r] = cur[r]
            cur[r] = following
            return carry

        lax.fori_loop(0, n_row, advance, 0)
        acc[...] = acc[...] + coef * cur[me_r]
        return carry

    prev[...] = jnp.zeros_like(prev)
    lax.fori_loop(0, DEGREES, degree_step, 0)

    each_row(lambda r: b_col_copy(r).wait_send())
    each_col(lambda c: b_row_copy(c).wait_send())
    each(lambda r, c: a_copy(r, c).wait_send())
    each(lambda r, c: e_copy(r, c).wait_send())

    def far_arrive(r, c):
        p = r * n_col + c
        remote(
            far_send.at[p], far_recv.at[p], far_ss.at[p], far_rs.at[p], r, c
        ).wait_recv()

    each(far_arrive)
    each(lambda r, c: far_copy(r, c).wait_send())
    far = lax.fori_loop(
        1, nd, lambda p, t: t + far_recv[p], far_recv[0]
    )
    near = acc[...]
    for a in range(3):
        out_ref[a] = near[:, a * TB : (a + 1) * TB] + far[2 * a : 2 * a + 2, :]


def spread_device(noise_field, offsets, tile_list, send_cells, bead_slot, spectral):
    n_row = lax.axis_size("row")
    n_col = lax.axis_size("col")
    nd = n_row * n_col
    xs, ys, glen = spectral.shape[3:]
    slots = tile_list.shape[3]
    cap = send_cells.shape[2]
    cr = cap * nd // LANES
    xy = xs * ys
    kq = max(LANES, nd * cr)
    beads = n_col * TB
    a_rows = -(-(1 + cr) // 4) * 4
    chunks = 4 if xy % 256 == 0 else 1
    dims = (n_row, n_col, slots, xs, ys, glen, cap)
    vmem = pl.BlockSpec(memory_space=pltpu.VMEM)
    dma = pltpu.SemaphoreType.DMA
    wide = 3 * TB
    return pl.pallas_call(
        functools.partial(kernel, dims),
        out_shape=jax.ShapeDtypeStruct(noise_field.shape, f32),
        in_specs=[pl.BlockSpec(memory_space=pltpu.SMEM), vmem, vmem, vmem, vmem,
                  pl.BlockSpec(memory_space=pl.ANY)],
        out_specs=vmem,
        scratch_shapes=[
            pltpu.VMEM((12, xy, glen), f32),
            pltpu.VMEM((6 * (xy // chunks), 2 * glen), bf16),
            pltpu.VMEM((2 * xy, 6 * glen), bf16),
            pltpu.VMEM((beads, 2 * xy), bf16),
            pltpu.VMEM((beads, 3 * LANES), f32),
            pltpu.VMEM((3 * LANES, 3 * LANES), bf16),
            pltpu.VMEM((kq, LANES), f32),
            pltpu.VMEM((kq, 3 * LANES), bf16),
            pltpu.VMEM((slots, wide, wide), bf16),
            pltpu.VMEM((a_rows, LANES), f32),
            pltpu.VMEM((nd, a_rows, LANES), f32),
            pltpu.VMEM((4, wide), f32),
            pltpu.VMEM((n_col, 4, wide), f32),
            pltpu.VMEM((n_row, 4, wide), f32),
            pltpu.VMEM((n_col, wide), f32),
            pltpu.VMEM((nd, n_col, wide), f32),
            pltpu.VMEM((2, n_col, 2, wide), f32),
            pltpu.VMEM((2, nd, 2, wide), f32),
            pltpu.VMEM((nd, 8, TB), f32),
            pltpu.VMEM((nd, 8, TB), f32),
            pltpu.VMEM((n_row, 2, wide), f32),
            pltpu.VMEM((n_row, 2, wide), f32),
            pltpu.VMEM((2, wide), f32),
            pltpu.VMEM((8, LANES), f32),
            dma((chunks,)),
            dma((nd,)), dma((nd,)),
            dma((n_row + n_col,)), dma((n_row + n_col,)),
            dma((nd,)), dma((nd,)),
            dma((2, nd)), dma((2, nd)),
            dma((nd,)), dma((nd,)),
        ],
        compiler_params=pltpu.CompilerParams(
            collective_id=0, has_side_effects=True, vmem_limit_bytes=56 * 1024 * 1024
        ),
    )(
        tile_list.reshape(2, slots),
        noise_field,
        offsets,
        bead_slot.reshape(1, TB),
        send_cells.reshape(cap, nd),
        spectral.reshape(12, xy, glen),
    )


PLANES = PERIOD // 2 + 1
FLAT = PERIOD * PERIOD
MODES = PLANES * 2 * FLAT
PAIRS = ((0, 0), (1, 1), (2, 2), (0, 1), (0, 2), (1, 2))


def lattice_spectrum():
    code = np.arange(PERIOD**3)
    site = np.stack([code // FLAT, code // PERIOD % PERIOD, code % PERIOD])
    disp = (site + PERIOD // 2) % PERIOD - PERIOD // 2
    d = disp.astype(np.float32)
    squares = d[0] * d[0] + d[1] * d[1] + d[2] * d[2]
    scale_sq = np.float32(kernel_range * kernel_range)
    envelope = np.exp(squares * np.float32(-0.5 / scale_sq)) / scale_sq
    table = np.zeros((3, 3, PERIOD**3))
    for a, b in PAIRS:
        element = d[a] * d[b]
        if a == b:
            element = element - squares / np.float32(3.0)
        table[a, b] = (envelope * element).astype(ml_dtypes.bfloat16).astype(np.float64)
        table[b, a] = table[a, b]
    energy = (table * table).sum(axis=1)
    qz = np.arange(PLANES)[:, None, None, None]
    part = np.arange(2)[None, :, None, None]
    qx = np.arange(PERIOD)[None, None, :, None]
    qy = np.arange(PERIOD)[None, None, None, :]
    qx, qy, qz, part = (t.reshape(-1) for t in np.broadcast_arrays(qx, qy, qz, part))
    angle = 2.0 * np.pi / PERIOD * ((np.stack([qx, qy, qz], 1) @ site) % PERIOD)
    weight = np.where((qz == 0) | (qz == PERIOD // 2), 1.0, 2.0) / PERIOD**3
    turn = np.where(part == 0, 1.0, -1.0)
    rows = [weight * (np.cos(angle) @ table[p]) for p in PAIRS]
    rows += [-turn * weight * (np.sin(angle) @ table[p]) for p in PAIRS[3:]]
    rows += [weight * (np.cos(angle) @ energy[a]) for a in range(3)]
    rows += [np.zeros(MODES)] * (-len(rows) % 8)
    return np.stack(rows).astype(np.float32)


def shared_kernel(
    dims,
    tiles_hbm, noise_hbm, off_hbm, slot_hbm, cells_hbm, spectrum_hbm, spec_hbm,
    out_ref,
    tiles_ref, noise_ref, off_ref, slot_ref, cells_ref,
    spec, pre, hat, phase_a, phase_b, phi, modes, wide, cheb_a, cheb_b, mixer, mixed, lattice,
    msg_f, msg, inbox, table, offs, spectrum, last,
    far_send, far_recv,
    load_sem, spec_sem, spectrum_sem, m_ss, m_rs, far_ss, far_rs,
):
    n_row, n_col, slots, xs, ys, glen, cap = dims
    nd = n_row * n_col
    xy = xs * ys
    per_row = LANES // nd
    cr = cap // per_row
    cells_at = 10
    tile_at = cells_at + 2 * cr
    beads = nd * TB
    me_r = lax.axis_index("row")
    me_c = lax.axis_index("col")
    me = me_r * n_col + me_c
    chunks = spec_sem.shape[0]
    part = xy // chunks
    nb = 2 * nd
    rows_t = 3 * nb
    rows_e = rows_t + nd

    def spec_copy(i):
        rows = pl.ds(i * part, part)
        return pltpu.make_async_copy(
            spec_hbm.at[:, rows, :], spec.at[:, rows, :], spec_sem.at[i]
        )

    loads = [
        pltpu.make_async_copy(src, dst, load_sem.at[k])
        for k, (src, dst) in enumerate((
            (cells_hbm, cells_ref), (tiles_hbm, tiles_ref), (noise_hbm, noise_ref),
            (off_hbm, off_ref), (slot_hbm, slot_ref),
        ))
    ]

    peers = sorted(
        [(i, j) for i in range(n_row) for j in range(n_col)], key=lambda t: (-t[1], -t[0])
    )
    others = peers[:-1]

    def place(i, j):
        return jnp.bitwise_xor(me_r, i), jnp.bitwise_xor(me_c, j)

    barrier = pltpu.get_barrier_semaphore()
    for i, j in others:
        r, c = place(i, j)
        pl.semaphore_signal(
            barrier, inc=1, device_id={"row": r, "col": c},
            device_id_type=pl.DeviceIdType.MESH,
        )
    for load in loads:
        load.start()
    for i in range(chunks):
        spec_copy(i).start()
    spectrum_copy = pltpu.make_async_copy(spectrum_hbm, spectrum, spectrum_sem)
    spectrum_copy.start()

    def remote(src, dst, ss, rs, r, c):
        return pltpu.make_async_remote_copy(
            src_ref=src, dst_ref=dst, send_sem=ss, recv_sem=rs,
            device_id={"row": r, "col": c}, device_id_type=pl.DeviceIdType.MESH,
        )

    for load in loads:
        load.wait()
    for a in range(3):
        msg_f[2 * a : 2 * a + 2, :] = noise_ref[a]
    msg_f[6:9, :] = off_ref[...].astype(f32)
    msg_f[9:10, :] = slot_ref[...].astype(f32)
    spread = over(iota((nd, LANES), 1), per_row) == iota((nd, LANES), 0)
    spread = spread.astype(f32).astype(bf16)
    keep = (iota((cap, LANES), 1) & (per_row - 1)) == (iota((cap, LANES), 0) & (per_row - 1))
    cells = cells_ref[...]
    for h, half_cell in enumerate((over(cells, 512), (cells & 511) - 256)):
        out = dot(half_cell.astype(f32).astype(bf16), spread)
        out = jnp.sum(jnp.where(keep, out, 0.0).reshape(cr, per_row, LANES), axis=1)
        msg_f[cells_at + h * cr : cells_at + (h + 1) * cr, :] = out
    lane_row = iota((1, LANES), 1)
    row_list = jnp.zeros((1, LANES), jnp.int32)
    col_list = jnp.zeros((1, LANES), jnp.int32)
    for s in range(slots):
        here = lane_row == me * slots + s
        tr, tc = tiles_ref[0, s], tiles_ref[1, s]
        row_list = jnp.where(
            here & (jnp.full((1, LANES), tr) >= 0), me_r * n_col + tr + 1, row_list
        )
        col_list = jnp.where(here, tc * n_col + me_c + 1, col_list)
    msg_f[tile_at : tile_at + 1, :] = row_list.astype(f32)
    msg_f[tile_at + 1 : tile_at + 2, :] = col_list.astype(f32)
    if tile_at + 2 < msg_f.shape[0]:
        msg_f[tile_at + 2 :, :] = jnp.zeros((msg_f.shape[0] - tile_at - 2, LANES), f32)
    msg[...] = msg_f[...].astype(bf16)
    inbox[me] = msg_f[...].astype(bf16)

    pl.semaphore_wait(barrier, nd - 1)

    def msg_copy(i, j):
        r, c = place(i, j)
        p = i * n_col + j
        return remote(msg, inbox.at[me], m_ss.at[p], m_rs.at[me], r, c)

    def msg_arrive(i, j):
        r, c = place(i, j)
        p = r * n_col + c
        remote(msg, inbox.at[p], m_ss.at[0], m_rs.at[p], r, c).wait_recv()

    for i, j in others:
        msg_copy(i, j).start()

    wide[...] = jnp.zeros_like(wide)
    mixed[...] = jnp.zeros_like(mixed)
    cheb_a[...] = jnp.zeros_like(cheb_a)
    for o in range(nd):
        ones = (iota((nd, TB), 0) == o).astype(f32)
        wide[rows_t:rows_e, o * TB : (o + 1) * TB] = ones.astype(bf16)

    gj = iota((2 * glen, 2 * glen), 0)
    gi = iota((2 * glen, 2 * glen), 1)
    zi, zj = gi & (glen - 1), gj & (glen - 1)
    in_im, out_im = gi >= glen, gj >= glen
    half = glen // 2
    same = zi == zj
    mirror = (zi + zj == glen) & (zi != zj)
    even = zj <= half
    plain = in_im == out_im
    fold = jnp.where(
        even,
        jnp.where(plain & (same | mirror), 1.0, 0.0),
        jnp.where(
            plain,
            0.0,
            jnp.where(same, 1.0, 0.0) - jnp.where(mirror, 1.0, 0.0),
        )
        * jnp.where(out_im, -1.0, 1.0),
    ).astype(bf16)

    width_sq = (glen / 8.0) ** 2
    front = math.sqrt(1.5) / (2.0 * math.pi * width_sq) ** 0.75

    def signed(n):
        return jnp.where(n < half, n, n - glen).astype(f32)

    ky = signed(me_c * ys + iota((ys, glen), 0))
    kz = signed(iota((ys, glen), 1))
    kyz_sq = ky * ky + kz * kz

    def hat_block(i, first):
        kx = signed(me_r * xs + i)
        q = kx * kx + kyz_sq
        amp = jnp.where(q > 0, front * jnp.exp(q * (-0.25 / width_sq)), 0.0)
        damp = amp / jnp.maximum(q, 1.0)
        rows = pl.ds(pl.multiple_of(i * ys, ys), ys)
        at = pl.multiple_of((i - first) * ys, ys)
        waves = (kx, ky, kz)
        for v in range(2):
            for p in range(2):
                s = [spec[(p * 3 + a) * 2 + v, rows, :] for a in range(3)]
                along = (kx * s[0] + ky * s[1] + kz * s[2]) * damp
                for a in range(3):
                    pre[pl.ds((a * 2 + v) * part + at, ys), p * glen : (p + 1) * glen] = (
                        amp * s[a] - waves[a] * along
                    ).astype(bf16)
        return first

    per = part // ys
    for i in range(chunks):
        spec_copy(i).wait()
        lax.fori_loop(i * per, (i + 1) * per, hat_block, i * per)
        for k in range(6):
            folded = dot_nt(fold, pre[k * part : (k + 1) * part, :]).astype(bf16)
            for p in range(2):
                hat[
                    k * glen : (k + 1) * glen, p * xy + i * part : p * xy + (i + 1) * part
                ] = folded[p * glen : (p + 1) * glen, :]

    spectrum_copy.wait()
    for i, j in others[::-1]:
        msg_arrive(i, j)

    row_list = jnp.zeros((1, LANES), f32)
    col_list = jnp.zeros((1, LANES), f32)
    slot_rows = nb // 2 * cr
    for o in range(nd):
        got = inbox[o].astype(f32)
        row_list = row_list + got[tile_at : tile_at + 1]
        col_list = col_list + got[tile_at + 1 : tile_at + 2]
        for h in range(2):
            table[h, o * cr : (o + 1) * cr, :] = got[
                cells_at + h * cr : cells_at + (h + 1) * cr
            ]
        offs[:, o * TB : (o + 1) * TB] = got[6:9]
        first = 2 * o % 16
        base = 2 * o // 16 * 16
        for a in range(3):
            cheb_a[a, o, first : first + 2, :] = got[2 * a : 2 * a + 2]
            wide[a * nb + base : a * nb + base + 16, o * TB : (o + 1) * TB] = (
                cheb_a[a, o].astype(bf16)
            )
    tables = []
    for h in range(2):
        tables.append(jnp.transpose(table[h])[:, :slot_rows])
    for h in range(2):
        table[2 + h, :, :slot_rows] = tables[h]

    def kind_of(n):
        return jnp.where(n < rows_t, over(n, nb) * 2 + (n & 1), 6)

    def owner_of(n):
        return jnp.where(n < rows_t, over(n & (nb - 1), 2), n - rows_t)

    mix_rows = iota((rows_e, LANES), 0)
    mix_lanes = iota((rows_e, LANES), 1)
    all_rows = iota((LANES, LANES), 0)
    to = ((owner_of(mix_rows) + 1).astype(f32) == row_list).astype(f32).astype(bf16)
    frm = ((owner_of(all_rows) + 1).astype(f32) == col_list).astype(f32).astype(bf16)
    joined = jnp.where(
        (kind_of(mix_rows) == kind_of(mix_lanes)) & (mix_lanes < rows_e), dot_nt(to, frm), 0.0
    ).astype(bf16)
    mixer[:, :LANES] = joined
    mixer[:, LANES:] = joined

    def build_phi(o):
        lanes = slice(o * TB, (o + 1) * TB)
        q = iota((PERIOD, TB), 0).astype(f32) * (1.0 / PERIOD)
        co, si = [], []
        for a in range(3):
            turn = q * offs[a : a + 1, lanes]
            co.append(cos_turn(turn))
            si.append(cos_turn(turn - 0.25))
        flat_c, flat_s = [], []
        for x in range(PERIOD):
            cx, sx = co[0][x : x + 1], si[0][x : x + 1]
            flat_c.append(cx * co[1] - sx * si[1])
            flat_s.append(sx * co[1] + cx * si[1])
        flat_c = jnp.concatenate(flat_c, axis=0)
        flat_s = jnp.concatenate(flat_s, axis=0)
        for z in range(PLANES):
            cz, sz = co[2][z : z + 1], si[2][z : z + 1]
            at = z * 2 * FLAT
            block = jnp.concatenate([flat_c * cz - flat_s * sz, flat_s * cz + flat_c * sz], axis=0)
            phi[at : at + 2 * FLAT, lanes] = block.astype(bf16)
            modes[lanes, at : at + 2 * FLAT] = jnp.transpose(block).astype(bf16)

    y_slab, z_slab = glen // n_row, glen // n_col
    scaled = 1.0 / glen

    def locate(r, c):
        o = r * n_col + c
        code = inbox[o].astype(f32)[9:10].astype(jnp.int32)
        slot = over(code, nd)
        holder = code & (nd - 1)
        row_at = holder * cr + over(slot, per_row)
        hot = (iota((slot_rows, TB), 0) == row_at).astype(f32).astype(bf16)
        at = pl.ds(pl.multiple_of(o * per_row, per_row), per_row)
        lists = jnp.concatenate(
            [table[2, at, :slot_rows], table[3, at, :slot_rows]], axis=0
        ).astype(bf16)
        found = dot(lists, hot)
        mine = iota((per_row, TB), 0) == (slot & (per_row - 1))
        high = jnp.sum(jnp.where(mine, found[:per_row], 0.0), axis=0, keepdims=True)
        low = jnp.sum(jnp.where(mine, found[per_row:], 0.0), axis=0, keepdims=True)
        cell = high.astype(jnp.int32) * 512 + low.astype(jnp.int32) + 256
        pos_x = over(cell, y_slab * z_slab)
        pos_y = over(holder, n_col) * y_slab + (over(cell, z_slab) & (y_slab - 1))
        pos_z = (holder & (n_col - 1)) * z_slab + (cell & (z_slab - 1))
        return [p.astype(f32) * scaled for p in (pos_x, pos_y, pos_z)]

    kx_col = (me_r * xs + iota((xs, 2 * TB), 0)).astype(f32)
    ky_col = (me_c * ys + iota((ys, 2 * TB), 0)).astype(f32)
    kz_col = iota((glen, 2 * TB), 0)

    def build_phase(pair, phase):
        spots = [locate(*place(i, j)) for i, j in pair]
        px, py, pz = (
            jnp.concatenate([spots[0][t], spots[1][t]], axis=1) for t in range(3)
        )
        turn = kx_col * px
        cx, nx = cos_turn(turn), cos_turn(turn + 0.25)
        turn = ky_col * py
        cy, ny = cos_turn(turn), cos_turn(turn + 0.25)
        for i in range(xs):
            a, b = cx[i : i + 1], nx[i : i + 1]
            phase[i * ys : (i + 1) * ys, :] = (a * cy - b * ny).astype(bf16)
            phase[xy + i * ys : xy + (i + 1) * ys, :] = (b * cy + a * ny).astype(bf16)
        return cos_turn(kz_col.astype(f32) * pz + jnp.where(kz_col > half, 0.25, 0.0))

    def far_copy(i, j):
        r, c = place(i, j)
        p = r * n_col + c
        q = i * n_col + j
        return remote(far_send.at[q], far_recv.at[me], far_ss.at[q], far_rs.at[me], r, c)

    def far_sums(pair, phase, tz):
        sums = dot(hat[...], phase[...])
        for k in range(6):
            line = jnp.sum(sums[k * glen : (k + 1) * glen] * tz, axis=0, keepdims=True)
            for t, (i, j) in enumerate(pair):
                half_line = line[:, t * TB : (t + 1) * TB]
                if i + j:
                    far_send[i * n_col + j, k : k + 1, :] = half_line
                else:
                    far_recv[me, k : k + 1, :] = half_line

    def far_start(some):
        for i, j in some:
            if i + j:
                far_copy(i, j).start()

    near = [cheb_coef[0] * noise_ref[a] for a in range(3)]
    own_rows = pl.ds(lax.rem(2 * me, 16), 2)
    scales = []

    def to_modes(m):
        rows = rows_e if m == 0 else rows_t
        sums = dot(wide[0:rows, :], modes[...])
        high = sums.astype(bf16)
        mixed[0:rows, :] = high
        mixed[LANES : LANES + rows, :] = (sums - high.astype(f32)).astype(bf16)

    def convolve(m):
        rows = rows_e if m == 0 else rows_t
        sums = dot(mixer[0:rows, :], mixed[...])
        turned = jnp.concatenate(
            [
                pltpu.roll(sums[0:rows_t, g * LANES : (g + 1) * LANES], FLAT, 1)
                for g in range(PLANES)
            ],
            axis=1,
        )
        for a in range(3):
            total = spectrum[a : a + 1, :] * sums[a * nb : (a + 1) * nb]
            for b in range(3):
                if a != b:
                    e = PAIRS.index((min(a, b), max(a, b)))
                    total = total + spectrum[e : e + 1, :] * sums[b * nb : (b + 1) * nb]
                    total = total + spectrum[e + 3 : e + 4, :] * turned[b * nb : (b + 1) * nb]
            lattice[a * nb : (a + 1) * nb, :] = total.astype(bf16)
        if m == 0:
            for a in range(3):
                total = spectrum[9 + a : 10 + a, :] * sums[rows_t:rows_e]
                high = total.astype(bf16)
                at = rows_t + a * nd
                lattice[at : at + nd, :] = high
                lattice[at + 3 * nd : at + 4 * nd, :] = (total - high.astype(f32)).astype(bf16)

    def to_beads(m):
        if m == 0:
            out = dot(lattice[...], phi[...])
            energy = out[rows_t : rows_t + 3 * nd] + out[rows_t + 3 * nd :]
            top = jnp.zeros((3 * nd, TB), f32)
            owner = iota((3 * nd, TB), 0) & (nd - 1)
            for o in range(nd):
                top = jnp.maximum(
                    top, jnp.where(owner == o, energy[:, o * TB : (o + 1) * TB], 0.0)
                )
            top = jnp.max(jnp.max(top, axis=1, keepdims=True), axis=0, keepdims=True)
            scales.append(jnp.broadcast_to(1.0 / jnp.sqrt(top + 1e-06), (16, TB)))
        elif m < DEGREES - 1:
            out = dot(lattice[0:rows_t, :], phi[...])
        scale = scales[0]
        before = cheb_b if m % 2 == 0 else cheb_a
        if m < DEGREES - 1:
            line = iota((16, TB), 0)
            for o in range(nd):
                first = 2 * o % 16
                base = 2 * o // 16 * 16
                mine = (line >= first) & (line < first + 2)
                for a in range(3):
                    got = out[a * nb + base : a * nb + base + 16, o * TB : (o + 1) * TB]
                    got = jnp.where(mine, scale * got, 0.0)
                    if m > 0:
                        got = 2.0 * got - before[a, o]
                    before[a, o] = got
                    wide[a * nb + base : a * nb + base + 16, o * TB : (o + 1) * TB] = (
                        got.astype(bf16)
                    )
            for a in range(3):
                near[a] = near[a] + cheb_coef[m + 1] * before[a, me, own_rows, :]
        else:
            last[...] = dot(
                lattice[0:rows_t, :], phi[:, pl.ds(pl.multiple_of(me * TB, TB), TB)]
            )
            for a in range(3):
                got = 2.0 * (scale[0:2] * last[pl.ds(a * nb + 2 * me, 2), :])
                near[a] = near[a] + cheb_coef[m + 1] * (got - before[a, me, own_rows, :])

    stages = [
        functools.partial(stage, m)
        for m in range(DEGREES) for stage in (to_modes, convolve, to_beads)
    ]
    pairs = [peers[t : t + 2] for t in range(0, nd, 2)]
    phases = (phase_a, phase_b)
    built = -(-3 * len(pairs) // 8)
    sends = (len(pairs) - 3, len(pairs) - 1)
    held = []
    tz = build_phase(pairs[0], phase_a)
    for n, pair in enumerate(pairs):
        nxt = None
        if n + 1 < len(pairs):
            nxt = build_phase(pairs[n + 1], phases[(n + 1) % 2])
        if n >= built and False:
            stages.pop(0)()
        far_sums(pair, phases[n % 2], tz)
        tz = nxt
        held += pair
        if n in sends:
            far_start(held)
            held = []
        if n < built:
            for o in range(n * nd // built, (n + 1) * nd // built):
                build_phi(o)
    for stage in stages:
        stage()

    for i, j in others:
        msg_copy(i, j).wait_send()

    def far_arrive(i, j):
        r, c = place(i, j)
        p = r * n_col + c
        remote(far_send.at[0], far_recv.at[p], far_ss.at[0], far_rs.at[p], r, c).wait_recv()

    for i, j in others:
        far_arrive(i, j)
    for i, j in others:
        far_copy(i, j).wait_send()
    far = far_recv[0]
    for p in range(1, nd):
        far = far + far_recv[p]
    for a in range(3):
        out_ref[a] = near[a] + far[2 * a : 2 * a + 2, :]


def shared_device(noise_field, offsets, tile_list, send_cells, bead_slot, spectral):
    n_row = lax.axis_size("row")
    n_col = lax.axis_size("col")
    nd = n_row * n_col
    xs, ys, glen = spectral.shape[3:]
    slots = tile_list.shape[3]
    cap = send_cells.shape[2]
    xy = xs * ys
    cr = cap * nd // LANES
    msg_rows = -(-(12 + 2 * cr) // 16) * 16
    chunks = 4 if xy % 256 == 0 else 1
    dims = (n_row, n_col, slots, xs, ys, glen, cap)
    vmem = pl.BlockSpec(memory_space=pltpu.VMEM)
    hbm = pl.BlockSpec(memory_space=pl.ANY)
    dma = pltpu.SemaphoreType.DMA
    rows_t = 6 * nd
    spectrum = lattice_spectrum()
    return pl.pallas_call(
        functools.partial(shared_kernel, dims),
        out_shape=pltpu.VMEM(noise_field.shape, f32),
        in_specs=[hbm] * 7,
        out_specs=vmem,
        scratch_shapes=[
            pltpu.SMEM((2, slots), jnp.int32),
            pltpu.VMEM(noise_field.shape, f32),
            pltpu.VMEM(offsets.shape, jnp.int32),
            pltpu.VMEM((1, TB), jnp.int32),
            pltpu.VMEM((cap, nd), jnp.int32),
            pltpu.VMEM((12, xy, glen), f32),
            pltpu.VMEM((6 * (xy // chunks), 2 * glen), bf16),
            pltpu.VMEM((6 * glen, 2 * xy), bf16),
            pltpu.VMEM((2 * xy, 2 * TB), bf16),
            pltpu.VMEM((2 * xy, 2 * TB), bf16),
            pltpu.VMEM((MODES, nd * TB), bf16),
            pltpu.VMEM((nd * TB, MODES), bf16),
            pltpu.VMEM((rows_t + nd, nd * TB), bf16),
            pltpu.VMEM((3, nd, 16, TB), f32),
            pltpu.VMEM((3, nd, 16, TB), f32),
            pltpu.VMEM((rows_t + nd, 2 * LANES), bf16),
            pltpu.VMEM((2 * LANES, MODES), bf16),
            pltpu.VMEM((rows_t + 6 * nd, MODES), bf16),
            pltpu.VMEM((msg_rows, LANES), f32),
            pltpu.VMEM((msg_rows, LANES), bf16),
            pltpu.VMEM((nd, msg_rows, LANES), bf16),
            pltpu.VMEM((4, LANES, LANES), f32),
            pltpu.VMEM((3, nd * TB), f32),
            pltpu.VMEM(spectrum.shape, f32),
            pltpu.VMEM((rows_t, TB), f32),
            pltpu.VMEM((nd, 8, TB), f32),
            pltpu.VMEM((nd, 8, TB), f32),
            dma((5,)), dma((chunks,)), dma,
            dma((nd,)), dma((nd,)),
            dma((nd,)), dma((nd,)),
        ],
        compiler_params=pltpu.CompilerParams(
            collective_id=1, has_side_effects=True, vmem_limit_bytes=56 * 1024 * 1024
        ),
    )(
        tile_list.reshape(2, slots),
        noise_field,
        offsets,
        bead_slot.reshape(1, TB),
        send_cells.reshape(cap, nd),
        jnp.asarray(spectrum),
        spectral.reshape(12, xy, glen),
    )


def power_of_two(n):
    return n & (n - 1) == 0


def per_device(noise_field, offsets, tile_list, send_cells, bead_slot, spectral):
    n_row = lax.axis_size("row")
    n_col = lax.axis_size("col")
    nd = n_row * n_col
    xs, ys, glen = spectral.shape[3:]
    cap = send_cells.shape[2]
    fits = (
        8 <= nd <= 16
        and power_of_two(n_row)
        and power_of_two(n_col)
        and power_of_two(glen)
        and nd * tile_list.shape[3] <= LANES
        and cap % (LANES // nd) == 0
        and cap * nd <= 256
        and glen * (glen // n_row) * (glen // n_col) <= 1 << 17
        and ys % 16 == 0
    )
    run = shared_device if fits else spread_device
    return run(noise_field, offsets, tile_list, send_cells, bead_slot, spectral)


def solution(mesh):
    return jax.shard_map(
        per_device,
        mesh=mesh,
        in_specs=(
            P(None, None, ("groups", "row", "col")),
            P(None, ("groups", "row", "col")),
            P(("groups", "row"), "col", None, None),
            P(("groups", "row"), "col", None, None),
            P(("groups", "row", "col")),
            P(None, None, None, ("groups", "row"), "col", None),
        ),
        out_specs=P(None, None, ("groups", "row", "col")),
        check_vma=False,
    )
```

```python
import functools
import math

import jax
import jax.numpy as jnp
import ml_dtypes
import numpy as np
from jax import lax
from jax.experimental import pallas as pl
from jax.experimental.pallas import tpu as pltpu
from jax.sharding import PartitionSpec as P

TB = 128
LANES = 128
PERIOD = 8
DEGREES = 4

cheb_coef = (1.0, 0.45, -0.2, 0.12, -0.08)
kernel_range = 1.5

f32 = jnp.float32
bf16 = jnp.bfloat16


def iota(shape, dim):
    return lax.broadcasted_iota(jnp.int32, shape, dim)


def over(n, d):
    return lax.shift_right_logical(n, jnp.full(n.shape, d.bit_length() - 1, jnp.int32))


def dot(a, b):
    return jnp.dot(a, b, preferred_element_type=f32)


def dot_nt(a, b):
    return lax.dot_general(a, b, (((1,), (1,)), ((), ())), preferred_element_type=f32)


def cos_turn(turns):
    x = jnp.abs(turns - jnp.floor(turns) - 0.5) * 4.0 - 1.0
    x2 = x * x
    p = 0.00015148419
    for c in (-0.00467376557, 0.07968967928, -0.64596371106, 1.57079631847):
        p = p * x2 + c
    return p * x


def kernel(
    dims,
    tiles_ref, noise_ref, off_ref, slot_ref, cells_ref, spec_hbm,
    out_ref,
    spec, pre, hat, phase, ang, wang, tabf, tab, kmat,
    a_send, a_recv, b_send, row_b, col_b,
    e_send, e_recv, y_send, y_recv, far_send, far_recv,
    cur, prev, acc, scale,
    spec_sem, a_ss, a_rs, b_ss, b_rs, e_ss, e_rs, y_ss, y_rs, far_ss, far_rs,
):
    n_row, n_col, slots, xs, ys, glen, cap = dims
    nd = n_row * n_col
    xy = xs * ys
    cr = cap * nd // LANES
    kq = tab.shape[0]
    beads = n_col * TB
    me_r = lax.axis_index("row")
    me_c = lax.axis_index("col")
    me = me_r * n_col + me_c
    chunks = spec_sem.shape[0]
    part = xy // chunks
    per_row = LANES // nd

    def spec_copy(i):
        rows = pl.ds(i * part, part)
        return pltpu.make_async_copy(
            spec_hbm.at[:, rows, :], spec.at[:, rows, :], spec_sem.at[i]
        )

    for i in range(chunks):
        spec_copy(i).start()

    straight = nd <= 32
    if straight:
        rows_of = [me_r] + [lax.rem(me_r + d, n_row) for d in range(1, n_row)]
        cols_of = [me_c] + [lax.rem(me_c + d, n_col) for d in range(1, n_col)]
        order = sorted(
            [(i, j) for i in range(n_row) for j in range(n_col) if i + j],
            key=lambda t: (abs(t[1] - n_col // 2), abs(t[0] - n_row // 2)),
        )

    def each(body):
        if straight:
            for i, j in order:
                body(rows_of[i], cols_of[j])
            return

        def turn(d, carry):
            body(lax.rem(me_r + d // n_col, n_row), lax.rem(me_c + lax.rem(d, n_col), n_col))
            return carry

        lax.fori_loop(1, nd, turn, 0)

    def each_row(body):
        if straight:
            for d in range(1, n_row):
                body(rows_of[d])
        else:
            lax.fori_loop(1, n_row, lambda d, t: (body(lax.rem(me_r + d, n_row)), t)[1], 0)

    def each_col(body):
        if straight:
            for d in range(1, n_col):
                body(cols_of[d])
        else:
            lax.fori_loop(1, n_col, lambda d, t: (body(lax.rem(me_c + d, n_col)), t)[1], 0)

    barrier = pltpu.get_barrier_semaphore()

    def greet(r, c):
        pl.semaphore_signal(
            barrier, inc=1, device_id={"row": r, "col": c},
            device_id_type=pl.DeviceIdType.MESH,
        )

    each(greet)

    def remote(src, dst, ss, rs, r, c):
        return pltpu.make_async_remote_copy(
            src_ref=src, dst_ref=dst, send_sem=ss, recv_sem=rs,
            device_id={"row": r, "col": c}, device_id_type=pl.DeviceIdType.MESH,
        )

    def packed_cells():
        flat = cells_ref[...].astype(f32)
        if per_row == 1:
            return flat
        spread = (iota((nd, LANES), 1) & (nd - 1)) == iota((nd, LANES), 0)
        wide = jnp.dot(
            flat, spread.astype(f32), precision=lax.Precision.HIGHEST,
            preferred_element_type=f32,
        )
        mine = over(iota((cap, LANES), 1), nd) == (iota((cap, LANES), 0) & (per_row - 1))
        return jnp.sum(jnp.where(mine, wide, 0.0).reshape(cr, per_row, LANES), axis=1)

    a_send[0:1, :] = slot_ref[...].astype(f32)
    cells = packed_cells()
    a_send[1 : 1 + cr, :] = cells
    a_recv[me, 0:1, :] = slot_ref[...].astype(f32)
    a_recv[me, 1 : 1 + cr, :] = cells
    own_noise = jnp.concatenate([noise_ref[0], noise_ref[1], noise_ref[2]], axis=1)
    off = off_ref[...].astype(f32)
    own_off = jnp.concatenate([off[0:1], off[1:2], off[2:3]], axis=1)
    b_send[0:2, :] = own_noise
    b_send[2:3, :] = own_off
    row_b[me_c, 0:2, :] = own_noise
    row_b[me_c, 2:3, :] = own_off
    col_b[me_r, 0:2, :] = own_noise
    col_b[me_r, 2:3, :] = own_off
    tabf[...] = jnp.zeros_like(tabf)

    pl.semaphore_wait(barrier, nd - 1)

    def b_row_copy(c):
        return remote(b_send, row_b.at[me_c], b_ss.at[c], b_rs.at[me_c], me_r, c)

    def b_col_copy(r):
        return remote(
            b_send, col_b.at[me_r], b_ss.at[n_col + r], b_rs.at[n_col + me_r], r, me_c
        )

    each_col(lambda c: b_row_copy(c).start())
    each_row(lambda r: b_col_copy(r).start())

    def a_copy(r, c):
        p = r * n_col + c
        return remote(a_send, a_recv.at[me], a_ss.at[p], a_rs.at[me], r, c)

    each(lambda r, c: a_copy(r, c).start())

    gi = iota((2 * glen, 2 * glen), 0)
    gj = iota((2 * glen, 2 * glen), 1)
    zi, zj = gi & (glen - 1), gj & (glen - 1)
    in_im, out_im = gi >= glen, gj >= glen
    half = glen // 2
    same = zi == zj
    mirror = (zi + zj == glen) & (zi != zj)
    even = zj <= half
    plain = in_im == out_im
    fold = jnp.where(
        even,
        jnp.where(plain & (same | mirror), 1.0, 0.0),
        jnp.where(
            plain,
            0.0,
            jnp.where(same, 1.0, 0.0) - jnp.where(mirror, 1.0, 0.0),
        )
        * jnp.where(out_im, -1.0, 1.0),
    ).astype(bf16)

    width_sq = (glen / 8.0) ** 2
    front = math.sqrt(1.5) / (2.0 * math.pi * width_sq) ** 0.75
    def signed(n):
        return jnp.where(n < half, n, n - glen).astype(f32)

    ky = signed(me_c * ys + iota((ys, glen), 0))
    kz = signed(iota((ys, glen), 1))
    kyz_sq = ky * ky + kz * kz

    def hat_block(i, first):
        kx = signed(me_r * xs + i)
        q = kx * kx + kyz_sq
        amp = jnp.where(q > 0, front * jnp.exp(q * (-0.25 / width_sq)), 0.0)
        damp = amp / jnp.maximum(q, 1.0)
        rows = pl.ds(pl.multiple_of(i * ys, ys), ys)
        at = pl.multiple_of((i - first) * ys, ys)
        waves = (kx, ky, kz)
        for v in range(2):
            for p in range(2):
                s = [spec[(p * 3 + a) * 2 + v, rows, :] for a in range(3)]
                along = (kx * s[0] + ky * s[1] + kz * s[2]) * damp
                for a in range(3):
                    pre[pl.ds((a * 2 + v) * part + at, ys), p * glen : (p + 1) * glen] = (
                        amp * s[a] - waves[a] * along
                    ).astype(bf16)
        return first

    per = part // ys
    for i in range(chunks):
        spec_copy(i).wait()
        lax.fori_loop(i * per, (i + 1) * per, hat_block, i * per)
        folded = dot(pre[...], fold)
        for k in range(6):
            for p in range(2):
                hat[
                    p * xy + i * part : p * xy + (i + 1) * part, k * glen : (k + 1) * glen
                ] = folded[
                    k * part : (k + 1) * part, p * glen : (p + 1) * glen
                ].astype(bf16)

    def b_col_arrive(r):
        remote(b_send, col_b.at[r], b_ss.at[n_col + r], b_rs.at[n_col + r], r, me_c).wait_recv()

    def b_row_arrive(c):
        remote(b_send, row_b.at[c], b_ss.at[c], b_rs.at[c], me_r, c).wait_recv()

    each_row(b_col_arrive)
    each_col(b_row_arrive)

    eye = (iota((TB, TB), 0) == iota((TB, TB), 1)).astype(f32)
    ones = jnp.ones((TB, TB), bf16)
    scale_sq = kernel_range * kernel_range

    def pick(values, into, s):
        tr = tiles_ref[0, s]
        return tuple(
            into[i] + values * jnp.where(tr == i, 1.0, 0.0).astype(f32) for i in range(n_col)
        )

    def build(s, energies):
        tr = jnp.maximum(tiles_ref[0, s], 0)
        tc = jnp.maximum(tiles_ref[1, s], 0)
        row_off = row_b[tr][2:3, :]
        col_off = col_b[tc][2:3, :]
        disp = []
        for a in range(3):
            lanes = slice(a * TB, (a + 1) * TB)
            rp = dot((eye * row_off[:, lanes]).astype(bf16), ones)
            gap = (rp - col_off[:, lanes]).astype(jnp.int32) + PERIOD // 2
            disp.append(((gap & (PERIOD - 1)) - PERIOD // 2).astype(f32))
        squares = disp[0] * disp[0] + disp[1] * disp[1] + disp[2] * disp[2]
        envelope = jnp.exp(squares * (-0.5 / scale_sq)) / scale_sq
        third = squares / 3.0
        for a in range(3):
            for b in range(a, 3):
                element = disp[a] * disp[b]
                if a == b:
                    element = element - third
                entry = (envelope * element).astype(bf16)
                kmat[s, a * TB : (a + 1) * TB, b * TB : (b + 1) * TB] = entry
                if a != b:
                    kmat[s, b * TB : (b + 1) * TB, a * TB : (a + 1) * TB] = entry
        wide = kmat[s].astype(f32)
        sq = wide * wide
        high = sq.astype(bf16)
        low = (sq - high.astype(f32)).astype(bf16)
        one_row = jnp.ones((8, 3 * TB), bf16)
        energy = dot_nt(one_row, high) + dot_nt(one_row, low)
        return pick(energy[0:1], energies, s)

    energies = lax.fori_loop(
        0, slots, build, tuple(jnp.zeros((1, 3 * TB), f32) for _ in range(n_col)),
        unroll=slots <= 4,
    )
    for i in range(n_col):
        e_send[i : i + 1, :] = energies[i]
        e_recv[me, i : i + 1, :] = energies[i]

    def e_copy(r, c):
        p = r * n_col + c
        return remote(e_send, e_recv.at[me], e_ss.at[p], e_rs.at[me], r, c)

    for r in range(n_row):
        cur[r] = col_b[r, 0:2, :]
    acc[...] = cheb_coef[0] * own_noise

    def a_arrive(r, c):
        p = r * n_col + c
        remote(a_send, a_recv.at[p], a_ss.at[p], a_rs.at[p], r, c).wait_recv()

    def prepare_table():
        each(a_arrive)

        def spread(h, carry):
            tabf[pl.ds(h * cr, cr), :] = a_recv[h, 1 : 1 + cr, :]
            return carry

        lax.fori_loop(0, nd, spread, 0)
        cell = tabf[...].astype(jnp.int32)
        y_slab, z_slab = glen // n_row, glen // n_col
        holder = over(iota((kq, LANES), 0), cr)
        pos_x = over(cell, y_slab * z_slab)
        pos_y = over(holder, n_col) * y_slab + (over(cell, z_slab) & (y_slab - 1))
        pos_z = (holder & (n_col - 1)) * z_slab + (cell & (z_slab - 1))
        for at, pos in enumerate((pos_x, pos_y, pos_z)):
            tab[:, at * LANES : (at + 1) * LANES] = pos.astype(f32).astype(bf16)

    x_step = LANES // ys
    lane = iota((LANES, LANES), 1)
    scaled = 1.0 / glen
    along_x = ((me_r * xs + over(lane, ys)).astype(f32) * scaled).astype(bf16)
    along_y = ((me_c * ys + (lane & (ys - 1))).astype(f32) * scaled).astype(bf16)
    wang[...] = jnp.zeros_like(wang)
    wang[0:LANES, 0:LANES] = along_x
    wang[LANES : 2 * LANES, 0:LANES] = along_y
    wang[0:LANES, LANES : 2 * LANES] = jnp.full((LANES, LANES), x_step * scaled, bf16)
    wang[2 * LANES :, 2 * LANES :] = (lane.astype(f32) * scaled).astype(bf16)
    rep = over(iota((8, 6 * glen), 1), glen) == iota((8, 6 * glen), 0)
    rep = rep.astype(f32).astype(bf16)
    wide_ones = jnp.ones((TB, kq), bf16)
    step_rows = 32

    def far_copy(i, c):
        return remote(
            far_send.at[i * n_col + c], far_recv.at[me],
            far_ss.at[i * n_col + c], far_rs.at[me], i, c,
        )

    def far_chunk(i, carry):
        spots = jnp.concatenate(
            [eye * a_recv[i * n_col + c, 0:1, :] for c in range(n_col)], axis=0
        ).astype(bf16)
        code = dot(spots, wide_ones).astype(jnp.int32)
        s_idx = over(code, nd)
        row_idx = (code & (nd - 1)) * cr + over(s_idx, per_row)
        hot = (row_idx == iota((beads, kq), 1)).astype(f32).astype(bf16)
        found = dot(hot, tab[...])
        owner_of = i * n_col + over(iota((beads, LANES), 0), TB)
        want = (s_idx[:, :LANES] & (per_row - 1)) * nd + owner_of
        keep = want == iota((beads, LANES), 1)
        places = jnp.concatenate(
            [jnp.where(keep, found[:, k * LANES : (k + 1) * LANES], 0.0) for k in range(3)],
            axis=1,
        ).astype(bf16)
        ang[...] = dot(places, wang[...])

        def phase_block(j, carry):
            rows = pl.ds(pl.multiple_of(j * step_rows, step_rows), step_rows)
            at_lane = iota((step_rows, LANES), 1)
            start = ang[rows, 0:LANES]
            co = cos_turn(start)
            ns = cos_turn(start + 0.25)
            turn_x = cos_turn(
                ang[rows, LANES : 2 * LANES] - jnp.where(at_lane == 1, 0.25, 0.0)
            )
            cd = jnp.broadcast_to(turn_x[:, 0:1], co.shape)
            sd = jnp.broadcast_to(turn_x[:, 1:2], co.shape)
            ang[rows, 2 * LANES :] = cos_turn(
                ang[rows, 2 * LANES :] + jnp.where(at_lane > half, 0.25, 0.0)
            )
            for g in range(xy // LANES):
                phase[rows, g * LANES : (g + 1) * LANES] = co.astype(bf16)
                phase[rows, xy + g * LANES : xy + (g + 1) * LANES] = ns.astype(bf16)
                co, ns = co * cd + ns * sd, ns * cd - co * sd
            return carry

        lax.fori_loop(0, beads // step_rows, phase_block, 0)
        sums = dot(phase[...], hat[...])
        tz = ang[:, 2 * LANES :]
        weighted = jnp.concatenate(
            [(sums[:, k * glen : (k + 1) * glen] * tz).astype(bf16) for k in range(6)], axis=1
        )
        res = dot_nt(rep, weighted)
        for c in range(n_col):
            owner = i * n_col + c
            far_send[owner] = res[:, c * TB : (c + 1) * TB]

            @pl.when(owner == me)
            def _():
                far_recv[me] = res[:, c * TB : (c + 1) * TB]

            @pl.when(owner != me)
            def _():
                far_copy(i, c).start()

        return carry

    def y_copy(r, c, par):
        p = r * n_col + c
        return remote(
            y_send.at[par, c], y_recv.at[par, me], y_ss.at[par, p], y_rs.at[par, me], r, c
        )

    def y_arrive(r, c, par):
        p = r * n_col + c
        remote(
            y_send.at[par, 0], y_recv.at[par, p], y_ss.at[par, p], y_rs.at[par, p], r, c
        ).wait_recv()

    each(lambda r, c: e_copy(r, c).start())

    def degree_step(m, carry):
        par = lax.rem(m, 2)

        def apply(s, sums):
            tc = jnp.maximum(tiles_ref[1, s], 0)
            w = cur[tc]
            w = jnp.concatenate([w, jnp.zeros((6, 3 * TB), f32)], axis=0).astype(bf16)
            return pick(dot_nt(w, kmat[s])[0:2], sums, s)

        sums = lax.fori_loop(
            0, slots, apply, tuple(jnp.zeros((2, 3 * TB), f32) for _ in range(n_col)),
            unroll=slots <= 4,
        )
        own = jnp.zeros((2, 3 * TB), f32)
        for i in range(n_col):
            y_send[par, i] = sums[i]
            own = own + sums[i] * jnp.where(me_c == i, 1.0, 0.0).astype(f32)
        y_recv[par, me] = own
        each(lambda r, c: y_copy(r, c, par).start())

        @pl.when(m == 0)
        def _():
            prepare_table()

        lax.fori_loop(m * n_row // DEGREES, (m + 1) * n_row // DEGREES, far_chunk, 0)

        @pl.when(m == 0)
        def _():
            def e_arrive(r, c):
                p = r * n_col + c
                remote(e_send, e_recv.at[p], e_ss.at[p], e_rs.at[p], r, c).wait_recv()

            each(e_arrive)
            top = jnp.zeros((n_col, 3 * TB), f32)
            for r in range(n_row):
                total = e_recv[r * n_col]
                for c in range(1, n_col):
                    total = total + e_recv[r * n_col + c]
                top = jnp.maximum(top, total)
            largest = jnp.max(jnp.max(top, axis=1, keepdims=True), axis=0, keepdims=True)
            scale[...] = jnp.broadcast_to(1.0 / jnp.sqrt(largest + 1e-06), scale.shape)

        each(lambda r, c: y_arrive(r, c, par))
        each(lambda r, c: y_copy(r, c, par).wait_send())
        first = jnp.where(m == 0, 1.0, 0.0).astype(f32)
        coef = jnp.where(
            m == 0, cheb_coef[1],
            jnp.where(m == 1, cheb_coef[2], jnp.where(m == 2, cheb_coef[3], cheb_coef[4])),
        ).astype(f32)
        sc = jnp.concatenate([scale[0:2, :]] * 3, axis=1)

        def advance(r, carry):
            total = y_recv[par, r * n_col]
            for c in range(1, n_col):
                total = total + y_recv[par, r * n_col + c]
            now = sc * total
            following = jnp.where(m == 0, now, 2.0 * now - prev[r])
            prev[r] = cur[r]
            cur[r] = following
            return carry

        lax.fori_loop(0, n_row, advance, 0)
        acc[...] = acc[...] + coef * cur[me_r]
        return carry

    prev[...] = jnp.zeros_like(prev)
    lax.fori_loop(0, DEGREES, degree_step, 0)

    each_row(lambda r: b_col_copy(r).wait_send())
    each_col(lambda c: b_row_copy(c).wait_send())
    each(lambda r, c: a_copy(r, c).wait_send())
    each(lambda r, c: e_copy(r, c).wait_send())

    def far_arrive(r, c):
        p = r * n_col + c
        remote(
            far_send.at[p], far_recv.at[p], far_ss.at[p], far_rs.at[p], r, c
        ).wait_recv()

    each(far_arrive)
    each(lambda r, c: far_copy(r, c).wait_send())
    far = lax.fori_loop(
        1, nd, lambda p, t: t + far_recv[p], far_recv[0]
    )
    near = acc[...]
    for a in range(3):
        out_ref[a] = near[:, a * TB : (a + 1) * TB] + far[2 * a : 2 * a + 2, :]


def spread_device(noise_field, offsets, tile_list, send_cells, bead_slot, spectral):
    n_row = lax.axis_size("row")
    n_col = lax.axis_size("col")
    nd = n_row * n_col
    xs, ys, glen = spectral.shape[3:]
    slots = tile_list.shape[3]
    cap = send_cells.shape[2]
    cr = cap * nd // LANES
    xy = xs * ys
    kq = max(LANES, nd * cr)
    beads = n_col * TB
    a_rows = -(-(1 + cr) // 4) * 4
    chunks = 4 if xy % 256 == 0 else 1
    dims = (n_row, n_col, slots, xs, ys, glen, cap)
    vmem = pl.BlockSpec(memory_space=pltpu.VMEM)
    dma = pltpu.SemaphoreType.DMA
    wide = 3 * TB
    return pl.pallas_call(
        functools.partial(kernel, dims),
        out_shape=jax.ShapeDtypeStruct(noise_field.shape, f32),
        in_specs=[pl.BlockSpec(memory_space=pltpu.SMEM), vmem, vmem, vmem, vmem,
                  pl.BlockSpec(memory_space=pl.ANY)],
        out_specs=vmem,
        scratch_shapes=[
            pltpu.VMEM((12, xy, glen), f32),
            pltpu.VMEM((6 * (xy // chunks), 2 * glen), bf16),
            pltpu.VMEM((2 * xy, 6 * glen), bf16),
            pltpu.VMEM((beads, 2 * xy), bf16),
            pltpu.VMEM((beads, 3 * LANES), f32),
            pltpu.VMEM((3 * LANES, 3 * LANES), bf16),
            pltpu.VMEM((kq, LANES), f32),
            pltpu.VMEM((kq, 3 * LANES), bf16),
            pltpu.VMEM((slots, wide, wide), bf16),
            pltpu.VMEM((a_rows, LANES), f32),
            pltpu.VMEM((nd, a_rows, LANES), f32),
            pltpu.VMEM((4, wide), f32),
            pltpu.VMEM((n_col, 4, wide), f32),
            pltpu.VMEM((n_row, 4, wide), f32),
            pltpu.VMEM((n_col, wide), f32),
            pltpu.VMEM((nd, n_col, wide), f32),
            pltpu.VMEM((2, n_col, 2, wide), f32),
            pltpu.VMEM((2, nd, 2, wide), f32),
            pltpu.VMEM((nd, 8, TB), f32),
            pltpu.VMEM((nd, 8, TB), f32),
            pltpu.VMEM((n_row, 2, wide), f32),
            pltpu.VMEM((n_row, 2, wide), f32),
            pltpu.VMEM((2, wide), f32),
            pltpu.VMEM((8, LANES), f32),
            dma((chunks,)),
            dma((nd,)), dma((nd,)),
            dma((n_row + n_col,)), dma((n_row + n_col,)),
            dma((nd,)), dma((nd,)),
            dma((2, nd)), dma((2, nd)),
            dma((nd,)), dma((nd,)),
        ],
        compiler_params=pltpu.CompilerParams(
            collective_id=0, has_side_effects=True, vmem_limit_bytes=56 * 1024 * 1024
        ),
    )(
        tile_list.reshape(2, slots),
        noise_field,
        offsets,
        bead_slot.reshape(1, TB),
        send_cells.reshape(cap, nd),
        spectral.reshape(12, xy, glen),
    )


HALF = PERIOD // 2
FLAT = PERIOD * PERIOD
GROUPS = HALF
MODES = PERIOD**3
PAIRS = ((0, 0), (1, 1), (2, 2), (0, 1), (0, 2), (1, 2))


def lattice_spectrum():
    code = np.arange(PERIOD**3)
    site = np.stack([code // FLAT, code // PERIOD % PERIOD, code % PERIOD])
    disp = (site + PERIOD // 2) % PERIOD - PERIOD // 2
    d = disp.astype(np.float32)
    squares = d[0] * d[0] + d[1] * d[1] + d[2] * d[2]
    scale_sq = np.float32(kernel_range * kernel_range)
    envelope = np.exp(squares * np.float32(-0.5 / scale_sq)) / scale_sq
    table = np.zeros((3, 3, PERIOD**3))
    for a, b in PAIRS:
        element = d[a] * d[b]
        if a == b:
            element = element - squares / np.float32(3.0)
        table[a, b] = (envelope * element).astype(ml_dtypes.bfloat16).astype(np.float64)
        table[b, a] = table[a, b]
    energy = (table * table).sum(axis=1)
    ends = [(x, y) for y in (0, HALF) for x in range(HALF)]
    middle = [(x, y) for y in range(1, HALF) for x in range(PERIOD)]
    turned = [(HALF if x == 0 else x, y) for x, y in ends]
    modes = []
    for part, lead in enumerate((ends, turned)):
        modes += [(x, y, z, part) for z in (0, HALF) for x, y in lead + middle]
    for z in range(1, HALF):
        modes += [(n % PERIOD, n // PERIOD, z, p) for p in range(2) for n in range(FLAT)]
    wave = np.array(modes)
    angle = 2.0 * np.pi / PERIOD * ((wave[:, :3] @ site) % PERIOD)
    alone = (wave[:, :3] % HALF == 0).all(axis=1)
    weight = np.where(alone, 1.0, 2.0) / PERIOD**3
    turn = np.where(wave[:, 3] == 0, 1.0, -1.0)
    rows = [weight * (np.cos(angle) @ table[p]) for p in PAIRS]
    rows += [-turn * weight * (np.sin(angle) @ table[p]) for p in PAIRS[3:]]
    rows += [weight * (np.cos(angle) @ energy[a]) for a in range(3)]
    rows += [np.zeros(MODES)] * (-len(rows) % 8)
    return np.stack(rows).astype(np.float32)


def shared_kernel(
    dims,
    tiles_hbm, noise_hbm, off_hbm, slot_hbm, cells_hbm, spectrum_hbm, spec_hbm,
    out_ref,
    tiles_ref, noise_ref, off_ref, slot_ref, cells_ref,
    spec, pre, hat, phase_a, phase_b, phi, modes, wide, cheb_a, cheb_b, mixer, mixed, lattice,
    msg_f, msg, inbox, table, offs, spectrum, last,
    far_send, far_recv,
    load_sem, spec_sem, spectrum_sem, m_ss, m_rs, far_ss, far_rs,
):
    n_row, n_col, slots, xs, ys, glen, cap = dims
    nd = n_row * n_col
    xy = xs * ys
    per_row = LANES // nd
    cr = cap // per_row
    cells_at = 10
    tile_at = cells_at + 2 * cr
    beads = nd * TB
    me_r = lax.axis_index("row")
    me_c = lax.axis_index("col")
    me = me_r * n_col + me_c
    chunks = spec_sem.shape[0]
    part = xy // chunks
    nb = 2 * nd
    rows_t = 3 * nb
    rows_e = rows_t + nd

    def spec_copy(i):
        rows = pl.ds(i * part, part)
        return pltpu.make_async_copy(
            spec_hbm.at[:, rows, :], spec.at[:, rows, :], spec_sem.at[i]
        )

    loads = [
        pltpu.make_async_copy(src, dst, load_sem.at[k])
        for k, (src, dst) in enumerate((
            (cells_hbm, cells_ref), (tiles_hbm, tiles_ref), (noise_hbm, noise_ref),
            (off_hbm, off_ref), (slot_hbm, slot_ref),
        ))
    ]

    peers = sorted(
        [(i, j) for i in range(n_row) for j in range(n_col)], key=lambda t: (-t[1], -t[0])
    )
    others = peers[:-1]

    def place(i, j):
        return jnp.bitwise_xor(me_r, i), jnp.bitwise_xor(me_c, j)

    barrier = pltpu.get_barrier_semaphore()
    for i, j in others:
        r, c = place(i, j)
        pl.semaphore_signal(
            barrier, inc=1, device_id={"row": r, "col": c},
            device_id_type=pl.DeviceIdType.MESH,
        )
    for load in loads:
        load.start()
    for i in range(chunks):
        spec_copy(i).start()
    spectrum_copy = pltpu.make_async_copy(spectrum_hbm, spectrum, spectrum_sem)
    spectrum_copy.start()

    def remote(src, dst, ss, rs, r, c):
        return pltpu.make_async_remote_copy(
            src_ref=src, dst_ref=dst, send_sem=ss, recv_sem=rs,
            device_id={"row": r, "col": c}, device_id_type=pl.DeviceIdType.MESH,
        )

    for load in loads:
        load.wait()
    for a in range(3):
        msg_f[2 * a : 2 * a + 2, :] = noise_ref[a]
    msg_f[6:9, :] = off_ref[...].astype(f32)
    msg_f[9:10, :] = slot_ref[...].astype(f32)
    spread = over(iota((nd, LANES), 1), per_row) == iota((nd, LANES), 0)
    spread = spread.astype(f32).astype(bf16)
    keep = (iota((cap, LANES), 1) & (per_row - 1)) == (iota((cap, LANES), 0) & (per_row - 1))
    cells = cells_ref[...]
    for h, half_cell in enumerate((over(cells, 512), (cells & 511) - 256)):
        out = dot(half_cell.astype(f32).astype(bf16), spread)
        out = jnp.sum(jnp.where(keep, out, 0.0).reshape(cr, per_row, LANES), axis=1)
        msg_f[cells_at + h * cr : cells_at + (h + 1) * cr, :] = out
    lane_row = iota((1, LANES), 1)
    row_list = jnp.zeros((1, LANES), jnp.int32)
    col_list = jnp.zeros((1, LANES), jnp.int32)
    for s in range(slots):
        here = lane_row == me * slots + s
        tr, tc = tiles_ref[0, s], tiles_ref[1, s]
        row_list = jnp.where(
            here & (jnp.full((1, LANES), tr) >= 0), me_r * n_col + tr + 1, row_list
        )
        col_list = jnp.where(here, tc * n_col + me_c + 1, col_list)
    msg_f[tile_at : tile_at + 1, :] = row_list.astype(f32)
    msg_f[tile_at + 1 : tile_at + 2, :] = col_list.astype(f32)
    if tile_at + 2 < msg_f.shape[0]:
        msg_f[tile_at + 2 :, :] = jnp.zeros((msg_f.shape[0] - tile_at - 2, LANES), f32)
    msg[...] = msg_f[...].astype(bf16)
    inbox[me] = msg_f[...].astype(bf16)

    pl.semaphore_wait(barrier, nd - 1)

    def msg_copy(i, j):
        r, c = place(i, j)
        p = i * n_col + j
        return remote(msg, inbox.at[me], m_ss.at[p], m_rs.at[me], r, c)

    def msg_arrive(i, j):
        r, c = place(i, j)
        p = r * n_col + c
        remote(msg, inbox.at[p], m_ss.at[0], m_rs.at[p], r, c).wait_recv()

    for i, j in others:
        msg_copy(i, j).start()

    wide[...] = jnp.zeros_like(wide)
    mixed[...] = jnp.zeros_like(mixed)
    cheb_a[...] = jnp.zeros_like(cheb_a)
    for o in range(nd):
        ones = (iota((nd, TB), 0) == o).astype(f32)
        wide[rows_t:rows_e, o * TB : (o + 1) * TB] = ones.astype(bf16)

    gj = iota((2 * glen, 2 * glen), 0)
    gi = iota((2 * glen, 2 * glen), 1)
    zi, zj = gi & (glen - 1), gj & (glen - 1)
    in_im, out_im = gi >= glen, gj >= glen
    half = glen // 2
    same = zi == zj
    mirror = (zi + zj == glen) & (zi != zj)
    even = zj <= half
    plain = in_im == out_im
    fold = jnp.where(
        even,
        jnp.where(plain & (same | mirror), 1.0, 0.0),
        jnp.where(
            plain,
            0.0,
            jnp.where(same, 1.0, 0.0) - jnp.where(mirror, 1.0, 0.0),
        )
        * jnp.where(out_im, -1.0, 1.0),
    ).astype(bf16)

    width_sq = (glen / 8.0) ** 2
    front = math.sqrt(1.5) / (2.0 * math.pi * width_sq) ** 0.75

    def signed(n):
        return jnp.where(n < half, n, n - glen).astype(f32)

    ky = signed(me_c * ys + iota((ys, glen), 0))
    kz = signed(iota((ys, glen), 1))
    kyz_sq = ky * ky + kz * kz

    def hat_block(i, first):
        kx = signed(me_r * xs + i)
        q = kx * kx + kyz_sq
        amp = jnp.where(q > 0, front * jnp.exp(q * (-0.25 / width_sq)), 0.0)
        damp = amp / jnp.maximum(q, 1.0)
        rows = pl.ds(pl.multiple_of(i * ys, ys), ys)
        at = pl.multiple_of((i - first) * ys, ys)
        waves = (kx, ky, kz)
        for v in range(2):
            for p in range(2):
                s = [spec[(p * 3 + a) * 2 + v, rows, :] for a in range(3)]
                along = (kx * s[0] + ky * s[1] + kz * s[2]) * damp
                for a in range(3):
                    pre[pl.ds((a * 2 + v) * part + at, ys), p * glen : (p + 1) * glen] = (
                        amp * s[a] - waves[a] * along
                    ).astype(bf16)
        return first

    per = part // ys
    for i in range(chunks):
        spec_copy(i).wait()
        lax.fori_loop(i * per, (i + 1) * per, hat_block, i * per)
        for k in range(6):
            folded = dot_nt(fold, pre[k * part : (k + 1) * part, :]).astype(bf16)
            for p in range(2):
                hat[
                    k * glen : (k + 1) * glen, p * xy + i * part : p * xy + (i + 1) * part
                ] = folded[p * glen : (p + 1) * glen, :]

    spectrum_copy.wait()
    for i, j in others[::-1]:
        msg_arrive(i, j)

    row_list = jnp.zeros((1, LANES), f32)
    col_list = jnp.zeros((1, LANES), f32)
    slot_rows = nb // 2 * cr
    for o in range(nd):
        got = inbox[o].astype(f32)
        row_list = row_list + got[tile_at : tile_at + 1]
        col_list = col_list + got[tile_at + 1 : tile_at + 2]
        for h in range(2):
            table[h, o * cr : (o + 1) * cr, :] = got[
                cells_at + h * cr : cells_at + (h + 1) * cr
            ]
        offs[:, o * TB : (o + 1) * TB] = got[6:9]
        first = 2 * o % 16
        base = 2 * o // 16 * 16
        for a in range(3):
            cheb_a[a, o, first : first + 2, :] = got[2 * a : 2 * a + 2]
            wide[a * nb + base : a * nb + base + 16, o * TB : (o + 1) * TB] = (
                cheb_a[a, o].astype(bf16)
            )
    tables = []
    for h in range(2):
        tables.append(jnp.transpose(table[h])[:, :slot_rows])
    for h in range(2):
        table[2 + h, :, :slot_rows] = tables[h]

    def kind_of(n):
        return jnp.where(n < rows_t, over(n, nb) * 2 + (n & 1), 6)

    def owner_of(n):
        return jnp.where(n < rows_t, over(n & (nb - 1), 2), n - rows_t)

    mix_rows = iota((rows_e, LANES), 0)
    mix_lanes = iota((rows_e, LANES), 1)
    all_rows = iota((LANES, LANES), 0)
    to = ((owner_of(mix_rows) + 1).astype(f32) == row_list).astype(f32).astype(bf16)
    frm = ((owner_of(all_rows) + 1).astype(f32) == col_list).astype(f32).astype(bf16)
    joined = jnp.where(
        (kind_of(mix_rows) == kind_of(mix_lanes)) & (mix_lanes < rows_e), dot_nt(to, frm), 0.0
    ).astype(bf16)
    mixer[:, :LANES] = joined
    mixer[:, LANES:] = joined

    def build_phi(o):
        lanes = slice(o * TB, (o + 1) * TB)
        q = iota((PERIOD, TB), 0).astype(f32) * (1.0 / PERIOD)
        co, si = [], []
        for a in range(3):
            turn = q * offs[a : a + 1, lanes]
            co.append(cos_turn(turn))
            si.append(cos_turn(turn - 0.25))
        flat_c, flat_s = [], []
        for y in range(PERIOD):
            cy, sy = co[1][y : y + 1], si[1][y : y + 1]
            flat_c.append(cy * co[0] - sy * si[0])
            flat_s.append(sy * co[0] + cy * si[0])
        line = iota((PERIOD, TB), 0)

        def ends(first, second):
            return jnp.where(line < HALF, first, pltpu.roll(second, HALF, 0))

        sides = [
            jnp.where(line == 0, pltpu.roll(flat_c[y], HALF, 0), flat_s[y]) for y in (0, HALF)
        ]
        real = jnp.concatenate([ends(flat_c[0], flat_c[HALF])] + flat_c[1:HALF], axis=0)
        imag = jnp.concatenate([ends(*sides)] + flat_s[1:HALF], axis=0)
        flip = co[2][HALF : HALF + 1]
        blocks = [jnp.concatenate([real, real * flip, imag, imag * flip], axis=0)]
        flat_c = jnp.concatenate(flat_c, axis=0)
        flat_s = jnp.concatenate(flat_s, axis=0)
        for z in range(1, HALF):
            cz, sz = co[2][z : z + 1], si[2][z : z + 1]
            blocks.append(
                jnp.concatenate([flat_c * cz - flat_s * sz, flat_s * cz + flat_c * sz], axis=0)
            )
        for g, block in enumerate(blocks):
            at = g * 2 * FLAT
            phi[at : at + 2 * FLAT, lanes] = block.astype(bf16)
            modes[lanes, at : at + 2 * FLAT] = jnp.transpose(block).astype(bf16)

    y_slab, z_slab = glen // n_row, glen // n_col
    scaled = 1.0 / glen

    def locate(r, c):
        o = r * n_col + c
        code = inbox[o].astype(f32)[9:10].astype(jnp.int32)
        slot = over(code, nd)
        holder = code & (nd - 1)
        row_at = holder * cr + over(slot, per_row)
        hot = (iota((slot_rows, TB), 0) == row_at).astype(f32).astype(bf16)
        at = pl.ds(pl.multiple_of(o * per_row, per_row), per_row)
        lists = jnp.concatenate(
            [table[2, at, :slot_rows], table[3, at, :slot_rows]], axis=0
        ).astype(bf16)
        found = dot(lists, hot)
        mine = iota((per_row, TB), 0) == (slot & (per_row - 1))
        high = jnp.sum(jnp.where(mine, found[:per_row], 0.0), axis=0, keepdims=True)
        low = jnp.sum(jnp.where(mine, found[per_row:], 0.0), axis=0, keepdims=True)
        cell = high.astype(jnp.int32) * 512 + low.astype(jnp.int32) + 256
        pos_x = over(cell, y_slab * z_slab)
        pos_y = over(holder, n_col) * y_slab + (over(cell, z_slab) & (y_slab - 1))
        pos_z = (holder & (n_col - 1)) * z_slab + (cell & (z_slab - 1))
        return [p.astype(f32) * scaled for p in (pos_x, pos_y, pos_z)]

    kx_col = (me_r * xs + iota((xs, 2 * TB), 0)).astype(f32)
    ky_col = (me_c * ys + iota((ys, 2 * TB), 0)).astype(f32)
    kz_col = iota((glen, 2 * TB), 0)

    def build_phase(pair, phase):
        spots = [locate(*place(i, j)) for i, j in pair]
        px, py, pz = (
            jnp.concatenate([spots[0][t], spots[1][t]], axis=1) for t in range(3)
        )
        turn = kx_col * px
        cx, nx = cos_turn(turn), cos_turn(turn + 0.25)
        turn = ky_col * py
        cy, ny = cos_turn(turn), cos_turn(turn + 0.25)
        for i in range(xs):
            a, b = cx[i : i + 1], nx[i : i + 1]
            phase[i * ys : (i + 1) * ys, :] = (a * cy - b * ny).astype(bf16)
            phase[xy + i * ys : xy + (i + 1) * ys, :] = (b * cy + a * ny).astype(bf16)
        return cos_turn(kz_col.astype(f32) * pz + jnp.where(kz_col > half, 0.25, 0.0))

    def far_copy(i, j):
        r, c = place(i, j)
        p = r * n_col + c
        q = i * n_col + j
        return remote(far_send.at[q], far_recv.at[me], far_ss.at[q], far_rs.at[me], r, c)

    def far_sums(pair, phase, tz):
        sums = dot(hat[...], phase[...])
        for k in range(6):
            line = jnp.sum(sums[k * glen : (k + 1) * glen] * tz, axis=0, keepdims=True)
            for t, (i, j) in enumerate(pair):
                half_line = line[:, t * TB : (t + 1) * TB]
                if i + j:
                    far_send[i * n_col + j, k : k + 1, :] = half_line
                else:
                    far_recv[me, k : k + 1, :] = half_line

    def far_start(some):
        for i, j in some:
            if i + j:
                far_copy(i, j).start()

    near = [cheb_coef[0] * noise_ref[a] for a in range(3)]
    own_rows = pl.ds(lax.rem(2 * me, 16), 2)
    scales = []

    def to_modes(m):
        rows = rows_e if m == 0 else rows_t
        sums = dot(wide[0:rows, :], modes[...])
        high = sums.astype(bf16)
        mixed[0:rows, :] = high
        mixed[LANES : LANES + rows, :] = (sums - high.astype(f32)).astype(bf16)

    def convolve(m):
        rows = rows_e if m == 0 else rows_t
        sums = dot(mixer[0:rows, :], mixed[...])
        turned = jnp.concatenate(
            [
                pltpu.roll(sums[0:rows_t, g * LANES : (g + 1) * LANES], FLAT, 1)
                for g in range(GROUPS)
            ],
            axis=1,
        )
        for a in range(3):
            total = spectrum[a : a + 1, :] * sums[a * nb : (a + 1) * nb]
            for b in range(3):
                if a != b:
                    e = PAIRS.index((min(a, b), max(a, b)))
                    total = total + spectrum[e : e + 1, :] * sums[b * nb : (b + 1) * nb]
                    total = total + spectrum[e + 3 : e + 4, :] * turned[b * nb : (b + 1) * nb]
            lattice[a * nb : (a + 1) * nb, :] = total.astype(bf16)
        if m == 0:
            for a in range(3):
                total = spectrum[9 + a : 10 + a, :] * sums[rows_t:rows_e]
                high = total.astype(bf16)
                at = rows_t + a * nd
                lattice[at : at + nd, :] = high
                lattice[at + 3 * nd : at + 4 * nd, :] = (total - high.astype(f32)).astype(bf16)

    def to_beads(m):
        if m == 0:
            out = dot(lattice[...], phi[...])
            energy = out[rows_t : rows_t + 3 * nd] + out[rows_t + 3 * nd :]
            top = jnp.zeros((3 * nd, TB), f32)
            owner = iota((3 * nd, TB), 0) & (nd - 1)
            for o in range(nd):
                top = jnp.maximum(
                    top, jnp.where(owner == o, energy[:, o * TB : (o + 1) * TB], 0.0)
                )
            top = jnp.max(jnp.max(top, axis=1, keepdims=True), axis=0, keepdims=True)
            scales.append(jnp.broadcast_to(1.0 / jnp.sqrt(top + 1e-06), (16, TB)))
        elif m < DEGREES - 1:
            out = dot(lattice[0:rows_t, :], phi[...])
        scale = scales[0]
        before = cheb_b if m % 2 == 0 else cheb_a
        if m < DEGREES - 1:
            line = iota((16, TB), 0)
            for o in range(nd):
                first = 2 * o % 16
                base = 2 * o // 16 * 16
                mine = (line >= first) & (line < first + 2)
                for a in range(3):
                    got = out[a * nb + base : a * nb + base + 16, o * TB : (o + 1) * TB]
                    got = jnp.where(mine, scale * got, 0.0)
                    if m > 0:
                        got = 2.0 * got - before[a, o]
                    before[a, o] = got
                    wide[a * nb + base : a * nb + base + 16, o * TB : (o + 1) * TB] = (
                        got.astype(bf16)
                    )
            for a in range(3):
                near[a] = near[a] + cheb_coef[m + 1] * before[a, me, own_rows, :]
        else:
            last[...] = dot(
                lattice[0:rows_t, :], phi[:, pl.ds(pl.multiple_of(me * TB, TB), TB)]
            )
            for a in range(3):
                got = 2.0 * (scale[0:2] * last[pl.ds(a * nb + 2 * me, 2), :])
                near[a] = near[a] + cheb_coef[m + 1] * (got - before[a, me, own_rows, :])

    stages = [
        functools.partial(stage, m)
        for m in range(DEGREES) for stage in (to_modes, convolve, to_beads)
    ]
    pairs = [peers[t : t + 2] for t in range(0, nd, 2)]
    phases = (phase_a, phase_b)
    built = -(-3 * len(pairs) // 8)
    sends = (len(pairs) - 3, len(pairs) - 1)
    held = []
    tz = build_phase(pairs[0], phase_a)
    for n, pair in enumerate(pairs):
        nxt = None
        if n + 1 < len(pairs):
            nxt = build_phase(pairs[n + 1], phases[(n + 1) % 2])
        if n >= built and False:
            stages.pop(0)()
        far_sums(pair, phases[n % 2], tz)
        tz = nxt
        held += pair
        if n in sends:
            far_start(held)
            held = []
        if n < built:
            for o in range(n * nd // built, (n + 1) * nd // built):
                build_phi(o)
    for stage in stages:
        stage()

    for i, j in others:
        msg_copy(i, j).wait_send()

    def far_arrive(i, j):
        r, c = place(i, j)
        p = r * n_col + c
        remote(far_send.at[0], far_recv.at[p], far_ss.at[0], far_rs.at[p], r, c).wait_recv()

    for i, j in others:
        far_arrive(i, j)
    for i, j in others:
        far_copy(i, j).wait_send()
    far = far_recv[0]
    for p in range(1, nd):
        far = far + far_recv[p]
    for a in range(3):
        out_ref[a] = near[a] + far[2 * a : 2 * a + 2, :]


def shared_device(noise_field, offsets, tile_list, send_cells, bead_slot, spectral):
    n_row = lax.axis_size("row")
    n_col = lax.axis_size("col")
    nd = n_row * n_col
    xs, ys, glen = spectral.shape[3:]
    slots = tile_list.shape[3]
    cap = send_cells.shape[2]
    xy = xs * ys
    cr = cap * nd // LANES
    msg_rows = -(-(12 + 2 * cr) // 16) * 16
    chunks = 4 if xy % 256 == 0 else 1
    dims = (n_row, n_col, slots, xs, ys, glen, cap)
    vmem = pl.BlockSpec(memory_space=pltpu.VMEM)
    hbm = pl.BlockSpec(memory_space=pl.ANY)
    dma = pltpu.SemaphoreType.DMA
    rows_t = 6 * nd
    spectrum = lattice_spectrum()
    return pl.pallas_call(
        functools.partial(shared_kernel, dims),
        out_shape=pltpu.VMEM(noise_field.shape, f32),
        in_specs=[hbm] * 7,
        out_specs=vmem,
        scratch_shapes=[
            pltpu.SMEM((2, slots), jnp.int32),
            pltpu.VMEM(noise_field.shape, f32),
            pltpu.VMEM(offsets.shape, jnp.int32),
            pltpu.VMEM((1, TB), jnp.int32),
            pltpu.VMEM((cap, nd), jnp.int32),
            pltpu.VMEM((12, xy, glen), f32),
            pltpu.VMEM((6 * (xy // chunks), 2 * glen), bf16),
            pltpu.VMEM((6 * glen, 2 * xy), bf16),
            pltpu.VMEM((2 * xy, 2 * TB), bf16),
            pltpu.VMEM((2 * xy, 2 * TB), bf16),
            pltpu.VMEM((MODES, nd * TB), bf16),
            pltpu.VMEM((nd * TB, MODES), bf16),
            pltpu.VMEM((rows_t + nd, nd * TB), bf16),
            pltpu.VMEM((3, nd, 16, TB), f32),
            pltpu.VMEM((3, nd, 16, TB), f32),
            pltpu.VMEM((rows_t + nd, 2 * LANES), bf16),
            pltpu.VMEM((2 * LANES, MODES), bf16),
            pltpu.VMEM((rows_t + 6 * nd, MODES), bf16),
            pltpu.VMEM((msg_rows, LANES), f32),
            pltpu.VMEM((msg_rows, LANES), bf16),
            pltpu.VMEM((nd, msg_rows, LANES), bf16),
            pltpu.VMEM((4, LANES, LANES), f32),
            pltpu.VMEM((3, nd * TB), f32),
            pltpu.VMEM(spectrum.shape, f32),
            pltpu.VMEM((rows_t, TB), f32),
            pltpu.VMEM((nd, 8, TB), f32),
            pltpu.VMEM((nd, 8, TB), f32),
            dma((5,)), dma((chunks,)), dma,
            dma((nd,)), dma((nd,)),
            dma((nd,)), dma((nd,)),
        ],
        compiler_params=pltpu.CompilerParams(
            collective_id=1, has_side_effects=True, vmem_limit_bytes=56 * 1024 * 1024
        ),
    )(
        tile_list.reshape(2, slots),
        noise_field,
        offsets,
        bead_slot.reshape(1, TB),
        send_cells.reshape(cap, nd),
        jnp.asarray(spectrum),
        spectral.reshape(12, xy, glen),
    )


def power_of_two(n):
    return n & (n - 1) == 0


def per_device(noise_field, offsets, tile_list, send_cells, bead_slot, spectral):
    n_row = lax.axis_size("row")
    n_col = lax.axis_size("col")
    nd = n_row * n_col
    xs, ys, glen = spectral.shape[3:]
    cap = send_cells.shape[2]
    fits = (
        8 <= nd <= 16
        and power_of_two(n_row)
        and power_of_two(n_col)
        and power_of_two(glen)
        and nd * tile_list.shape[3] <= LANES
        and cap % (LANES // nd) == 0
        and cap * nd <= 256
        and glen * (glen // n_row) * (glen // n_col) <= 1 << 17
        and ys % 16 == 0
    )
    run = shared_device if fits else spread_device
    return run(noise_field, offsets, tile_list, send_cells, bead_slot, spectral)


def solution(mesh):
    return jax.shard_map(
        per_device,
        mesh=mesh,
        in_specs=(
            P(None, None, ("groups", "row", "col")),
            P(None, ("groups", "row", "col")),
            P(("groups", "row"), "col", None, None),
            P(("groups", "row"), "col", None, None),
            P(("groups", "row", "col")),
            P(None, None, None, ("groups", "row"), "col", None),
        ),
        out_specs=P(None, None, ("groups", "row", "col")),
        check_vma=False,
    )
```

```python
import functools
import math

import jax
import jax.numpy as jnp
import ml_dtypes
import numpy as np
from jax import lax
from jax.experimental import pallas as pl
from jax.experimental.pallas import tpu as pltpu
from jax.sharding import PartitionSpec as P

TB = 128
LANES = 128
PERIOD = 8
DEGREES = 4

cheb_coef = (1.0, 0.45, -0.2, 0.12, -0.08)
kernel_range = 1.5

f32 = jnp.float32
bf16 = jnp.bfloat16


def iota(shape, dim):
    return lax.broadcasted_iota(jnp.int32, shape, dim)


def over(n, d):
    return lax.shift_right_logical(n, jnp.full(n.shape, d.bit_length() - 1, jnp.int32))


def dot(a, b):
    return jnp.dot(a, b, preferred_element_type=f32)


def dot_nt(a, b):
    return lax.dot_general(a, b, (((1,), (1,)), ((), ())), preferred_element_type=f32)


def cos_turn(turns):
    x = jnp.abs(turns - jnp.floor(turns) - 0.5) * 4.0 - 1.0
    x2 = x * x
    p = 0.00015148419
    for c in (-0.00467376557, 0.07968967928, -0.64596371106, 1.57079631847):
        p = p * x2 + c
    return p * x


def kernel(
    dims,
    tiles_ref, noise_ref, off_ref, slot_ref, cells_ref, spec_hbm,
    out_ref,
    spec, pre, hat, phase, ang, wang, tabf, tab, kmat,
    a_send, a_recv, b_send, row_b, col_b,
    e_send, e_recv, y_send, y_recv, far_send, far_recv,
    cur, prev, acc, scale,
    spec_sem, a_ss, a_rs, b_ss, b_rs, e_ss, e_rs, y_ss, y_rs, far_ss, far_rs,
):
    n_row, n_col, slots, xs, ys, glen, cap = dims
    nd = n_row * n_col
    xy = xs * ys
    cr = cap * nd // LANES
    kq = tab.shape[0]
    beads = n_col * TB
    me_r = lax.axis_index("row")
    me_c = lax.axis_index("col")
    me = me_r * n_col + me_c
    chunks = spec_sem.shape[0]
    part = xy // chunks
    per_row = LANES // nd

    def spec_copy(i):
        rows = pl.ds(i * part, part)
        return pltpu.make_async_copy(
            spec_hbm.at[:, rows, :], spec.at[:, rows, :], spec_sem.at[i]
        )

    for i in range(chunks):
        spec_copy(i).start()

    straight = nd <= 32
    if straight:
        rows_of = [me_r] + [lax.rem(me_r + d, n_row) for d in range(1, n_row)]
        cols_of = [me_c] + [lax.rem(me_c + d, n_col) for d in range(1, n_col)]
        order = sorted(
            [(i, j) for i in range(n_row) for j in range(n_col) if i + j],
            key=lambda t: (abs(t[1] - n_col // 2), abs(t[0] - n_row // 2)),
        )

    def each(body):
        if straight:
            for i, j in order:
                body(rows_of[i], cols_of[j])
            return

        def turn(d, carry):
            body(lax.rem(me_r + d // n_col, n_row), lax.rem(me_c + lax.rem(d, n_col), n_col))
            return carry

        lax.fori_loop(1, nd, turn, 0)

    def each_row(body):
        if straight:
            for d in range(1, n_row):
                body(rows_of[d])
        else:
            lax.fori_loop(1, n_row, lambda d, t: (body(lax.rem(me_r + d, n_row)), t)[1], 0)

    def each_col(body):
        if straight:
            for d in range(1, n_col):
                body(cols_of[d])
        else:
            lax.fori_loop(1, n_col, lambda d, t: (body(lax.rem(me_c + d, n_col)), t)[1], 0)

    barrier = pltpu.get_barrier_semaphore()

    def greet(r, c):
        pl.semaphore_signal(
            barrier, inc=1, device_id={"row": r, "col": c},
            device_id_type=pl.DeviceIdType.MESH,
        )

    each(greet)

    def remote(src, dst, ss, rs, r, c):
        return pltpu.make_async_remote_copy(
            src_ref=src, dst_ref=dst, send_sem=ss, recv_sem=rs,
            device_id={"row": r, "col": c}, device_id_type=pl.DeviceIdType.MESH,
        )

    def packed_cells():
        flat = cells_ref[...].astype(f32)
        if per_row == 1:
            return flat
        spread = (iota((nd, LANES), 1) & (nd - 1)) == iota((nd, LANES), 0)
        wide = jnp.dot(
            flat, spread.astype(f32), precision=lax.Precision.HIGHEST,
            preferred_element_type=f32,
        )
        mine = over(iota((cap, LANES), 1), nd) == (iota((cap, LANES), 0) & (per_row - 1))
        return jnp.sum(jnp.where(mine, wide, 0.0).reshape(cr, per_row, LANES), axis=1)

    a_send[0:1, :] = slot_ref[...].astype(f32)
    cells = packed_cells()
    a_send[1 : 1 + cr, :] = cells
    a_recv[me, 0:1, :] = slot_ref[...].astype(f32)
    a_recv[me, 1 : 1 + cr, :] = cells
    own_noise = jnp.concatenate([noise_ref[0], noise_ref[1], noise_ref[2]], axis=1)
    off = off_ref[...].astype(f32)
    own_off = jnp.concatenate([off[0:1], off[1:2], off[2:3]], axis=1)
    b_send[0:2, :] = own_noise
    b_send[2:3, :] = own_off
    row_b[me_c, 0:2, :] = own_noise
    row_b[me_c, 2:3, :] = own_off
    col_b[me_r, 0:2, :] = own_noise
    col_b[me_r, 2:3, :] = own_off
    tabf[...] = jnp.zeros_like(tabf)

    pl.semaphore_wait(barrier, nd - 1)

    def b_row_copy(c):
        return remote(b_send, row_b.at[me_c], b_ss.at[c], b_rs.at[me_c], me_r, c)

    def b_col_copy(r):
        return remote(
            b_send, col_b.at[me_r], b_ss.at[n_col + r], b_rs.at[n_col + me_r], r, me_c
        )

    each_col(lambda c: b_row_copy(c).start())
    each_row(lambda r: b_col_copy(r).start())

    def a_copy(r, c):
        p = r * n_col + c
        return remote(a_send, a_recv.at[me], a_ss.at[p], a_rs.at[me], r, c)

    each(lambda r, c: a_copy(r, c).start())

    gi = iota((2 * glen, 2 * glen), 0)
    gj = iota((2 * glen, 2 * glen), 1)
    zi, zj = gi & (glen - 1), gj & (glen - 1)
    in_im, out_im = gi >= glen, gj >= glen
    half = glen // 2
    same = zi == zj
    mirror = (zi + zj == glen) & (zi != zj)
    even = zj <= half
    plain = in_im == out_im
    fold = jnp.where(
        even,
        jnp.where(plain & (same | mirror), 1.0, 0.0),
        jnp.where(
            plain,
            0.0,
            jnp.where(same, 1.0, 0.0) - jnp.where(mirror, 1.0, 0.0),
        )
        * jnp.where(out_im, -1.0, 1.0),
    ).astype(bf16)

    width_sq = (glen / 8.0) ** 2
    front = math.sqrt(1.5) / (2.0 * math.pi * width_sq) ** 0.75
    def signed(n):
        return jnp.where(n < half, n, n - glen).astype(f32)

    ky = signed(me_c * ys + iota((ys, glen), 0))
    kz = signed(iota((ys, glen), 1))
    kyz_sq = ky * ky + kz * kz

    def hat_block(i, first):
        kx = signed(me_r * xs + i)
        q = kx * kx + kyz_sq
        amp = jnp.where(q > 0, front * jnp.exp(q * (-0.25 / width_sq)), 0.0)
        damp = amp / jnp.maximum(q, 1.0)
        rows = pl.ds(pl.multiple_of(i * ys, ys), ys)
        at = pl.multiple_of((i - first) * ys, ys)
        waves = (kx, ky, kz)
        for v in range(2):
            for p in range(2):
                s = [spec[(p * 3 + a) * 2 + v, rows, :] for a in range(3)]
                along = (kx * s[0] + ky * s[1] + kz * s[2]) * damp
                for a in range(3):
                    pre[pl.ds((a * 2 + v) * part + at, ys), p * glen : (p + 1) * glen] = (
                        amp * s[a] - waves[a] * along
                    ).astype(bf16)
        return first

    per = part // ys
    for i in range(chunks):
        spec_copy(i).wait()
        lax.fori_loop(i * per, (i + 1) * per, hat_block, i * per)
        folded = dot(pre[...], fold)
        for k in range(6):
            for p in range(2):
                hat[
                    p * xy + i * part : p * xy + (i + 1) * part, k * glen : (k + 1) * glen
                ] = folded[
                    k * part : (k + 1) * part, p * glen : (p + 1) * glen
                ].astype(bf16)

    def b_col_arrive(r):
        remote(b_send, col_b.at[r], b_ss.at[n_col + r], b_rs.at[n_col + r], r, me_c).wait_recv()

    def b_row_arrive(c):
        remote(b_send, row_b.at[c], b_ss.at[c], b_rs.at[c], me_r, c).wait_recv()

    each_row(b_col_arrive)
    each_col(b_row_arrive)

    eye = (iota((TB, TB), 0) == iota((TB, TB), 1)).astype(f32)
    ones = jnp.ones((TB, TB), bf16)
    scale_sq = kernel_range * kernel_range

    def pick(values, into, s):
        tr = tiles_ref[0, s]
        return tuple(
            into[i] + values * jnp.where(tr == i, 1.0, 0.0).astype(f32) for i in range(n_col)
        )

    def build(s, energies):
        tr = jnp.maximum(tiles_ref[0, s], 0)
        tc = jnp.maximum(tiles_ref[1, s], 0)
        row_off = row_b[tr][2:3, :]
        col_off = col_b[tc][2:3, :]
        disp = []
        for a in range(3):
            lanes = slice(a * TB, (a + 1) * TB)
            rp = dot((eye * row_off[:, lanes]).astype(bf16), ones)
            gap = (rp - col_off[:, lanes]).astype(jnp.int32) + PERIOD // 2
            disp.append(((gap & (PERIOD - 1)) - PERIOD // 2).astype(f32))
        squares = disp[0] * disp[0] + disp[1] * disp[1] + disp[2] * disp[2]
        envelope = jnp.exp(squares * (-0.5 / scale_sq)) / scale_sq
        third = squares / 3.0
        for a in range(3):
            for b in range(a, 3):
                element = disp[a] * disp[b]
                if a == b:
                    element = element - third
                entry = (envelope * element).astype(bf16)
                kmat[s, a * TB : (a + 1) * TB, b * TB : (b + 1) * TB] = entry
                if a != b:
                    kmat[s, b * TB : (b + 1) * TB, a * TB : (a + 1) * TB] = entry
        wide = kmat[s].astype(f32)
        sq = wide * wide
        high = sq.astype(bf16)
        low = (sq - high.astype(f32)).astype(bf16)
        one_row = jnp.ones((8, 3 * TB), bf16)
        energy = dot_nt(one_row, high) + dot_nt(one_row, low)
        return pick(energy[0:1], energies, s)

    energies = lax.fori_loop(
        0, slots, build, tuple(jnp.zeros((1, 3 * TB), f32) for _ in range(n_col)),
        unroll=slots <= 4,
    )
    for i in range(n_col):
        e_send[i : i + 1, :] = energies[i]
        e_recv[me, i : i + 1, :] = energies[i]

    def e_copy(r, c):
        p = r * n_col + c
        return remote(e_send, e_recv.at[me], e_ss.at[p], e_rs.at[me], r, c)

    for r in range(n_row):
        cur[r] = col_b[r, 0:2, :]
    acc[...] = cheb_coef[0] * own_noise

    def a_arrive(r, c):
        p = r * n_col + c
        remote(a_send, a_recv.at[p], a_ss.at[p], a_rs.at[p], r, c).wait_recv()

    def prepare_table():
        each(a_arrive)

        def spread(h, carry):
            tabf[pl.ds(h * cr, cr), :] = a_recv[h, 1 : 1 + cr, :]
            return carry

        lax.fori_loop(0, nd, spread, 0)
        cell = tabf[...].astype(jnp.int32)
        y_slab, z_slab = glen // n_row, glen // n_col
        holder = over(iota((kq, LANES), 0), cr)
        pos_x = over(cell, y_slab * z_slab)
        pos_y = over(holder, n_col) * y_slab + (over(cell, z_slab) & (y_slab - 1))
        pos_z = (holder & (n_col - 1)) * z_slab + (cell & (z_slab - 1))
        for at, pos in enumerate((pos_x, pos_y, pos_z)):
            tab[:, at * LANES : (at + 1) * LANES] = pos.astype(f32).astype(bf16)

    x_step = LANES // ys
    lane = iota((LANES, LANES), 1)
    scaled = 1.0 / glen
    along_x = ((me_r * xs + over(lane, ys)).astype(f32) * scaled).astype(bf16)
    along_y = ((me_c * ys + (lane & (ys - 1))).astype(f32) * scaled).astype(bf16)
    wang[...] = jnp.zeros_like(wang)
    wang[0:LANES, 0:LANES] = along_x
    wang[LANES : 2 * LANES, 0:LANES] = along_y
    wang[0:LANES, LANES : 2 * LANES] = jnp.full((LANES, LANES), x_step * scaled, bf16)
    wang[2 * LANES :, 2 * LANES :] = (lane.astype(f32) * scaled).astype(bf16)
    rep = over(iota((8, 6 * glen), 1), glen) == iota((8, 6 * glen), 0)
    rep = rep.astype(f32).astype(bf16)
    wide_ones = jnp.ones((TB, kq), bf16)
    step_rows = 32

    def far_copy(i, c):
        return remote(
            far_send.at[i * n_col + c], far_recv.at[me],
            far_ss.at[i * n_col + c], far_rs.at[me], i, c,
        )

    def far_chunk(i, carry):
        spots = jnp.concatenate(
            [eye * a_recv[i * n_col + c, 0:1, :] for c in range(n_col)], axis=0
        ).astype(bf16)
        code = dot(spots, wide_ones).astype(jnp.int32)
        s_idx = over(code, nd)
        row_idx = (code & (nd - 1)) * cr + over(s_idx, per_row)
        hot = (row_idx == iota((beads, kq), 1)).astype(f32).astype(bf16)
        found = dot(hot, tab[...])
        owner_of = i * n_col + over(iota((beads, LANES), 0), TB)
        want = (s_idx[:, :LANES] & (per_row - 1)) * nd + owner_of
        keep = want == iota((beads, LANES), 1)
        places = jnp.concatenate(
            [jnp.where(keep, found[:, k * LANES : (k + 1) * LANES], 0.0) for k in range(3)],
            axis=1,
        ).astype(bf16)
        ang[...] = dot(places, wang[...])

        def phase_block(j, carry):
            rows = pl.ds(pl.multiple_of(j * step_rows, step_rows), step_rows)
            at_lane = iota((step_rows, LANES), 1)
            start = ang[rows, 0:LANES]
            co = cos_turn(start)
            ns = cos_turn(start + 0.25)
            turn_x = cos_turn(
                ang[rows, LANES : 2 * LANES] - jnp.where(at_lane == 1, 0.25, 0.0)
            )
            cd = jnp.broadcast_to(turn_x[:, 0:1], co.shape)
            sd = jnp.broadcast_to(turn_x[:, 1:2], co.shape)
            ang[rows, 2 * LANES :] = cos_turn(
                ang[rows, 2 * LANES :] + jnp.where(at_lane > half, 0.25, 0.0)
            )
            for g in range(xy // LANES):
                phase[rows, g * LANES : (g + 1) * LANES] = co.astype(bf16)
                phase[rows, xy + g * LANES : xy + (g + 1) * LANES] = ns.astype(bf16)
                co, ns = co * cd + ns * sd, ns * cd - co * sd
            return carry

        lax.fori_loop(0, beads // step_rows, phase_block, 0)
        sums = dot(phase[...], hat[...])
        tz = ang[:, 2 * LANES :]
        weighted = jnp.concatenate(
            [(sums[:, k * glen : (k + 1) * glen] * tz).astype(bf16) for k in range(6)], axis=1
        )
        res = dot_nt(rep, weighted)
        for c in range(n_col):
            owner = i * n_col + c
            far_send[owner] = res[:, c * TB : (c + 1) * TB]

            @pl.when(owner == me)
            def _():
                far_recv[me] = res[:, c * TB : (c + 1) * TB]

            @pl.when(owner != me)
            def _():
                far_copy(i, c).start()

        return carry

    def y_copy(r, c, par):
        p = r * n_col + c
        return remote(
            y_send.at[par, c], y_recv.at[par, me], y_ss.at[par, p], y_rs.at[par, me], r, c
        )

    def y_arrive(r, c, par):
        p = r * n_col + c
        remote(
            y_send.at[par, 0], y_recv.at[par, p], y_ss.at[par, p], y_rs.at[par, p], r, c
        ).wait_recv()

    each(lambda r, c: e_copy(r, c).start())

    def degree_step(m, carry):
        par = lax.rem(m, 2)

        def apply(s, sums):
            tc = jnp.maximum(tiles_ref[1, s], 0)
            w = cur[tc]
            w = jnp.concatenate([w, jnp.zeros((6, 3 * TB), f32)], axis=0).astype(bf16)
            return pick(dot_nt(w, kmat[s])[0:2], sums, s)

        sums = lax.fori_loop(
            0, slots, apply, tuple(jnp.zeros((2, 3 * TB), f32) for _ in range(n_col)),
            unroll=slots <= 4,
        )
        own = jnp.zeros((2, 3 * TB), f32)
        for i in range(n_col):
            y_send[par, i] = sums[i]
            own = own + sums[i] * jnp.where(me_c == i, 1.0, 0.0).astype(f32)
        y_recv[par, me] = own
        each(lambda r, c: y_copy(r, c, par).start())

        @pl.when(m == 0)
        def _():
            prepare_table()

        lax.fori_loop(m * n_row // DEGREES, (m + 1) * n_row // DEGREES, far_chunk, 0)

        @pl.when(m == 0)
        def _():
            def e_arrive(r, c):
                p = r * n_col + c
                remote(e_send, e_recv.at[p], e_ss.at[p], e_rs.at[p], r, c).wait_recv()

            each(e_arrive)
            top = jnp.zeros((n_col, 3 * TB), f32)
            for r in range(n_row):
                total = e_recv[r * n_col]
                for c in range(1, n_col):
                    total = total + e_recv[r * n_col + c]
                top = jnp.maximum(top, total)
            largest = jnp.max(jnp.max(top, axis=1, keepdims=True), axis=0, keepdims=True)
            scale[...] = jnp.broadcast_to(1.0 / jnp.sqrt(largest + 1e-06), scale.shape)

        each(lambda r, c: y_arrive(r, c, par))
        each(lambda r, c: y_copy(r, c, par).wait_send())
        first = jnp.where(m == 0, 1.0, 0.0).astype(f32)
        coef = jnp.where(
            m == 0, cheb_coef[1],
            jnp.where(m == 1, cheb_coef[2], jnp.where(m == 2, cheb_coef[3], cheb_coef[4])),
        ).astype(f32)
        sc = jnp.concatenate([scale[0:2, :]] * 3, axis=1)

        def advance(r, carry):
            total = y_recv[par, r * n_col]
            for c in range(1, n_col):
                total = total + y_recv[par, r * n_col + c]
            now = sc * total
            following = jnp.where(m == 0, now, 2.0 * now - prev[r])
            prev[r] = cur[r]
            cur[r] = following
            return carry

        lax.fori_loop(0, n_row, advance, 0)
        acc[...] = acc[...] + coef * cur[me_r]
        return carry

    prev[...] = jnp.zeros_like(prev)
    lax.fori_loop(0, DEGREES, degree_step, 0)

    each_row(lambda r: b_col_copy(r).wait_send())
    each_col(lambda c: b_row_copy(c).wait_send())
    each(lambda r, c: a_copy(r, c).wait_send())
    each(lambda r, c: e_copy(r, c).wait_send())

    def far_arrive(r, c):
        p = r * n_col + c
        remote(
            far_send.at[p], far_recv.at[p], far_ss.at[p], far_rs.at[p], r, c
        ).wait_recv()

    each(far_arrive)
    each(lambda r, c: far_copy(r, c).wait_send())
    far = lax.fori_loop(
        1, nd, lambda p, t: t + far_recv[p], far_recv[0]
    )
    near = acc[...]
    for a in range(3):
        out_ref[a] = near[:, a * TB : (a + 1) * TB] + far[2 * a : 2 * a + 2, :]


def spread_device(noise_field, offsets, tile_list, send_cells, bead_slot, spectral):
    n_row = lax.axis_size("row")
    n_col = lax.axis_size("col")
    nd = n_row * n_col
    xs, ys, glen = spectral.shape[3:]
    slots = tile_list.shape[3]
    cap = send_cells.shape[2]
    cr = cap * nd // LANES
    xy = xs * ys
    kq = max(LANES, nd * cr)
    beads = n_col * TB
    a_rows = -(-(1 + cr) // 4) * 4
    chunks = 4 if xy % 256 == 0 else 1
    dims = (n_row, n_col, slots, xs, ys, glen, cap)
    vmem = pl.BlockSpec(memory_space=pltpu.VMEM)
    dma = pltpu.SemaphoreType.DMA
    wide = 3 * TB
    return pl.pallas_call(
        functools.partial(kernel, dims),
        out_shape=jax.ShapeDtypeStruct(noise_field.shape, f32),
        in_specs=[pl.BlockSpec(memory_space=pltpu.SMEM), vmem, vmem, vmem, vmem,
                  pl.BlockSpec(memory_space=pl.ANY)],
        out_specs=vmem,
        scratch_shapes=[
            pltpu.VMEM((12, xy, glen), f32),
            pltpu.VMEM((6 * (xy // chunks), 2 * glen), bf16),
            pltpu.VMEM((2 * xy, 6 * glen), bf16),
            pltpu.VMEM((beads, 2 * xy), bf16),
            pltpu.VMEM((beads, 3 * LANES), f32),
            pltpu.VMEM((3 * LANES, 3 * LANES), bf16),
            pltpu.VMEM((kq, LANES), f32),
            pltpu.VMEM((kq, 3 * LANES), bf16),
            pltpu.VMEM((slots, wide, wide), bf16),
            pltpu.VMEM((a_rows, LANES), f32),
            pltpu.VMEM((nd, a_rows, LANES), f32),
            pltpu.VMEM((4, wide), f32),
            pltpu.VMEM((n_col, 4, wide), f32),
            pltpu.VMEM((n_row, 4, wide), f32),
            pltpu.VMEM((n_col, wide), f32),
            pltpu.VMEM((nd, n_col, wide), f32),
            pltpu.VMEM((2, n_col, 2, wide), f32),
            pltpu.VMEM((2, nd, 2, wide), f32),
            pltpu.VMEM((nd, 8, TB), f32),
            pltpu.VMEM((nd, 8, TB), f32),
            pltpu.VMEM((n_row, 2, wide), f32),
            pltpu.VMEM((n_row, 2, wide), f32),
            pltpu.VMEM((2, wide), f32),
            pltpu.VMEM((8, LANES), f32),
            dma((chunks,)),
            dma((nd,)), dma((nd,)),
            dma((n_row + n_col,)), dma((n_row + n_col,)),
            dma((nd,)), dma((nd,)),
            dma((2, nd)), dma((2, nd)),
            dma((nd,)), dma((nd,)),
        ],
        compiler_params=pltpu.CompilerParams(
            collective_id=0, has_side_effects=True, vmem_limit_bytes=56 * 1024 * 1024
        ),
    )(
        tile_list.reshape(2, slots),
        noise_field,
        offsets,
        bead_slot.reshape(1, TB),
        send_cells.reshape(cap, nd),
        spectral.reshape(12, xy, glen),
    )


HALF = PERIOD // 2
FLAT = PERIOD * PERIOD
GROUPS = HALF
MODES = PERIOD**3
PAIRS = ((0, 0), (1, 1), (2, 2), (0, 1), (0, 2), (1, 2))


def lattice_spectrum():
    code = np.arange(PERIOD**3)
    site = np.stack([code // FLAT, code // PERIOD % PERIOD, code % PERIOD])
    disp = (site + PERIOD // 2) % PERIOD - PERIOD // 2
    d = disp.astype(np.float32)
    squares = d[0] * d[0] + d[1] * d[1] + d[2] * d[2]
    scale_sq = np.float32(kernel_range * kernel_range)
    envelope = np.exp(squares * np.float32(-0.5 / scale_sq)) / scale_sq
    table = np.zeros((3, 3, PERIOD**3))
    for a, b in PAIRS:
        element = d[a] * d[b]
        if a == b:
            element = element - squares / np.float32(3.0)
        table[a, b] = (envelope * element).astype(ml_dtypes.bfloat16).astype(np.float64)
        table[b, a] = table[a, b]
    energy = (table * table).sum(axis=1)
    ends = [(x, y) for y in (0, HALF) for x in range(HALF)]
    middle = [(x, y) for y in range(1, HALF) for x in range(PERIOD)]
    turned = [(HALF if x == 0 else x, y) for x, y in ends]
    modes = []
    for part, lead in enumerate((ends, turned)):
        modes += [(x, y, z, part) for z in (0, HALF) for x, y in lead + middle]
    for z in range(1, HALF):
        modes += [(n % PERIOD, n // PERIOD, z, p) for p in range(2) for n in range(FLAT)]
    wave = np.array(modes)
    angle = 2.0 * np.pi / PERIOD * ((wave[:, :3] @ site) % PERIOD)
    alone = (wave[:, :3] % HALF == 0).all(axis=1)
    weight = np.where(alone, 1.0, 2.0) / PERIOD**3
    turn = np.where(wave[:, 3] == 0, 1.0, -1.0)
    rows = [weight * (np.cos(angle) @ table[p]) for p in PAIRS]
    rows += [-turn * weight * (np.sin(angle) @ table[p]) for p in PAIRS[3:]]
    rows += [weight * (np.cos(angle) @ energy[a]) for a in range(3)]
    rows += [np.zeros(MODES)] * (-len(rows) % 8)
    return np.stack(rows).astype(np.float32)


def shared_kernel(
    dims,
    tiles_hbm, noise_hbm, off_hbm, slot_hbm, cells_hbm, spectrum_hbm, spec_hbm,
    out_ref,
    tiles_ref, noise_ref, off_ref, slot_ref, cells_ref,
    spec, pre, hat, phase_a, phase_b, phi, modes, wide, cheb_a, cheb_b, mixer, mixed, lattice,
    msg_f, msg, inbox, table, offs, spectrum, last,
    far_send, far_recv,
    load_sem, spec_sem, spectrum_sem, m_ss, m_rs, far_ss, far_rs,
):
    n_row, n_col, slots, xs, ys, glen, cap = dims
    nd = n_row * n_col
    xy = xs * ys
    per_row = LANES // nd
    cr = cap // per_row
    cells_at = 10
    tile_at = cells_at + 2 * cr
    beads = nd * TB
    me_r = lax.axis_index("row")
    me_c = lax.axis_index("col")
    me = me_r * n_col + me_c
    chunks = spec_sem.shape[0]
    part = xy // chunks
    nb = 2 * nd
    rows_t = 3 * nb
    rows_e = rows_t + nd

    def spec_copy(i):
        rows = pl.ds(i * part, part)
        return pltpu.make_async_copy(
            spec_hbm.at[:, rows, :], spec.at[:, rows, :], spec_sem.at[i]
        )

    loads = [
        pltpu.make_async_copy(src, dst, load_sem.at[k])
        for k, (src, dst) in enumerate((
            (cells_hbm, cells_ref), (tiles_hbm, tiles_ref), (noise_hbm, noise_ref),
            (off_hbm, off_ref), (slot_hbm, slot_ref),
        ))
    ]

    peers = sorted(
        [(i, j) for i in range(n_row) for j in range(n_col)], key=lambda t: (-t[1], -t[0])
    )
    others = peers[:-1]

    def place(i, j):
        return jnp.bitwise_xor(me_r, i), jnp.bitwise_xor(me_c, j)

    barrier = pltpu.get_barrier_semaphore()
    for i, j in others:
        r, c = place(i, j)
        pl.semaphore_signal(
            barrier, inc=1, device_id={"row": r, "col": c},
            device_id_type=pl.DeviceIdType.MESH,
        )
    for load in loads:
        load.start()
    for i in range(chunks):
        spec_copy(i).start()
    spectrum_copy = pltpu.make_async_copy(spectrum_hbm, spectrum, spectrum_sem)
    spectrum_copy.start()

    def remote(src, dst, ss, rs, r, c):
        return pltpu.make_async_remote_copy(
            src_ref=src, dst_ref=dst, send_sem=ss, recv_sem=rs,
            device_id={"row": r, "col": c}, device_id_type=pl.DeviceIdType.MESH,
        )

    for load in loads:
        load.wait()
    for a in range(3):
        msg_f[2 * a : 2 * a + 2, :] = noise_ref[a]
    msg_f[6:9, :] = off_ref[...].astype(f32)
    msg_f[9:10, :] = slot_ref[...].astype(f32)
    spread = over(iota((nd, LANES), 1), per_row) == iota((nd, LANES), 0)
    spread = spread.astype(f32).astype(bf16)
    keep = (iota((cap, LANES), 1) & (per_row - 1)) == (iota((cap, LANES), 0) & (per_row - 1))
    cells = cells_ref[...]
    for h, half_cell in enumerate((over(cells, 512), (cells & 511) - 256)):
        out = dot(half_cell.astype(f32).astype(bf16), spread)
        out = jnp.sum(jnp.where(keep, out, 0.0).reshape(cr, per_row, LANES), axis=1)
        msg_f[cells_at + h * cr : cells_at + (h + 1) * cr, :] = out
    lane_row = iota((1, LANES), 1)
    row_list = jnp.zeros((1, LANES), jnp.int32)
    col_list = jnp.zeros((1, LANES), jnp.int32)
    for s in range(slots):
        here = lane_row == me * slots + s
        tr, tc = tiles_ref[0, s], tiles_ref[1, s]
        row_list = jnp.where(
            here & (jnp.full((1, LANES), tr) >= 0), me_r * n_col + tr + 1, row_list
        )
        col_list = jnp.where(here, tc * n_col + me_c + 1, col_list)
    msg_f[tile_at : tile_at + 1, :] = row_list.astype(f32)
    msg_f[tile_at + 1 : tile_at + 2, :] = col_list.astype(f32)
    if tile_at + 2 < msg_f.shape[0]:
        msg_f[tile_at + 2 :, :] = jnp.zeros((msg_f.shape[0] - tile_at - 2, LANES), f32)
    msg[...] = msg_f[...].astype(bf16)
    inbox[me] = msg_f[...].astype(bf16)

    pl.semaphore_wait(barrier, nd - 1)

    def msg_copy(i, j):
        r, c = place(i, j)
        p = i * n_col + j
        return remote(msg, inbox.at[me], m_ss.at[p], m_rs.at[me], r, c)

    def msg_arrive(i, j):
        r, c = place(i, j)
        p = r * n_col + c
        remote(msg, inbox.at[p], m_ss.at[0], m_rs.at[p], r, c).wait_recv()

    for i, j in others:
        msg_copy(i, j).start()

    wide[...] = jnp.zeros_like(wide)
    mixed[...] = jnp.zeros_like(mixed)
    cheb_a[...] = jnp.zeros_like(cheb_a)
    for o in range(nd):
        ones = (iota((nd, TB), 0) == o).astype(f32)
        wide[rows_t:rows_e, o * TB : (o + 1) * TB] = ones.astype(bf16)

    gj = iota((2 * glen, 2 * glen), 0)
    gi = iota((2 * glen, 2 * glen), 1)
    zi, zj = gi & (glen - 1), gj & (glen - 1)
    in_im, out_im = gi >= glen, gj >= glen
    half = glen // 2
    same = zi == zj
    mirror = (zi + zj == glen) & (zi != zj)
    even = zj <= half
    plain = in_im == out_im
    fold = jnp.where(
        even,
        jnp.where(plain & (same | mirror), 1.0, 0.0),
        jnp.where(
            plain,
            0.0,
            jnp.where(same, 1.0, 0.0) - jnp.where(mirror, 1.0, 0.0),
        )
        * jnp.where(out_im, -1.0, 1.0),
    ).astype(bf16)

    width_sq = (glen / 8.0) ** 2
    front = math.sqrt(1.5) / (2.0 * math.pi * width_sq) ** 0.75

    def signed(n):
        return jnp.where(n < half, n, n - glen).astype(f32)

    ky = signed(me_c * ys + iota((ys, glen), 0))
    kz = signed(iota((ys, glen), 1))
    kyz_sq = ky * ky + kz * kz

    def hat_block(i, first):
        kx = signed(me_r * xs + i)
        q = kx * kx + kyz_sq
        amp = jnp.where(q > 0, front * jnp.exp(q * (-0.25 / width_sq)), 0.0)
        damp = amp / jnp.maximum(q, 1.0)
        rows = pl.ds(pl.multiple_of(i * ys, ys), ys)
        at = pl.multiple_of((i - first) * ys, ys)
        waves = (kx, ky, kz)
        for v in range(2):
            for p in range(2):
                s = [spec[(p * 3 + a) * 2 + v, rows, :] for a in range(3)]
                along = (kx * s[0] + ky * s[1] + kz * s[2]) * damp
                for a in range(3):
                    pre[pl.ds((a * 2 + v) * part + at, ys), p * glen : (p + 1) * glen] = (
                        amp * s[a] - waves[a] * along
                    ).astype(bf16)
        return first

    per = part // ys
    for i in range(chunks):
        spec_copy(i).wait()
        lax.fori_loop(i * per, (i + 1) * per, hat_block, i * per)
        for k in range(6):
            folded = dot_nt(fold, pre[k * part : (k + 1) * part, :]).astype(bf16)
            for p in range(2):
                hat[
                    k * glen : (k + 1) * glen, p * xy + i * part : p * xy + (i + 1) * part
                ] = folded[p * glen : (p + 1) * glen, :]

    spectrum_copy.wait()
    for i, j in others[::-1]:
        msg_arrive(i, j)

    row_list = jnp.zeros((1, LANES), f32)
    col_list = jnp.zeros((1, LANES), f32)
    slot_rows = nb // 2 * cr
    for o in range(nd):
        got = inbox[o].astype(f32)
        row_list = row_list + got[tile_at : tile_at + 1]
        col_list = col_list + got[tile_at + 1 : tile_at + 2]
        for h in range(2):
            table[h, o * cr : (o + 1) * cr, :] = got[
                cells_at + h * cr : cells_at + (h + 1) * cr
            ]
        offs[:, o * TB : (o + 1) * TB] = got[6:9]
        first = 2 * o % 16
        base = 2 * o // 16 * 16
        for a in range(3):
            cheb_a[a, o, first : first + 2, :] = got[2 * a : 2 * a + 2]
            wide[a * nb + base : a * nb + base + 16, o * TB : (o + 1) * TB] = (
                cheb_a[a, o].astype(bf16)
            )
    tables = []
    for h in range(2):
        tables.append(jnp.transpose(table[h])[:, :slot_rows])
    for h in range(2):
        table[2 + h, :, :slot_rows] = tables[h]

    def kind_of(n):
        return jnp.where(n < rows_t, over(n, nb) * 2 + (n & 1), 6)

    def owner_of(n):
        return jnp.where(n < rows_t, over(n & (nb - 1), 2), n - rows_t)

    mix_rows = iota((rows_e, LANES), 0)
    mix_lanes = iota((rows_e, LANES), 1)
    all_rows = iota((LANES, LANES), 0)
    to = ((owner_of(mix_rows) + 1).astype(f32) == row_list).astype(f32).astype(bf16)
    frm = ((owner_of(all_rows) + 1).astype(f32) == col_list).astype(f32).astype(bf16)
    joined = jnp.where(
        (kind_of(mix_rows) == kind_of(mix_lanes)) & (mix_lanes < rows_e), dot_nt(to, frm), 0.0
    ).astype(bf16)
    mixer[:, :LANES] = joined
    mixer[:, LANES:] = joined

    def build_phi(o):
        lanes = slice(o * TB, (o + 1) * TB)
        q = iota((PERIOD, TB), 0).astype(f32) * (1.0 / PERIOD)
        co, si = [], []
        for a in range(3):
            turn = q * offs[a : a + 1, lanes]
            co.append(cos_turn(turn))
            si.append(cos_turn(turn - 0.25))
        flat_c, flat_s = [], []
        for y in range(PERIOD):
            cy, sy = co[1][y : y + 1], si[1][y : y + 1]
            flat_c.append(cy * co[0] - sy * si[0])
            flat_s.append(sy * co[0] + cy * si[0])
        line = iota((PERIOD, TB), 0)

        def ends(first, second):
            return jnp.where(line < HALF, first, pltpu.roll(second, HALF, 0))

        sides = [
            jnp.where(line == 0, pltpu.roll(flat_c[y], HALF, 0), flat_s[y]) for y in (0, HALF)
        ]
        real = jnp.concatenate([ends(flat_c[0], flat_c[HALF])] + flat_c[1:HALF], axis=0)
        imag = jnp.concatenate([ends(*sides)] + flat_s[1:HALF], axis=0)
        flip = co[2][HALF : HALF + 1]
        blocks = [jnp.concatenate([real, real * flip, imag, imag * flip], axis=0)]
        flat_c = jnp.concatenate(flat_c, axis=0)
        flat_s = jnp.concatenate(flat_s, axis=0)
        for z in range(1, HALF):
            cz, sz = co[2][z : z + 1], si[2][z : z + 1]
            blocks.append(
                jnp.concatenate([flat_c * cz - flat_s * sz, flat_s * cz + flat_c * sz], axis=0)
            )
        for g, block in enumerate(blocks):
            at = g * 2 * FLAT
            phi[at : at + 2 * FLAT, lanes] = block.astype(bf16)
            modes[lanes, at : at + 2 * FLAT] = jnp.transpose(block).astype(bf16)

    y_slab, z_slab = glen // n_row, glen // n_col
    scaled = 1.0 / glen

    def locate(r, c):
        o = r * n_col + c
        code = inbox[o].astype(f32)[9:10].astype(jnp.int32)
        slot = over(code, nd)
        holder = code & (nd - 1)
        row_at = holder * cr + over(slot, per_row)
        hot = (iota((slot_rows, TB), 0) == row_at).astype(f32).astype(bf16)
        at = pl.ds(pl.multiple_of(o * per_row, per_row), per_row)
        lists = jnp.concatenate(
            [table[2, at, :slot_rows], table[3, at, :slot_rows]], axis=0
        ).astype(bf16)
        found = dot(lists, hot)
        mine = iota((per_row, TB), 0) == (slot & (per_row - 1))
        high = jnp.sum(jnp.where(mine, found[:per_row], 0.0), axis=0, keepdims=True)
        low = jnp.sum(jnp.where(mine, found[per_row:], 0.0), axis=0, keepdims=True)
        cell = high.astype(jnp.int32) * 512 + low.astype(jnp.int32) + 256
        pos_x = over(cell, y_slab * z_slab)
        pos_y = over(holder, n_col) * y_slab + (over(cell, z_slab) & (y_slab - 1))
        pos_z = (holder & (n_col - 1)) * z_slab + (cell & (z_slab - 1))
        return [p.astype(f32) * scaled for p in (pos_x, pos_y, pos_z)]

    kx_col = (me_r * xs + iota((xs, 2 * TB), 0)).astype(f32)
    ky_col = (me_c * ys + iota((ys, 2 * TB), 0)).astype(f32)
    kz_col = iota((glen, 2 * TB), 0)

    def build_phase(pair, phase):
        spots = [locate(*place(i, j)) for i, j in pair]
        px, py, pz = (
            jnp.concatenate([spots[0][t], spots[1][t]], axis=1) for t in range(3)
        )
        turn = kx_col * px
        cx, nx = cos_turn(turn), cos_turn(turn + 0.25)
        turn = ky_col * py
        cy, ny = cos_turn(turn), cos_turn(turn + 0.25)
        cx, nx, cy, ny = (t.astype(bf16) for t in (cx, nx, cy, ny))
        for i in range(xs):
            a, b = cx[i : i + 1], nx[i : i + 1]
            phase[i * ys : (i + 1) * ys, :] = (a * cy - b * ny).astype(bf16)
            phase[xy + i * ys : xy + (i + 1) * ys, :] = (b * cy + a * ny).astype(bf16)
        return cos_turn(kz_col.astype(f32) * pz + jnp.where(kz_col > half, 0.25, 0.0))

    def far_copy(i, j):
        r, c = place(i, j)
        p = r * n_col + c
        q = i * n_col + j
        return remote(far_send.at[q], far_recv.at[me], far_ss.at[q], far_rs.at[me], r, c)

    def far_sums(pair, phase, tz):
        sums = dot(hat[...], phase[...])
        for k in range(6):
            line = jnp.sum(sums[k * glen : (k + 1) * glen] * tz, axis=0, keepdims=True)
            for t, (i, j) in enumerate(pair):
                half_line = line[:, t * TB : (t + 1) * TB]
                if i + j:
                    far_send[i * n_col + j, k : k + 1, :] = half_line
                else:
                    far_recv[me, k : k + 1, :] = half_line

    def far_start(some):
        for i, j in some:
            if i + j:
                far_copy(i, j).start()

    near = [cheb_coef[0] * noise_ref[a] for a in range(3)]
    own_rows = pl.ds(lax.rem(2 * me, 16), 2)
    scales = []

    band = 2 * LANES
    bands = [slice(t, t + band) for t in range(0, MODES, band)]

    def to_modes(m):
        rows = rows_e if m == 0 else rows_t
        for lanes in bands:
            sums = dot(wide[0:rows, :], modes[:, lanes])
            high = sums.astype(bf16)
            mixed[0:rows, lanes] = high
            mixed[LANES : LANES + rows, lanes] = (sums - high.astype(f32)).astype(bf16)

    def convolve(m):
        rows = rows_e if m == 0 else rows_t
        for lanes in bands:
            sums = dot(mixer[0:rows, :], mixed[:, lanes])
            turned = jnp.concatenate(
                [
                    pltpu.roll(sums[0:rows_t, g * LANES : (g + 1) * LANES], FLAT, 1)
                    for g in range(band // LANES)
                ],
                axis=1,
            )
            for a in range(3):
                total = spectrum[a : a + 1, lanes] * sums[a * nb : (a + 1) * nb]
                for b in range(3):
                    if a != b:
                        e = PAIRS.index((min(a, b), max(a, b)))
                        total = total + spectrum[e : e + 1, lanes] * sums[b * nb : (b + 1) * nb]
                        total = total + (
                            spectrum[e + 3 : e + 4, lanes] * turned[b * nb : (b + 1) * nb]
                        )
                lattice[a * nb : (a + 1) * nb, lanes] = total.astype(bf16)
            if m == 0:
                for a in range(3):
                    total = spectrum[9 + a : 10 + a, lanes] * sums[rows_t:rows_e]
                    high = total.astype(bf16)
                    at = rows_t + a * nd
                    lattice[at : at + nd, lanes] = high
                    lattice[at + 3 * nd : at + 4 * nd, lanes] = (
                        total - high.astype(f32)
                    ).astype(bf16)

    def to_beads(m):
        if m == 0:
            out = dot(lattice[...], phi[...])
            energy = out[rows_t : rows_t + 3 * nd] + out[rows_t + 3 * nd :]
            top = jnp.zeros((3 * nd, TB), f32)
            owner = iota((3 * nd, TB), 0) & (nd - 1)
            for o in range(nd):
                top = jnp.maximum(
                    top, jnp.where(owner == o, energy[:, o * TB : (o + 1) * TB], 0.0)
                )
            top = jnp.max(jnp.max(top, axis=1, keepdims=True), axis=0, keepdims=True)
            scales.append(jnp.broadcast_to(1.0 / jnp.sqrt(top + 1e-06), (16, TB)))
        elif m < DEGREES - 1:
            out = dot(lattice[0:rows_t, :], phi[...])
        scale = scales[0]
        before = cheb_b if m % 2 == 0 else cheb_a
        if m < DEGREES - 1:
            line = iota((16, TB), 0)
            for o in range(nd):
                first = 2 * o % 16
                base = 2 * o // 16 * 16
                mine = (line >= first) & (line < first + 2)
                for a in range(3):
                    got = out[a * nb + base : a * nb + base + 16, o * TB : (o + 1) * TB]
                    got = jnp.where(mine, scale * got, 0.0)
                    if m > 0:
                        got = 2.0 * got - before[a, o]
                    before[a, o] = got
                    wide[a * nb + base : a * nb + base + 16, o * TB : (o + 1) * TB] = (
                        got.astype(bf16)
                    )
            for a in range(3):
                near[a] = near[a] + cheb_coef[m + 1] * before[a, me, own_rows, :]
        else:
            last[...] = dot(
                lattice[0:rows_t, :], phi[:, pl.ds(pl.multiple_of(me * TB, TB), TB)]
            )
            for a in range(3):
                got = 2.0 * (scale[0:2] * last[pl.ds(a * nb + 2 * me, 2), :])
                near[a] = near[a] + cheb_coef[m + 1] * (got - before[a, me, own_rows, :])

    stages = [
        functools.partial(stage, m)
        for m in range(DEGREES) for stage in (to_modes, convolve, to_beads)
    ]
    pairs = [peers[t : t + 2] for t in range(0, nd, 2)]
    phases = (phase_a, phase_b)
    built = -(-3 * len(pairs) // 8)
    sends = (len(pairs) - 1,)
    held = []
    tz = build_phase(pairs[0], phase_a)
    for n, pair in enumerate(pairs):
        nxt = None
        if n + 1 < len(pairs):
            nxt = build_phase(pairs[n + 1], phases[(n + 1) % 2])
        if n >= built and False:
            stages.pop(0)()
        far_sums(pair, phases[n % 2], tz)
        tz = nxt
        held += pair
        if n in sends:
            far_start(held)
            held = []
        if n < built:
            for o in range(n * nd // built, (n + 1) * nd // built):
                build_phi(o)
    for stage in stages:
        stage()

    for i, j in others:
        msg_copy(i, j).wait_send()

    def far_arrive(i, j):
        r, c = place(i, j)
        p = r * n_col + c
        remote(far_send.at[0], far_recv.at[p], far_ss.at[0], far_rs.at[p], r, c).wait_recv()

    for i, j in others:
        far_arrive(i, j)
    for i, j in others:
        far_copy(i, j).wait_send()
    far = far_recv[0]
    for p in range(1, nd):
        far = far + far_recv[p]
    for a in range(3):
        out_ref[a] = near[a] + far[2 * a : 2 * a + 2, :]


def shared_device(noise_field, offsets, tile_list, send_cells, bead_slot, spectral):
    n_row = lax.axis_size("row")
    n_col = lax.axis_size("col")
    nd = n_row * n_col
    xs, ys, glen = spectral.shape[3:]
    slots = tile_list.shape[3]
    cap = send_cells.shape[2]
    xy = xs * ys
    cr = cap * nd // LANES
    msg_rows = -(-(12 + 2 * cr) // 16) * 16
    chunks = 4 if xy % 256 == 0 else 1
    dims = (n_row, n_col, slots, xs, ys, glen, cap)
    vmem = pl.BlockSpec(memory_space=pltpu.VMEM)
    hbm = pl.BlockSpec(memory_space=pl.ANY)
    dma = pltpu.SemaphoreType.DMA
    rows_t = 6 * nd
    spectrum = lattice_spectrum()
    return pl.pallas_call(
        functools.partial(shared_kernel, dims),
        out_shape=pltpu.VMEM(noise_field.shape, f32),
        in_specs=[hbm] * 7,
        out_specs=vmem,
        scratch_shapes=[
            pltpu.SMEM((2, slots), jnp.int32),
            pltpu.VMEM(noise_field.shape, f32),
            pltpu.VMEM(offsets.shape, jnp.int32),
            pltpu.VMEM((1, TB), jnp.int32),
            pltpu.VMEM((cap, nd), jnp.int32),
            pltpu.VMEM((12, xy, glen), f32),
            pltpu.VMEM((6 * (xy // chunks), 2 * glen), bf16),
            pltpu.VMEM((6 * glen, 2 * xy), bf16),
            pltpu.VMEM((2 * xy, 2 * TB), bf16),
            pltpu.VMEM((2 * xy, 2 * TB), bf16),
            pltpu.VMEM((MODES, nd * TB), bf16),
            pltpu.VMEM((nd * TB, MODES), bf16),
            pltpu.VMEM((rows_t + nd, nd * TB), bf16),
            pltpu.VMEM((3, nd, 16, TB), f32),
            pltpu.VMEM((3, nd, 16, TB), f32),
            pltpu.VMEM((rows_t + nd, 2 * LANES), bf16),
            pltpu.VMEM((2 * LANES, MODES), bf16),
            pltpu.VMEM((rows_t + 6 * nd, MODES), bf16),
            pltpu.VMEM((msg_rows, LANES), f32),
            pltpu.VMEM((msg_rows, LANES), bf16),
            pltpu.VMEM((nd, msg_rows, LANES), bf16),
            pltpu.VMEM((4, LANES, LANES), f32),
            pltpu.VMEM((3, nd * TB), f32),
            pltpu.VMEM(spectrum.shape, f32),
            pltpu.VMEM((rows_t, TB), f32),
            pltpu.VMEM((nd, 8, TB), f32),
            pltpu.VMEM((nd, 8, TB), f32),
            dma((5,)), dma((chunks,)), dma,
            dma((nd,)), dma((nd,)),
            dma((nd,)), dma((nd,)),
        ],
        compiler_params=pltpu.CompilerParams(
            collective_id=1, has_side_effects=True, vmem_limit_bytes=56 * 1024 * 1024
        ),
    )(
        tile_list.reshape(2, slots),
        noise_field,
        offsets,
        bead_slot.reshape(1, TB),
        send_cells.reshape(cap, nd),
        jnp.asarray(spectrum),
        spectral.reshape(12, xy, glen),
    )


def power_of_two(n):
    return n & (n - 1) == 0


def per_device(noise_field, offsets, tile_list, send_cells, bead_slot, spectral):
    n_row = lax.axis_size("row")
    n_col = lax.axis_size("col")
    nd = n_row * n_col
    xs, ys, glen = spectral.shape[3:]
    cap = send_cells.shape[2]
    fits = (
        8 <= nd <= 16
        and power_of_two(n_row)
        and power_of_two(n_col)
        and power_of_two(glen)
        and nd * tile_list.shape[3] <= LANES
        and cap % (LANES // nd) == 0
        and cap * nd <= 256
        and glen * (glen // n_row) * (glen // n_col) <= 1 << 17
        and ys % 16 == 0
    )
    run = shared_device if fits else spread_device
    return run(noise_field, offsets, tile_list, send_cells, bead_slot, spectral)


def solution(mesh):
    return jax.shard_map(
        per_device,
        mesh=mesh,
        in_specs=(
            P(None, None, ("groups", "row", "col")),
            P(None, ("groups", "row", "col")),
            P(("groups", "row"), "col", None, None),
            P(("groups", "row"), "col", None, None),
            P(("groups", "row", "col")),
            P(None, None, None, ("groups", "row"), "col", None),
        ),
        out_specs=P(None, None, ("groups", "row", "col")),
        check_vma=False,
    )
```

```python
import functools
import math

import jax
import jax.numpy as jnp
import ml_dtypes
import numpy as np
from jax import lax
from jax.experimental import pallas as pl
from jax.experimental.pallas import tpu as pltpu
from jax.sharding import PartitionSpec as P

TB = 128
LANES = 128
PERIOD = 8
DEGREES = 4

cheb_coef = (1.0, 0.45, -0.2, 0.12, -0.08)
kernel_range = 1.5

f32 = jnp.float32
bf16 = jnp.bfloat16


def iota(shape, dim):
    return lax.broadcasted_iota(jnp.int32, shape, dim)


def over(n, d):
    return lax.shift_right_logical(n, jnp.full(n.shape, d.bit_length() - 1, jnp.int32))


def dot(a, b):
    return jnp.dot(a, b, preferred_element_type=f32)


def dot_nt(a, b):
    return lax.dot_general(a, b, (((1,), (1,)), ((), ())), preferred_element_type=f32)


def cos_turn(turns):
    x = jnp.abs(turns - jnp.floor(turns) - 0.5) * 4.0 - 1.0
    x2 = x * x
    p = 0.00015148419
    for c in (-0.00467376557, 0.07968967928, -0.64596371106, 1.57079631847):
        p = p * x2 + c
    return p * x


def kernel(
    dims,
    tiles_ref, noise_ref, off_ref, slot_ref, cells_ref, spec_hbm,
    out_ref,
    spec, pre, hat, phase, ang, wang, tabf, tab, kmat,
    a_send, a_recv, b_send, row_b, col_b,
    e_send, e_recv, y_send, y_recv, far_send, far_recv,
    cur, prev, acc, scale,
    spec_sem, a_ss, a_rs, b_ss, b_rs, e_ss, e_rs, y_ss, y_rs, far_ss, far_rs,
):
    n_row, n_col, slots, xs, ys, glen, cap = dims
    nd = n_row * n_col
    xy = xs * ys
    cr = cap * nd // LANES
    kq = tab.shape[0]
    beads = n_col * TB
    me_r = lax.axis_index("row")
    me_c = lax.axis_index("col")
    me = me_r * n_col + me_c
    chunks = spec_sem.shape[0]
    part = xy // chunks
    per_row = LANES // nd

    def spec_copy(i):
        rows = pl.ds(i * part, part)
        return pltpu.make_async_copy(
            spec_hbm.at[:, rows, :], spec.at[:, rows, :], spec_sem.at[i]
        )

    for i in range(chunks):
        spec_copy(i).start()

    straight = nd <= 32
    if straight:
        rows_of = [me_r] + [lax.rem(me_r + d, n_row) for d in range(1, n_row)]
        cols_of = [me_c] + [lax.rem(me_c + d, n_col) for d in range(1, n_col)]
        order = sorted(
            [(i, j) for i in range(n_row) for j in range(n_col) if i + j],
            key=lambda t: (abs(t[1] - n_col // 2), abs(t[0] - n_row // 2)),
        )

    def each(body):
        if straight:
            for i, j in order:
                body(rows_of[i], cols_of[j])
            return

        def turn(d, carry):
            body(lax.rem(me_r + d // n_col, n_row), lax.rem(me_c + lax.rem(d, n_col), n_col))
            return carry

        lax.fori_loop(1, nd, turn, 0)

    def each_row(body):
        if straight:
            for d in range(1, n_row):
                body(rows_of[d])
        else:
            lax.fori_loop(1, n_row, lambda d, t: (body(lax.rem(me_r + d, n_row)), t)[1], 0)

    def each_col(body):
        if straight:
            for d in range(1, n_col):
                body(cols_of[d])
        else:
            lax.fori_loop(1, n_col, lambda d, t: (body(lax.rem(me_c + d, n_col)), t)[1], 0)

    barrier = pltpu.get_barrier_semaphore()

    def greet(r, c):
        pl.semaphore_signal(
            barrier, inc=1, device_id={"row": r, "col": c},
            device_id_type=pl.DeviceIdType.MESH,
        )

    each(greet)

    def remote(src, dst, ss, rs, r, c):
        return pltpu.make_async_remote_copy(
            src_ref=src, dst_ref=dst, send_sem=ss, recv_sem=rs,
            device_id={"row": r, "col": c}, device_id_type=pl.DeviceIdType.MESH,
        )

    def packed_cells():
        flat = cells_ref[...].astype(f32)
        if per_row == 1:
            return flat
        spread = (iota((nd, LANES), 1) & (nd - 1)) == iota((nd, LANES), 0)
        wide = jnp.dot(
            flat, spread.astype(f32), precision=lax.Precision.HIGHEST,
            preferred_element_type=f32,
        )
        mine = over(iota((cap, LANES), 1), nd) == (iota((cap, LANES), 0) & (per_row - 1))
        return jnp.sum(jnp.where(mine, wide, 0.0).reshape(cr, per_row, LANES), axis=1)

    a_send[0:1, :] = slot_ref[...].astype(f32)
    cells = packed_cells()
    a_send[1 : 1 + cr, :] = cells
    a_recv[me, 0:1, :] = slot_ref[...].astype(f32)
    a_recv[me, 1 : 1 + cr, :] = cells
    own_noise = jnp.concatenate([noise_ref[0], noise_ref[1], noise_ref[2]], axis=1)
    off = off_ref[...].astype(f32)
    own_off = jnp.concatenate([off[0:1], off[1:2], off[2:3]], axis=1)
    b_send[0:2, :] = own_noise
    b_send[2:3, :] = own_off
    row_b[me_c, 0:2, :] = own_noise
    row_b[me_c, 2:3, :] = own_off
    col_b[me_r, 0:2, :] = own_noise
    col_b[me_r, 2:3, :] = own_off
    tabf[...] = jnp.zeros_like(tabf)

    pl.semaphore_wait(barrier, nd - 1)

    def b_row_copy(c):
        return remote(b_send, row_b.at[me_c], b_ss.at[c], b_rs.at[me_c], me_r, c)

    def b_col_copy(r):
        return remote(
            b_send, col_b.at[me_r], b_ss.at[n_col + r], b_rs.at[n_col + me_r], r, me_c
        )

    each_col(lambda c: b_row_copy(c).start())
    each_row(lambda r: b_col_copy(r).start())

    def a_copy(r, c):
        p = r * n_col + c
        return remote(a_send, a_recv.at[me], a_ss.at[p], a_rs.at[me], r, c)

    each(lambda r, c: a_copy(r, c).start())

    gi = iota((2 * glen, 2 * glen), 0)
    gj = iota((2 * glen, 2 * glen), 1)
    zi, zj = gi & (glen - 1), gj & (glen - 1)
    in_im, out_im = gi >= glen, gj >= glen
    half = glen // 2
    same = zi == zj
    mirror = (zi + zj == glen) & (zi != zj)
    even = zj <= half
    plain = in_im == out_im
    fold = jnp.where(
        even,
        jnp.where(plain & (same | mirror), 1.0, 0.0),
        jnp.where(
            plain,
            0.0,
            jnp.where(same, 1.0, 0.0) - jnp.where(mirror, 1.0, 0.0),
        )
        * jnp.where(out_im, -1.0, 1.0),
    ).astype(bf16)

    width_sq = (glen / 8.0) ** 2
    front = math.sqrt(1.5) / (2.0 * math.pi * width_sq) ** 0.75
    def signed(n):
        return jnp.where(n < half, n, n - glen).astype(f32)

    ky = signed(me_c * ys + iota((ys, glen), 0))
    kz = signed(iota((ys, glen), 1))
    kyz_sq = ky * ky + kz * kz

    def hat_block(i, first):
        kx = signed(me_r * xs + i)
        q = kx * kx + kyz_sq
        amp = jnp.where(q > 0, front * jnp.exp(q * (-0.25 / width_sq)), 0.0)
        damp = amp / jnp.maximum(q, 1.0)
        rows = pl.ds(pl.multiple_of(i * ys, ys), ys)
        at = pl.multiple_of((i - first) * ys, ys)
        waves = (kx, ky, kz)
        for v in range(2):
            for p in range(2):
                s = [spec[(p * 3 + a) * 2 + v, rows, :] for a in range(3)]
                along = (kx * s[0] + ky * s[1] + kz * s[2]) * damp
                for a in range(3):
                    pre[pl.ds((a * 2 + v) * part + at, ys), p * glen : (p + 1) * glen] = (
                        amp * s[a] - waves[a] * along
                    ).astype(bf16)
        return first

    per = part // ys
    for i in range(chunks):
        spec_copy(i).wait()
        lax.fori_loop(i * per, (i + 1) * per, hat_block, i * per)
        folded = dot(pre[...], fold)
        for k in range(6):
            for p in range(2):
                hat[
                    p * xy + i * part : p * xy + (i + 1) * part, k * glen : (k + 1) * glen
                ] = folded[
                    k * part : (k + 1) * part, p * glen : (p + 1) * glen
                ].astype(bf16)

    def b_col_arrive(r):
        remote(b_send, col_b.at[r], b_ss.at[n_col + r], b_rs.at[n_col + r], r, me_c).wait_recv()

    def b_row_arrive(c):
        remote(b_send, row_b.at[c], b_ss.at[c], b_rs.at[c], me_r, c).wait_recv()

    each_row(b_col_arrive)
    each_col(b_row_arrive)

    eye = (iota((TB, TB), 0) == iota((TB, TB), 1)).astype(f32)
    ones = jnp.ones((TB, TB), bf16)
    scale_sq = kernel_range * kernel_range

    def pick(values, into, s):
        tr = tiles_ref[0, s]
        return tuple(
            into[i] + values * jnp.where(tr == i, 1.0, 0.0).astype(f32) for i in range(n_col)
        )

    def build(s, energies):
        tr = jnp.maximum(tiles_ref[0, s], 0)
        tc = jnp.maximum(tiles_ref[1, s], 0)
        row_off = row_b[tr][2:3, :]
        col_off = col_b[tc][2:3, :]
        disp = []
        for a in range(3):
            lanes = slice(a * TB, (a + 1) * TB)
            rp = dot((eye * row_off[:, lanes]).astype(bf16), ones)
            gap = (rp - col_off[:, lanes]).astype(jnp.int32) + PERIOD // 2
            disp.append(((gap & (PERIOD - 1)) - PERIOD // 2).astype(f32))
        squares = disp[0] * disp[0] + disp[1] * disp[1] + disp[2] * disp[2]
        envelope = jnp.exp(squares * (-0.5 / scale_sq)) / scale_sq
        third = squares / 3.0
        for a in range(3):
            for b in range(a, 3):
                element = disp[a] * disp[b]
                if a == b:
                    element = element - third
                entry = (envelope * element).astype(bf16)
                kmat[s, a * TB : (a + 1) * TB, b * TB : (b + 1) * TB] = entry
                if a != b:
                    kmat[s, b * TB : (b + 1) * TB, a * TB : (a + 1) * TB] = entry
        wide = kmat[s].astype(f32)
        sq = wide * wide
        high = sq.astype(bf16)
        low = (sq - high.astype(f32)).astype(bf16)
        one_row = jnp.ones((8, 3 * TB), bf16)
        energy = dot_nt(one_row, high) + dot_nt(one_row, low)
        return pick(energy[0:1], energies, s)

    energies = lax.fori_loop(
        0, slots, build, tuple(jnp.zeros((1, 3 * TB), f32) for _ in range(n_col)),
        unroll=slots <= 4,
    )
    for i in range(n_col):
        e_send[i : i + 1, :] = energies[i]
        e_recv[me, i : i + 1, :] = energies[i]

    def e_copy(r, c):
        p = r * n_col + c
        return remote(e_send, e_recv.at[me], e_ss.at[p], e_rs.at[me], r, c)

    for r in range(n_row):
        cur[r] = col_b[r, 0:2, :]
    acc[...] = cheb_coef[0] * own_noise

    def a_arrive(r, c):
        p = r * n_col + c
        remote(a_send, a_recv.at[p], a_ss.at[p], a_rs.at[p], r, c).wait_recv()

    def prepare_table():
        each(a_arrive)

        def spread(h, carry):
            tabf[pl.ds(h * cr, cr), :] = a_recv[h, 1 : 1 + cr, :]
            return carry

        lax.fori_loop(0, nd, spread, 0)
        cell = tabf[...].astype(jnp.int32)
        y_slab, z_slab = glen // n_row, glen // n_col
        holder = over(iota((kq, LANES), 0), cr)
        pos_x = over(cell, y_slab * z_slab)
        pos_y = over(holder, n_col) * y_slab + (over(cell, z_slab) & (y_slab - 1))
        pos_z = (holder & (n_col - 1)) * z_slab + (cell & (z_slab - 1))
        for at, pos in enumerate((pos_x, pos_y, pos_z)):
            tab[:, at * LANES : (at + 1) * LANES] = pos.astype(f32).astype(bf16)

    x_step = LANES // ys
    lane = iota((LANES, LANES), 1)
    scaled = 1.0 / glen
    along_x = ((me_r * xs + over(lane, ys)).astype(f32) * scaled).astype(bf16)
    along_y = ((me_c * ys + (lane & (ys - 1))).astype(f32) * scaled).astype(bf16)
    wang[...] = jnp.zeros_like(wang)
    wang[0:LANES, 0:LANES] = along_x
    wang[LANES : 2 * LANES, 0:LANES] = along_y
    wang[0:LANES, LANES : 2 * LANES] = jnp.full((LANES, LANES), x_step * scaled, bf16)
    wang[2 * LANES :, 2 * LANES :] = (lane.astype(f32) * scaled).astype(bf16)
    rep = over(iota((8, 6 * glen), 1), glen) == iota((8, 6 * glen), 0)
    rep = rep.astype(f32).astype(bf16)
    wide_ones = jnp.ones((TB, kq), bf16)
    step_rows = 32

    def far_copy(i, c):
        return remote(
            far_send.at[i * n_col + c], far_recv.at[me],
            far_ss.at[i * n_col + c], far_rs.at[me], i, c,
        )

    def far_chunk(i, carry):
        spots = jnp.concatenate(
            [eye * a_recv[i * n_col + c, 0:1, :] for c in range(n_col)], axis=0
        ).astype(bf16)
        code = dot(spots, wide_ones).astype(jnp.int32)
        s_idx = over(code, nd)
        row_idx = (code & (nd - 1)) * cr + over(s_idx, per_row)
        hot = (row_idx == iota((beads, kq), 1)).astype(f32).astype(bf16)
        found = dot(hot, tab[...])
        owner_of = i * n_col + over(iota((beads, LANES), 0), TB)
        want = (s_idx[:, :LANES] & (per_row - 1)) * nd + owner_of
        keep = want == iota((beads, LANES), 1)
        places = jnp.concatenate(
            [jnp.where(keep, found[:, k * LANES : (k + 1) * LANES], 0.0) for k in range(3)],
            axis=1,
        ).astype(bf16)
        ang[...] = dot(places, wang[...])

        def phase_block(j, carry):
            rows = pl.ds(pl.multiple_of(j * step_rows, step_rows), step_rows)
            at_lane = iota((step_rows, LANES), 1)
            start = ang[rows, 0:LANES]
            co = cos_turn(start)
            ns = cos_turn(start + 0.25)
            turn_x = cos_turn(
                ang[rows, LANES : 2 * LANES] - jnp.where(at_lane == 1, 0.25, 0.0)
            )
            cd = jnp.broadcast_to(turn_x[:, 0:1], co.shape)
            sd = jnp.broadcast_to(turn_x[:, 1:2], co.shape)
            ang[rows, 2 * LANES :] = cos_turn(
                ang[rows, 2 * LANES :] + jnp.where(at_lane > half, 0.25, 0.0)
            )
            for g in range(xy // LANES):
                phase[rows, g * LANES : (g + 1) * LANES] = co.astype(bf16)
                phase[rows, xy + g * LANES : xy + (g + 1) * LANES] = ns.astype(bf16)
                co, ns = co * cd + ns * sd, ns * cd - co * sd
            return carry

        lax.fori_loop(0, beads // step_rows, phase_block, 0)
        sums = dot(phase[...], hat[...])
        tz = ang[:, 2 * LANES :]
        weighted = jnp.concatenate(
            [(sums[:, k * glen : (k + 1) * glen] * tz).astype(bf16) for k in range(6)], axis=1
        )
        res = dot_nt(rep, weighted)
        for c in range(n_col):
            owner = i * n_col + c
            far_send[owner] = res[:, c * TB : (c + 1) * TB]

            @pl.when(owner == me)
            def _():
                far_recv[me] = res[:, c * TB : (c + 1) * TB]

            @pl.when(owner != me)
            def _():
                far_copy(i, c).start()

        return carry

    def y_copy(r, c, par):
        p = r * n_col + c
        return remote(
            y_send.at[par, c], y_recv.at[par, me], y_ss.at[par, p], y_rs.at[par, me], r, c
        )

    def y_arrive(r, c, par):
        p = r * n_col + c
        remote(
            y_send.at[par, 0], y_recv.at[par, p], y_ss.at[par, p], y_rs.at[par, p], r, c
        ).wait_recv()

    each(lambda r, c: e_copy(r, c).start())

    def degree_step(m, carry):
        par = lax.rem(m, 2)

        def apply(s, sums):
            tc = jnp.maximum(tiles_ref[1, s], 0)
            w = cur[tc]
            w = jnp.concatenate([w, jnp.zeros((6, 3 * TB), f32)], axis=0).astype(bf16)
            return pick(dot_nt(w, kmat[s])[0:2], sums, s)

        sums = lax.fori_loop(
            0, slots, apply, tuple(jnp.zeros((2, 3 * TB), f32) for _ in range(n_col)),
            unroll=slots <= 4,
        )
        own = jnp.zeros((2, 3 * TB), f32)
        for i in range(n_col):
            y_send[par, i] = sums[i]
            own = own + sums[i] * jnp.where(me_c == i, 1.0, 0.0).astype(f32)
        y_recv[par, me] = own
        each(lambda r, c: y_copy(r, c, par).start())

        @pl.when(m == 0)
        def _():
            prepare_table()

        lax.fori_loop(m * n_row // DEGREES, (m + 1) * n_row // DEGREES, far_chunk, 0)

        @pl.when(m == 0)
        def _():
            def e_arrive(r, c):
                p = r * n_col + c
                remote(e_send, e_recv.at[p], e_ss.at[p], e_rs.at[p], r, c).wait_recv()

            each(e_arrive)
            top = jnp.zeros((n_col, 3 * TB), f32)
            for r in range(n_row):
                total = e_recv[r * n_col]
                for c in range(1, n_col):
                    total = total + e_recv[r * n_col + c]
                top = jnp.maximum(top, total)
            largest = jnp.max(jnp.max(top, axis=1, keepdims=True), axis=0, keepdims=True)
            scale[...] = jnp.broadcast_to(1.0 / jnp.sqrt(largest + 1e-06), scale.shape)

        each(lambda r, c: y_arrive(r, c, par))
        each(lambda r, c: y_copy(r, c, par).wait_send())
        first = jnp.where(m == 0, 1.0, 0.0).astype(f32)
        coef = jnp.where(
            m == 0, cheb_coef[1],
            jnp.where(m == 1, cheb_coef[2], jnp.where(m == 2, cheb_coef[3], cheb_coef[4])),
        ).astype(f32)
        sc = jnp.concatenate([scale[0:2, :]] * 3, axis=1)

        def advance(r, carry):
            total = y_recv[par, r * n_col]
            for c in range(1, n_col):
                total = total + y_recv[par, r * n_col + c]
            now = sc * total
            following = jnp.where(m == 0, now, 2.0 * now - prev[r])
            prev[r] = cur[r]
            cur[r] = following
            return carry

        lax.fori_loop(0, n_row, advance, 0)
        acc[...] = acc[...] + coef * cur[me_r]
        return carry

    prev[...] = jnp.zeros_like(prev)
    lax.fori_loop(0, DEGREES, degree_step, 0)

    each_row(lambda r: b_col_copy(r).wait_send())
    each_col(lambda c: b_row_copy(c).wait_send())
    each(lambda r, c: a_copy(r, c).wait_send())
    each(lambda r, c: e_copy(r, c).wait_send())

    def far_arrive(r, c):
        p = r * n_col + c
        remote(
            far_send.at[p], far_recv.at[p], far_ss.at[p], far_rs.at[p], r, c
        ).wait_recv()

    each(far_arrive)
    each(lambda r, c: far_copy(r, c).wait_send())
    far = lax.fori_loop(
        1, nd, lambda p, t: t + far_recv[p], far_recv[0]
    )
    near = acc[...]
    for a in range(3):
        out_ref[a] = near[:, a * TB : (a + 1) * TB] + far[2 * a : 2 * a + 2, :]


def spread_device(noise_field, offsets, tile_list, send_cells, bead_slot, spectral):
    n_row = lax.axis_size("row")
    n_col = lax.axis_size("col")
    nd = n_row * n_col
    xs, ys, glen = spectral.shape[3:]
    slots = tile_list.shape[3]
    cap = send_cells.shape[2]
    cr = cap * nd // LANES
    xy = xs * ys
    kq = max(LANES, nd * cr)
    beads = n_col * TB
    a_rows = -(-(1 + cr) // 4) * 4
    chunks = 4 if xy % 256 == 0 else 1
    dims = (n_row, n_col, slots, xs, ys, glen, cap)
    vmem = pl.BlockSpec(memory_space=pltpu.VMEM)
    dma = pltpu.SemaphoreType.DMA
    wide = 3 * TB
    return pl.pallas_call(
        functools.partial(kernel, dims),
        out_shape=jax.ShapeDtypeStruct(noise_field.shape, f32),
        in_specs=[pl.BlockSpec(memory_space=pltpu.SMEM), vmem, vmem, vmem, vmem,
                  pl.BlockSpec(memory_space=pl.ANY)],
        out_specs=vmem,
        scratch_shapes=[
            pltpu.VMEM((12, xy, glen), f32),
            pltpu.VMEM((6 * (xy // chunks), 2 * glen), bf16),
            pltpu.VMEM((2 * xy, 6 * glen), bf16),
            pltpu.VMEM((beads, 2 * xy), bf16),
            pltpu.VMEM((beads, 3 * LANES), f32),
            pltpu.VMEM((3 * LANES, 3 * LANES), bf16),
            pltpu.VMEM((kq, LANES), f32),
            pltpu.VMEM((kq, 3 * LANES), bf16),
            pltpu.VMEM((slots, wide, wide), bf16),
            pltpu.VMEM((a_rows, LANES), f32),
            pltpu.VMEM((nd, a_rows, LANES), f32),
            pltpu.VMEM((4, wide), f32),
            pltpu.VMEM((n_col, 4, wide), f32),
            pltpu.VMEM((n_row, 4, wide), f32),
            pltpu.VMEM((n_col, wide), f32),
            pltpu.VMEM((nd, n_col, wide), f32),
            pltpu.VMEM((2, n_col, 2, wide), f32),
            pltpu.VMEM((2, nd, 2, wide), f32),
            pltpu.VMEM((nd, 8, TB), f32),
            pltpu.VMEM((nd, 8, TB), f32),
            pltpu.VMEM((n_row, 2, wide), f32),
            pltpu.VMEM((n_row, 2, wide), f32),
            pltpu.VMEM((2, wide), f32),
            pltpu.VMEM((8, LANES), f32),
            dma((chunks,)),
            dma((nd,)), dma((nd,)),
            dma((n_row + n_col,)), dma((n_row + n_col,)),
            dma((nd,)), dma((nd,)),
            dma((2, nd)), dma((2, nd)),
            dma((nd,)), dma((nd,)),
        ],
        compiler_params=pltpu.CompilerParams(
            collective_id=0, has_side_effects=True, vmem_limit_bytes=56 * 1024 * 1024
        ),
    )(
        tile_list.reshape(2, slots),
        noise_field,
        offsets,
        bead_slot.reshape(1, TB),
        send_cells.reshape(cap, nd),
        spectral.reshape(12, xy, glen),
    )


HALF = PERIOD // 2
FLAT = PERIOD * PERIOD
GROUPS = HALF
MODES = PERIOD**3
PAIRS = ((0, 0), (1, 1), (2, 2), (0, 1), (0, 2), (1, 2))


def lattice_spectrum():
    code = np.arange(PERIOD**3)
    site = np.stack([code // FLAT, code // PERIOD % PERIOD, code % PERIOD])
    disp = (site + PERIOD // 2) % PERIOD - PERIOD // 2
    d = disp.astype(np.float32)
    squares = d[0] * d[0] + d[1] * d[1] + d[2] * d[2]
    scale_sq = np.float32(kernel_range * kernel_range)
    envelope = np.exp(squares * np.float32(-0.5 / scale_sq)) / scale_sq
    table = np.zeros((3, 3, PERIOD**3))
    for a, b in PAIRS:
        element = d[a] * d[b]
        if a == b:
            element = element - squares / np.float32(3.0)
        table[a, b] = (envelope * element).astype(ml_dtypes.bfloat16).astype(np.float64)
        table[b, a] = table[a, b]
    energy = (table * table).sum(axis=1)
    ends = [(x, y) for y in (0, HALF) for x in range(HALF)]
    middle = [(x, y) for y in range(1, HALF) for x in range(PERIOD)]
    turned = [(HALF if x == 0 else x, y) for x, y in ends]
    modes = []
    for part, lead in enumerate((ends, turned)):
        modes += [(x, y, z, part) for z in (0, HALF) for x, y in lead + middle]
    for z in range(1, HALF):
        modes += [(n % PERIOD, n // PERIOD, z, p) for p in range(2) for n in range(FLAT)]
    wave = np.array(modes)
    angle = 2.0 * np.pi / PERIOD * ((wave[:, :3] @ site) % PERIOD)
    alone = (wave[:, :3] % HALF == 0).all(axis=1)
    weight = np.where(alone, 1.0, 2.0) / PERIOD**3
    turn = np.where(wave[:, 3] == 0, 1.0, -1.0)
    rows = [weight * (np.cos(angle) @ table[p]) for p in PAIRS]
    rows += [-turn * weight * (np.sin(angle) @ table[p]) for p in PAIRS[3:]]
    rows += [weight * (np.cos(angle) @ energy[a]) for a in range(3)]
    rows += [np.zeros(MODES)] * (-len(rows) % 8)
    return np.stack(rows).astype(np.float32)


def shared_kernel(
    dims,
    tiles_hbm, noise_hbm, off_hbm, slot_hbm, cells_hbm, spectrum_hbm, spec_hbm,
    out_ref,
    tiles_ref, noise_ref, off_ref, slot_ref, cells_ref,
    spec, pre, hat, phase_a, phase_b, phi, modes, wide, cheb_a, cheb_b, mixer, lattice,
    msg_f, msg, inbox, table, offs, spectrum, last,
    far_send, far_recv,
    load_sem, spec_sem, spectrum_sem, m_ss, m_rs, far_ss, far_rs,
):
    n_row, n_col, slots, xs, ys, glen, cap = dims
    nd = n_row * n_col
    xy = xs * ys
    per_row = LANES // nd
    cr = cap // per_row
    cells_at = 10
    tile_at = cells_at + 2 * cr
    beads = nd * TB
    me_r = lax.axis_index("row")
    me_c = lax.axis_index("col")
    me = me_r * n_col + me_c
    chunks = spec_sem.shape[0]
    part = xy // chunks
    nb = 2 * nd
    rows_t = 3 * nb
    rows_e = rows_t + nd

    def spec_copy(i):
        rows = pl.ds(i * part, part)
        return pltpu.make_async_copy(
            spec_hbm.at[:, rows, :], spec.at[:, rows, :], spec_sem.at[i]
        )

    loads = [
        pltpu.make_async_copy(src, dst, load_sem.at[k])
        for k, (src, dst) in enumerate((
            (cells_hbm, cells_ref), (tiles_hbm, tiles_ref), (noise_hbm, noise_ref),
            (off_hbm, off_ref), (slot_hbm, slot_ref),
        ))
    ]

    peers = sorted(
        [(i, j) for i in range(n_row) for j in range(n_col)], key=lambda t: (-t[1], -t[0])
    )
    others = peers[:-1]

    def place(i, j):
        return jnp.bitwise_xor(me_r, i), jnp.bitwise_xor(me_c, j)

    barrier = pltpu.get_barrier_semaphore()
    for i, j in others:
        r, c = place(i, j)
        pl.semaphore_signal(
            barrier, inc=1, device_id={"row": r, "col": c},
            device_id_type=pl.DeviceIdType.MESH,
        )
    for load in loads:
        load.start()
    for i in range(chunks):
        spec_copy(i).start()
    spectrum_copy = pltpu.make_async_copy(spectrum_hbm, spectrum, spectrum_sem)
    spectrum_copy.start()

    def remote(src, dst, ss, rs, r, c):
        return pltpu.make_async_remote_copy(
            src_ref=src, dst_ref=dst, send_sem=ss, recv_sem=rs,
            device_id={"row": r, "col": c}, device_id_type=pl.DeviceIdType.MESH,
        )

    for load in loads:
        load.wait()
    for a in range(3):
        msg_f[2 * a : 2 * a + 2, :] = noise_ref[a]
    msg_f[6:9, :] = off_ref[...].astype(f32)
    msg_f[9:10, :] = slot_ref[...].astype(f32)
    spread = over(iota((nd, LANES), 1), per_row) == iota((nd, LANES), 0)
    spread = spread.astype(f32).astype(bf16)
    keep = (iota((cap, LANES), 1) & (per_row - 1)) == (iota((cap, LANES), 0) & (per_row - 1))
    cells = cells_ref[...]
    for h, half_cell in enumerate((over(cells, 512), (cells & 511) - 256)):
        out = dot(half_cell.astype(f32).astype(bf16), spread)
        out = jnp.sum(jnp.where(keep, out, 0.0).reshape(cr, per_row, LANES), axis=1)
        msg_f[cells_at + h * cr : cells_at + (h + 1) * cr, :] = out
    lane_row = iota((1, LANES), 1)
    row_list = jnp.zeros((1, LANES), jnp.int32)
    col_list = jnp.zeros((1, LANES), jnp.int32)
    for s in range(slots):
        here = lane_row == me * slots + s
        tr, tc = tiles_ref[0, s], tiles_ref[1, s]
        row_list = jnp.where(
            here & (jnp.full((1, LANES), tr) >= 0), me_r * n_col + tr + 1, row_list
        )
        col_list = jnp.where(here, tc * n_col + me_c + 1, col_list)
    msg_f[tile_at : tile_at + 1, :] = row_list.astype(f32)
    msg_f[tile_at + 1 : tile_at + 2, :] = col_list.astype(f32)
    if tile_at + 2 < msg_f.shape[0]:
        msg_f[tile_at + 2 :, :] = jnp.zeros((msg_f.shape[0] - tile_at - 2, LANES), f32)
    msg[...] = msg_f[...].astype(bf16)
    inbox[me] = msg_f[...].astype(bf16)

    pl.semaphore_wait(barrier, nd - 1)

    def msg_copy(i, j):
        r, c = place(i, j)
        p = i * n_col + j
        return remote(msg, inbox.at[me], m_ss.at[p], m_rs.at[me], r, c)

    def msg_arrive(i, j):
        r, c = place(i, j)
        p = r * n_col + c
        remote(msg, inbox.at[p], m_ss.at[0], m_rs.at[p], r, c).wait_recv()

    for i, j in others:
        msg_copy(i, j).start()

    gj = iota((2 * glen, 2 * glen), 0)
    gi = iota((2 * glen, 2 * glen), 1)
    zi, zj = gi & (glen - 1), gj & (glen - 1)
    in_im, out_im = gi >= glen, gj >= glen
    half = glen // 2
    same = zi == zj
    mirror = (zi + zj == glen) & (zi != zj)
    even = zj <= half
    plain = in_im == out_im
    fold = jnp.where(
        even,
        jnp.where(plain & (same | mirror), 1.0, 0.0),
        jnp.where(
            plain,
            0.0,
            jnp.where(same, 1.0, 0.0) - jnp.where(mirror, 1.0, 0.0),
        )
        * jnp.where(out_im, -1.0, 1.0),
    ).astype(bf16)

    width_sq = (glen / 8.0) ** 2
    front = math.sqrt(1.5) / (2.0 * math.pi * width_sq) ** 0.75

    def signed(n):
        return jnp.where(n < half, n, n - glen).astype(f32)

    ky = signed(me_c * ys + iota((ys, glen), 0))
    kz = signed(iota((ys, glen), 1))
    kyz_sq = ky * ky + kz * kz

    def hat_block(i, first):
        kx = signed(me_r * xs + i)
        q = kx * kx + kyz_sq
        amp = jnp.where(q > 0, front * jnp.exp(q * (-0.25 / width_sq)), 0.0)
        damp = amp / jnp.maximum(q, 1.0)
        rows = pl.ds(pl.multiple_of(i * ys, ys), ys)
        at = pl.multiple_of((i - first) * ys, ys)
        waves = (kx, ky, kz)
        for v in range(2):
            for p in range(2):
                s = [spec[(p * 3 + a) * 2 + v, rows, :] for a in range(3)]
                along = (kx * s[0] + ky * s[1] + kz * s[2]) * damp
                for a in range(3):
                    pre[pl.ds((a * 2 + v) * part + at, ys), p * glen : (p + 1) * glen] = (
                        amp * s[a] - waves[a] * along
                    ).astype(bf16)
        return first

    per = part // ys
    for i in range(chunks):
        spec_copy(i).wait()
        lax.fori_loop(i * per, (i + 1) * per, hat_block, i * per)
        for k in range(6):
            folded = dot_nt(fold, pre[k * part : (k + 1) * part, :]).astype(bf16)
            for p in range(2):
                hat[
                    k * glen : (k + 1) * glen, p * xy + i * part : p * xy + (i + 1) * part
                ] = folded[p * glen : (p + 1) * glen, :]

    spectrum_copy.wait()
    for i, j in others[::-1]:
        msg_arrive(i, j)

    row_list = jnp.zeros((1, LANES), f32)
    col_list = jnp.zeros((1, LANES), f32)
    slot_rows = nb // 2 * cr
    for o in range(nd):
        got = inbox[o].astype(f32)
        row_list = row_list + got[tile_at : tile_at + 1]
        col_list = col_list + got[tile_at + 1 : tile_at + 2]
        for h in range(2):
            table[h, o * cr : (o + 1) * cr, :] = got[
                cells_at + h * cr : cells_at + (h + 1) * cr
            ]
        offs[:, o * TB : (o + 1) * TB] = got[6:9]
        for a in range(3):
            cheb_a[a, o] = got[2 * a : 2 * a + 2]
    tables = []
    for h in range(2):
        tables.append(jnp.transpose(table[h])[:, :slot_rows])
    for h in range(2):
        table[2 + h, :, :slot_rows] = tables[h]

    line = iota((nb + nd, LANES), 0)
    target = jnp.where(line < nb, over(line, 2), line - nb) + 1
    to = (target.astype(f32) == row_list).astype(f32).astype(bf16)
    source = iota((LANES, LANES), 0) + 1
    frm = (source.astype(f32) == col_list).astype(f32).astype(bf16)
    joined = dot_nt(to, frm)
    odd = (iota((nb, TB), 0) & 1) == 1

    def fill(o, a, values):
        lanes = slice(o * TB, (o + 1) * TB)
        spread = jnp.where(odd, values[1:2], values[0:1])
        wide[a * nb : (a + 1) * nb, lanes] = (mixer[0:nb, lanes] * spread).astype(bf16)

    for o in range(nd):
        lanes = slice(o * TB, (o + 1) * TB)
        mixer[:, lanes] = jnp.broadcast_to(joined[:, o : o + 1], (nb + nd, TB))
        wide[rows_t:rows_e, lanes] = mixer[nb:, lanes].astype(bf16)
        for a in range(3):
            fill(o, a, cheb_a[a, o])

    def build_phi(o):
        lanes = slice(o * TB, (o + 1) * TB)
        q = iota((PERIOD, TB), 0).astype(f32) * (1.0 / PERIOD)
        co, si = [], []
        for a in range(3):
            turn = q * offs[a : a + 1, lanes]
            co.append(cos_turn(turn))
            si.append(cos_turn(turn - 0.25))
        flat_c, flat_s = [], []
        for y in range(PERIOD):
            cy, sy = co[1][y : y + 1], si[1][y : y + 1]
            flat_c.append(cy * co[0] - sy * si[0])
            flat_s.append(sy * co[0] + cy * si[0])
        line = iota((PERIOD, TB), 0)

        def ends(first, second):
            return jnp.where(line < HALF, first, pltpu.roll(second, HALF, 0))

        sides = [
            jnp.where(line == 0, pltpu.roll(flat_c[y], HALF, 0), flat_s[y]) for y in (0, HALF)
        ]
        real = jnp.concatenate([ends(flat_c[0], flat_c[HALF])] + flat_c[1:HALF], axis=0)
        imag = jnp.concatenate([ends(*sides)] + flat_s[1:HALF], axis=0)
        flip = co[2][HALF : HALF + 1]
        blocks = [jnp.concatenate([real, real * flip, imag, imag * flip], axis=0)]
        flat_c = jnp.concatenate(flat_c, axis=0)
        flat_s = jnp.concatenate(flat_s, axis=0)
        for z in range(1, HALF):
            cz, sz = co[2][z : z + 1], si[2][z : z + 1]
            blocks.append(
                jnp.concatenate([flat_c * cz - flat_s * sz, flat_s * cz + flat_c * sz], axis=0)
            )
        for g, block in enumerate(blocks):
            at = g * 2 * FLAT
            phi[at : at + 2 * FLAT, lanes] = block.astype(bf16)
            modes[lanes, at : at + 2 * FLAT] = jnp.transpose(block).astype(bf16)

    y_slab, z_slab = glen // n_row, glen // n_col
    scaled = 1.0 / glen

    def locate(r, c):
        o = r * n_col + c
        code = inbox[o].astype(f32)[9:10].astype(jnp.int32)
        slot = over(code, nd)
        holder = code & (nd - 1)
        row_at = holder * cr + over(slot, per_row)
        hot = (iota((slot_rows, TB), 0) == row_at).astype(f32).astype(bf16)
        at = pl.ds(pl.multiple_of(o * per_row, per_row), per_row)
        lists = jnp.concatenate(
            [table[2, at, :slot_rows], table[3, at, :slot_rows]], axis=0
        ).astype(bf16)
        found = dot(lists, hot)
        mine = iota((per_row, TB), 0) == (slot & (per_row - 1))
        high = jnp.sum(jnp.where(mine, found[:per_row], 0.0), axis=0, keepdims=True)
        low = jnp.sum(jnp.where(mine, found[per_row:], 0.0), axis=0, keepdims=True)
        cell = high.astype(jnp.int32) * 512 + low.astype(jnp.int32) + 256
        pos_x = over(cell, y_slab * z_slab)
        pos_y = over(holder, n_col) * y_slab + (over(cell, z_slab) & (y_slab - 1))
        pos_z = (holder & (n_col - 1)) * z_slab + (cell & (z_slab - 1))
        return [p.astype(f32) * scaled for p in (pos_x, pos_y, pos_z)]

    kx_col = (me_r * xs + iota((xs, 2 * TB), 0)).astype(f32)
    ky_col = (me_c * ys + iota((ys, 2 * TB), 0)).astype(f32)
    kz_col = iota((glen, 2 * TB), 0)

    def build_phase(pair, phase):
        spots = [locate(*place(i, j)) for i, j in pair]
        px, py, pz = (
            jnp.concatenate([spots[0][t], spots[1][t]], axis=1) for t in range(3)
        )
        turn = kx_col * px
        cx, nx = cos_turn(turn), cos_turn(turn + 0.25)
        turn = ky_col * py
        cy, ny = cos_turn(turn), cos_turn(turn + 0.25)
        cx, nx, cy, ny = (t.astype(bf16) for t in (cx, nx, cy, ny))
        for i in range(xs):
            a, b = cx[i : i + 1], nx[i : i + 1]
            phase[i * ys : (i + 1) * ys, :] = (a * cy - b * ny).astype(bf16)
            phase[xy + i * ys : xy + (i + 1) * ys, :] = (b * cy + a * ny).astype(bf16)
        return cos_turn(kz_col.astype(f32) * pz + jnp.where(kz_col > half, 0.25, 0.0))

    def far_copy(i, j):
        r, c = place(i, j)
        p = r * n_col + c
        q = i * n_col + j
        return remote(far_send.at[q], far_recv.at[me], far_ss.at[q], far_rs.at[me], r, c)

    def far_sums(pair, phase, tz):
        sums = dot(hat[...], phase[...])
        for k in range(6):
            line = jnp.sum(sums[k * glen : (k + 1) * glen] * tz, axis=0, keepdims=True)
            for t, (i, j) in enumerate(pair):
                half_line = line[:, t * TB : (t + 1) * TB]
                if i + j:
                    far_send[i * n_col + j, k : k + 1, :] = half_line
                else:
                    far_recv[me, k : k + 1, :] = half_line

    def far_start(some):
        for i, j in some:
            if i + j:
                far_copy(i, j).start()

    near = [cheb_coef[0] * noise_ref[a] for a in range(3)]
    scales = []

    band = 2 * LANES
    bands = [slice(t, t + band) for t in range(0, MODES, band)]

    def to_modes(m):
        rows = rows_e if m == 0 else rows_t
        for lanes in bands:
            sums = dot(wide[0:rows, :], modes[:, lanes])
            turned = jnp.concatenate(
                [
                    pltpu.roll(sums[0:rows_t, g * LANES : (g + 1) * LANES], FLAT, 1)
                    for g in range(band // LANES)
                ],
                axis=1,
            )
            for a in range(3):
                total = spectrum[a : a + 1, lanes] * sums[a * nb : (a + 1) * nb]
                for b in range(3):
                    if a != b:
                        e = PAIRS.index((min(a, b), max(a, b)))
                        total = total + spectrum[e : e + 1, lanes] * sums[b * nb : (b + 1) * nb]
                        total = total + (
                            spectrum[e + 3 : e + 4, lanes] * turned[b * nb : (b + 1) * nb]
                        )
                lattice[a * nb : (a + 1) * nb, lanes] = total.astype(bf16)
            if m == 0:
                for a in range(3):
                    total = spectrum[9 + a : 10 + a, lanes] * sums[rows_t:rows_e]
                    high = total.astype(bf16)
                    at = rows_t + a * nd
                    lattice[at : at + nd, lanes] = high
                    lattice[at + 3 * nd : at + 4 * nd, lanes] = (
                        total - high.astype(f32)
                    ).astype(bf16)

    def to_beads(m):
        if m == 0:
            out = dot(lattice[...], phi[...])
            energy = out[rows_t : rows_t + 3 * nd] + out[rows_t + 3 * nd :]
            top = jnp.zeros((3 * nd, TB), f32)
            owner = iota((3 * nd, TB), 0) & (nd - 1)
            for o in range(nd):
                top = jnp.maximum(
                    top, jnp.where(owner == o, energy[:, o * TB : (o + 1) * TB], 0.0)
                )
            top = jnp.max(jnp.max(top, axis=1, keepdims=True), axis=0, keepdims=True)
            scales.append(jnp.broadcast_to(1.0 / jnp.sqrt(top + 1e-06), (2, TB)))
        elif m < DEGREES - 1:
            out = dot(lattice[0:rows_t, :], phi[...])
        scale = scales[0]
        before = cheb_b if m % 2 == 0 else cheb_a
        if m < DEGREES - 1:
            for o in range(nd):
                for a in range(3):
                    at = a * nb + 2 * o
                    got = scale * out[at : at + 2, o * TB : (o + 1) * TB]
                    if m > 0:
                        got = 2.0 * got - before[a, o]
                    before[a, o] = got
                    fill(o, a, got)
            for a in range(3):
                near[a] = near[a] + cheb_coef[m + 1] * before[a, me]
        else:
            last[...] = dot(
                lattice[0:rows_t, :], phi[:, pl.ds(pl.multiple_of(me * TB, TB), TB)]
            )
            for a in range(3):
                got = 2.0 * (scale * last[pl.ds(a * nb + 2 * me, 2), :])
                near[a] = near[a] + cheb_coef[m + 1] * (got - before[a, me])

    stages = [
        functools.partial(stage, m)
        for m in range(DEGREES) for stage in (to_modes, to_beads)
    ]
    pairs = [peers[t : t + 2] for t in range(0, nd, 2)]
    phases = (phase_a, phase_b)
    built = -(-3 * len(pairs) // 8)
    sends = (len(pairs) - 1,)
    held = []
    tz = build_phase(pairs[0], phase_a)
    for n, pair in enumerate(pairs):
        nxt = None
        if n + 1 < len(pairs):
            nxt = build_phase(pairs[n + 1], phases[(n + 1) % 2])
        if n >= built and False:
            stages.pop(0)()
        far_sums(pair, phases[n % 2], tz)
        tz = nxt
        held += pair
        if n in sends:
            far_start(held)
            held = []
        if n < built:
            for o in range(n * nd // built, (n + 1) * nd // built):
                build_phi(o)
    for stage in stages:
        stage()

    for i, j in others:
        msg_copy(i, j).wait_send()

    def far_arrive(i, j):
        r, c = place(i, j)
        p = r * n_col + c
        remote(far_send.at[0], far_recv.at[p], far_ss.at[0], far_rs.at[p], r, c).wait_recv()

    for i, j in others:
        far_arrive(i, j)
    for i, j in others:
        far_copy(i, j).wait_send()
    far = far_recv[0]
    for p in range(1, nd):
        far = far + far_recv[p]
    for a in range(3):
        out_ref[a] = near[a] + far[2 * a : 2 * a + 2, :]


def shared_device(noise_field, offsets, tile_list, send_cells, bead_slot, spectral):
    n_row = lax.axis_size("row")
    n_col = lax.axis_size("col")
    nd = n_row * n_col
    xs, ys, glen = spectral.shape[3:]
    slots = tile_list.shape[3]
    cap = send_cells.shape[2]
    xy = xs * ys
    cr = cap * nd // LANES
    msg_rows = -(-(12 + 2 * cr) // 16) * 16
    chunks = 4 if xy % 256 == 0 else 1
    dims = (n_row, n_col, slots, xs, ys, glen, cap)
    vmem = pl.BlockSpec(memory_space=pltpu.VMEM)
    hbm = pl.BlockSpec(memory_space=pl.ANY)
    dma = pltpu.SemaphoreType.DMA
    rows_t = 6 * nd
    spectrum = lattice_spectrum()
    return pl.pallas_call(
        functools.partial(shared_kernel, dims),
        out_shape=pltpu.VMEM(noise_field.shape, f32),
        in_specs=[hbm] * 7,
        out_specs=vmem,
        scratch_shapes=[
            pltpu.SMEM((2, slots), jnp.int32),
            pltpu.VMEM(noise_field.shape, f32),
            pltpu.VMEM(offsets.shape, jnp.int32),
            pltpu.VMEM((1, TB), jnp.int32),
            pltpu.VMEM((cap, nd), jnp.int32),
            pltpu.VMEM((12, xy, glen), f32),
            pltpu.VMEM((6 * (xy // chunks), 2 * glen), bf16),
            pltpu.VMEM((6 * glen, 2 * xy), bf16),
            pltpu.VMEM((2 * xy, 2 * TB), bf16),
            pltpu.VMEM((2 * xy, 2 * TB), bf16),
            pltpu.VMEM((MODES, nd * TB), bf16),
            pltpu.VMEM((nd * TB, MODES), bf16),
            pltpu.VMEM((rows_t + nd, nd * TB), bf16),
            pltpu.VMEM((3, nd, 2, TB), f32),
            pltpu.VMEM((3, nd, 2, TB), f32),
            pltpu.VMEM((3 * nd, nd * TB), f32),
            pltpu.VMEM((rows_t + 6 * nd, MODES), bf16),
            pltpu.VMEM((msg_rows, LANES), f32),
            pltpu.VMEM((msg_rows, LANES), bf16),
            pltpu.VMEM((nd, msg_rows, LANES), bf16),
            pltpu.VMEM((4, LANES, LANES), f32),
            pltpu.VMEM((3, nd * TB), f32),
            pltpu.VMEM(spectrum.shape, f32),
            pltpu.VMEM((rows_t, TB), f32),
            pltpu.VMEM((nd, 8, TB), f32),
            pltpu.VMEM((nd, 8, TB), f32),
            dma((5,)), dma((chunks,)), dma,
            dma((nd,)), dma((nd,)),
            dma((nd,)), dma((nd,)),
        ],
        compiler_params=pltpu.CompilerParams(
            collective_id=1, has_side_effects=True, vmem_limit_bytes=56 * 1024 * 1024
        ),
    )(
        tile_list.reshape(2, slots),
        noise_field,
        offsets,
        bead_slot.reshape(1, TB),
        send_cells.reshape(cap, nd),
        jnp.asarray(spectrum),
        spectral.reshape(12, xy, glen),
    )


def power_of_two(n):
    return n & (n - 1) == 0


def per_device(noise_field, offsets, tile_list, send_cells, bead_slot, spectral):
    n_row = lax.axis_size("row")
    n_col = lax.axis_size("col")
    nd = n_row * n_col
    xs, ys, glen = spectral.shape[3:]
    cap = send_cells.shape[2]
    fits = (
        8 <= nd <= 16
        and power_of_two(n_row)
        and power_of_two(n_col)
        and power_of_two(glen)
        and nd * tile_list.shape[3] <= LANES
        and cap % (LANES // nd) == 0
        and cap * nd <= 256
        and glen * (glen // n_row) * (glen // n_col) <= 1 << 17
        and ys % 16 == 0
    )
    run = shared_device if fits else spread_device
    return run(noise_field, offsets, tile_list, send_cells, bead_slot, spectral)


def solution(mesh):
    return jax.shard_map(
        per_device,
        mesh=mesh,
        in_specs=(
            P(None, None, ("groups", "row", "col")),
            P(None, ("groups", "row", "col")),
            P(("groups", "row"), "col", None, None),
            P(("groups", "row"), "col", None, None),
            P(("groups", "row", "col")),
            P(None, None, None, ("groups", "row"), "col", None),
        ),
        out_specs=P(None, None, ("groups", "row", "col")),
        check_vma=False,
    )
```

```python
import functools
import math

import jax
import jax.numpy as jnp
import ml_dtypes
import numpy as np
from jax import lax
from jax.experimental import pallas as pl
from jax.experimental.pallas import tpu as pltpu
from jax.sharding import PartitionSpec as P

TB = 128
LANES = 128
PERIOD = 8
DEGREES = 4

cheb_coef = (1.0, 0.45, -0.2, 0.12, -0.08)
kernel_range = 1.5

f32 = jnp.float32
bf16 = jnp.bfloat16


def iota(shape, dim):
    return lax.broadcasted_iota(jnp.int32, shape, dim)


def over(n, d):
    return lax.shift_right_logical(n, jnp.full(n.shape, d.bit_length() - 1, jnp.int32))


def dot(a, b):
    return jnp.dot(a, b, preferred_element_type=f32)


def dot_nt(a, b):
    return lax.dot_general(a, b, (((1,), (1,)), ((), ())), preferred_element_type=f32)


def cos_turn(turns):
    x = jnp.abs(turns - jnp.floor(turns) - 0.5) * 4.0 - 1.0
    x2 = x * x
    p = 0.00015148419
    for c in (-0.00467376557, 0.07968967928, -0.64596371106, 1.57079631847):
        p = p * x2 + c
    return p * x


def kernel(
    dims,
    tiles_ref, noise_ref, off_ref, slot_ref, cells_ref, spec_hbm,
    out_ref,
    spec, pre, hat, phase, ang, wang, tabf, tab, kmat,
    a_send, a_recv, b_send, row_b, col_b,
    e_send, e_recv, y_send, y_recv, far_send, far_recv,
    cur, prev, acc, scale,
    spec_sem, a_ss, a_rs, b_ss, b_rs, e_ss, e_rs, y_ss, y_rs, far_ss, far_rs,
):
    n_row, n_col, slots, xs, ys, glen, cap = dims
    nd = n_row * n_col
    xy = xs * ys
    cr = cap * nd // LANES
    kq = tab.shape[0]
    beads = n_col * TB
    me_r = lax.axis_index("row")
    me_c = lax.axis_index("col")
    me = me_r * n_col + me_c
    chunks = spec_sem.shape[0]
    part = xy // chunks
    per_row = LANES // nd

    def spec_copy(i):
        rows = pl.ds(i * part, part)
        return pltpu.make_async_copy(
            spec_hbm.at[:, rows, :], spec.at[:, rows, :], spec_sem.at[i]
        )

    for i in range(chunks):
        spec_copy(i).start()

    straight = nd <= 32
    if straight:
        rows_of = [me_r] + [lax.rem(me_r + d, n_row) for d in range(1, n_row)]
        cols_of = [me_c] + [lax.rem(me_c + d, n_col) for d in range(1, n_col)]
        order = sorted(
            [(i, j) for i in range(n_row) for j in range(n_col) if i + j],
            key=lambda t: (abs(t[1] - n_col // 2), abs(t[0] - n_row // 2)),
        )

    def each(body):
        if straight:
            for i, j in order:
                body(rows_of[i], cols_of[j])
            return

        def turn(d, carry):
            body(lax.rem(me_r + d // n_col, n_row), lax.rem(me_c + lax.rem(d, n_col), n_col))
            return carry

        lax.fori_loop(1, nd, turn, 0)

    def each_row(body):
        if straight:
            for d in range(1, n_row):
                body(rows_of[d])
        else:
            lax.fori_loop(1, n_row, lambda d, t: (body(lax.rem(me_r + d, n_row)), t)[1], 0)

    def each_col(body):
        if straight:
            for d in range(1, n_col):
                body(cols_of[d])
        else:
            lax.fori_loop(1, n_col, lambda d, t: (body(lax.rem(me_c + d, n_col)), t)[1], 0)

    barrier = pltpu.get_barrier_semaphore()

    def greet(r, c):
        pl.semaphore_signal(
            barrier, inc=1, device_id={"row": r, "col": c},
            device_id_type=pl.DeviceIdType.MESH,
        )

    each(greet)

    def remote(src, dst, ss, rs, r, c):
        return pltpu.make_async_remote_copy(
            src_ref=src, dst_ref=dst, send_sem=ss, recv_sem=rs,
            device_id={"row": r, "col": c}, device_id_type=pl.DeviceIdType.MESH,
        )

    def packed_cells():
        flat = cells_ref[...].astype(f32)
        if per_row == 1:
            return flat
        spread = (iota((nd, LANES), 1) & (nd - 1)) == iota((nd, LANES), 0)
        wide = jnp.dot(
            flat, spread.astype(f32), precision=lax.Precision.HIGHEST,
            preferred_element_type=f32,
        )
        mine = over(iota((cap, LANES), 1), nd) == (iota((cap, LANES), 0) & (per_row - 1))
        return jnp.sum(jnp.where(mine, wide, 0.0).reshape(cr, per_row, LANES), axis=1)

    a_send[0:1, :] = slot_ref[...].astype(f32)
    cells = packed_cells()
    a_send[1 : 1 + cr, :] = cells
    a_recv[me, 0:1, :] = slot_ref[...].astype(f32)
    a_recv[me, 1 : 1 + cr, :] = cells
    own_noise = jnp.concatenate([noise_ref[0], noise_ref[1], noise_ref[2]], axis=1)
    off = off_ref[...].astype(f32)
    own_off = jnp.concatenate([off[0:1], off[1:2], off[2:3]], axis=1)
    b_send[0:2, :] = own_noise
    b_send[2:3, :] = own_off
    row_b[me_c, 0:2, :] = own_noise
    row_b[me_c, 2:3, :] = own_off
    col_b[me_r, 0:2, :] = own_noise
    col_b[me_r, 2:3, :] = own_off
    tabf[...] = jnp.zeros_like(tabf)

    pl.semaphore_wait(barrier, nd - 1)

    def b_row_copy(c):
        return remote(b_send, row_b.at[me_c], b_ss.at[c], b_rs.at[me_c], me_r, c)

    def b_col_copy(r):
        return remote(
            b_send, col_b.at[me_r], b_ss.at[n_col + r], b_rs.at[n_col + me_r], r, me_c
        )

    each_col(lambda c: b_row_copy(c).start())
    each_row(lambda r: b_col_copy(r).start())

    def a_copy(r, c):
        p = r * n_col + c
        return remote(a_send, a_recv.at[me], a_ss.at[p], a_rs.at[me], r, c)

    each(lambda r, c: a_copy(r, c).start())

    gi = iota((2 * glen, 2 * glen), 0)
    gj = iota((2 * glen, 2 * glen), 1)
    zi, zj = gi & (glen - 1), gj & (glen - 1)
    in_im, out_im = gi >= glen, gj >= glen
    half = glen // 2
    same = zi == zj
    mirror = (zi + zj == glen) & (zi != zj)
    even = zj <= half
    plain = in_im == out_im
    fold = jnp.where(
        even,
        jnp.where(plain & (same | mirror), 1.0, 0.0),
        jnp.where(
            plain,
            0.0,
            jnp.where(same, 1.0, 0.0) - jnp.where(mirror, 1.0, 0.0),
        )
        * jnp.where(out_im, -1.0, 1.0),
    ).astype(bf16)

    width_sq = (glen / 8.0) ** 2
    front = math.sqrt(1.5) / (2.0 * math.pi * width_sq) ** 0.75
    def signed(n):
        return jnp.where(n < half, n, n - glen).astype(f32)

    ky = signed(me_c * ys + iota((ys, glen), 0))
    kz = signed(iota((ys, glen), 1))
    kyz_sq = ky * ky + kz * kz

    def hat_block(i, first):
        kx = signed(me_r * xs + i)
        q = kx * kx + kyz_sq
        amp = jnp.where(q > 0, front * jnp.exp(q * (-0.25 / width_sq)), 0.0)
        damp = amp / jnp.maximum(q, 1.0)
        rows = pl.ds(pl.multiple_of(i * ys, ys), ys)
        at = pl.multiple_of((i - first) * ys, ys)
        waves = (kx, ky, kz)
        for v in range(2):
            for p in range(2):
                s = [spec[(p * 3 + a) * 2 + v, rows, :] for a in range(3)]
                along = (kx * s[0] + ky * s[1] + kz * s[2]) * damp
                for a in range(3):
                    pre[pl.ds((a * 2 + v) * part + at, ys), p * glen : (p + 1) * glen] = (
                        amp * s[a] - waves[a] * along
                    ).astype(bf16)
        return first

    per = part // ys
    for i in range(chunks):
        spec_copy(i).wait()
        lax.fori_loop(i * per, (i + 1) * per, hat_block, i * per)
        folded = dot(pre[...], fold)
        for k in range(6):
            for p in range(2):
                hat[
                    p * xy + i * part : p * xy + (i + 1) * part, k * glen : (k + 1) * glen
                ] = folded[
                    k * part : (k + 1) * part, p * glen : (p + 1) * glen
                ].astype(bf16)

    def b_col_arrive(r):
        remote(b_send, col_b.at[r], b_ss.at[n_col + r], b_rs.at[n_col + r], r, me_c).wait_recv()

    def b_row_arrive(c):
        remote(b_send, row_b.at[c], b_ss.at[c], b_rs.at[c], me_r, c).wait_recv()

    each_row(b_col_arrive)
    each_col(b_row_arrive)

    eye = (iota((TB, TB), 0) == iota((TB, TB), 1)).astype(f32)
    ones = jnp.ones((TB, TB), bf16)
    scale_sq = kernel_range * kernel_range

    def pick(values, into, s):
        tr = tiles_ref[0, s]
        return tuple(
            into[i] + values * jnp.where(tr == i, 1.0, 0.0).astype(f32) for i in range(n_col)
        )

    def build(s, energies):
        tr = jnp.maximum(tiles_ref[0, s], 0)
        tc = jnp.maximum(tiles_ref[1, s], 0)
        row_off = row_b[tr][2:3, :]
        col_off = col_b[tc][2:3, :]
        disp = []
        for a in range(3):
            lanes = slice(a * TB, (a + 1) * TB)
            rp = dot((eye * row_off[:, lanes]).astype(bf16), ones)
            gap = (rp - col_off[:, lanes]).astype(jnp.int32) + PERIOD // 2
            disp.append(((gap & (PERIOD - 1)) - PERIOD // 2).astype(f32))
        squares = disp[0] * disp[0] + disp[1] * disp[1] + disp[2] * disp[2]
        envelope = jnp.exp(squares * (-0.5 / scale_sq)) / scale_sq
        third = squares / 3.0
        for a in range(3):
            for b in range(a, 3):
                element = disp[a] * disp[b]
                if a == b:
                    element = element - third
                entry = (envelope * element).astype(bf16)
                kmat[s, a * TB : (a + 1) * TB, b * TB : (b + 1) * TB] = entry
                if a != b:
                    kmat[s, b * TB : (b + 1) * TB, a * TB : (a + 1) * TB] = entry
        wide = kmat[s].astype(f32)
        sq = wide * wide
        high = sq.astype(bf16)
        low = (sq - high.astype(f32)).astype(bf16)
        one_row = jnp.ones((8, 3 * TB), bf16)
        energy = dot_nt(one_row, high) + dot_nt(one_row, low)
        return pick(energy[0:1], energies, s)

    energies = lax.fori_loop(
        0, slots, build, tuple(jnp.zeros((1, 3 * TB), f32) for _ in range(n_col)),
        unroll=slots <= 4,
    )
    for i in range(n_col):
        e_send[i : i + 1, :] = energies[i]
        e_recv[me, i : i + 1, :] = energies[i]

    def e_copy(r, c):
        p = r * n_col + c
        return remote(e_send, e_recv.at[me], e_ss.at[p], e_rs.at[me], r, c)

    for r in range(n_row):
        cur[r] = col_b[r, 0:2, :]
    acc[...] = cheb_coef[0] * own_noise

    def a_arrive(r, c):
        p = r * n_col + c
        remote(a_send, a_recv.at[p], a_ss.at[p], a_rs.at[p], r, c).wait_recv()

    def prepare_table():
        each(a_arrive)

        def spread(h, carry):
            tabf[pl.ds(h * cr, cr), :] = a_recv[h, 1 : 1 + cr, :]
            return carry

        lax.fori_loop(0, nd, spread, 0)
        cell = tabf[...].astype(jnp.int32)
        y_slab, z_slab = glen // n_row, glen // n_col
        holder = over(iota((kq, LANES), 0), cr)
        pos_x = over(cell, y_slab * z_slab)
        pos_y = over(holder, n_col) * y_slab + (over(cell, z_slab) & (y_slab - 1))
        pos_z = (holder & (n_col - 1)) * z_slab + (cell & (z_slab - 1))
        for at, pos in enumerate((pos_x, pos_y, pos_z)):
            tab[:, at * LANES : (at + 1) * LANES] = pos.astype(f32).astype(bf16)

    x_step = LANES // ys
    lane = iota((LANES, LANES), 1)
    scaled = 1.0 / glen
    along_x = ((me_r * xs + over(lane, ys)).astype(f32) * scaled).astype(bf16)
    along_y = ((me_c * ys + (lane & (ys - 1))).astype(f32) * scaled).astype(bf16)
    wang[...] = jnp.zeros_like(wang)
    wang[0:LANES, 0:LANES] = along_x
    wang[LANES : 2 * LANES, 0:LANES] = along_y
    wang[0:LANES, LANES : 2 * LANES] = jnp.full((LANES, LANES), x_step * scaled, bf16)
    wang[2 * LANES :, 2 * LANES :] = (lane.astype(f32) * scaled).astype(bf16)
    rep = over(iota((8, 6 * glen), 1), glen) == iota((8, 6 * glen), 0)
    rep = rep.astype(f32).astype(bf16)
    wide_ones = jnp.ones((TB, kq), bf16)
    step_rows = 32

    def far_copy(i, c):
        return remote(
            far_send.at[i * n_col + c], far_recv.at[me],
            far_ss.at[i * n_col + c], far_rs.at[me], i, c,
        )

    def far_chunk(i, carry):
        spots = jnp.concatenate(
            [eye * a_recv[i * n_col + c, 0:1, :] for c in range(n_col)], axis=0
        ).astype(bf16)
        code = dot(spots, wide_ones).astype(jnp.int32)
        s_idx = over(code, nd)
        row_idx = (code & (nd - 1)) * cr + over(s_idx, per_row)
        hot = (row_idx == iota((beads, kq), 1)).astype(f32).astype(bf16)
        found = dot(hot, tab[...])
        owner_of = i * n_col + over(iota((beads, LANES), 0), TB)
        want = (s_idx[:, :LANES] & (per_row - 1)) * nd + owner_of
        keep = want == iota((beads, LANES), 1)
        places = jnp.concatenate(
            [jnp.where(keep, found[:, k * LANES : (k + 1) * LANES], 0.0) for k in range(3)],
            axis=1,
        ).astype(bf16)
        ang[...] = dot(places, wang[...])

        def phase_block(j, carry):
            rows = pl.ds(pl.multiple_of(j * step_rows, step_rows), step_rows)
            at_lane = iota((step_rows, LANES), 1)
            start = ang[rows, 0:LANES]
            co = cos_turn(start)
            ns = cos_turn(start + 0.25)
            turn_x = cos_turn(
                ang[rows, LANES : 2 * LANES] - jnp.where(at_lane == 1, 0.25, 0.0)
            )
            cd = jnp.broadcast_to(turn_x[:, 0:1], co.shape)
            sd = jnp.broadcast_to(turn_x[:, 1:2], co.shape)
            ang[rows, 2 * LANES :] = cos_turn(
                ang[rows, 2 * LANES :] + jnp.where(at_lane > half, 0.25, 0.0)
            )
            for g in range(xy // LANES):
                phase[rows, g * LANES : (g + 1) * LANES] = co.astype(bf16)
                phase[rows, xy + g * LANES : xy + (g + 1) * LANES] = ns.astype(bf16)
                co, ns = co * cd + ns * sd, ns * cd - co * sd
            return carry

        lax.fori_loop(0, beads // step_rows, phase_block, 0)
        sums = dot(phase[...], hat[...])
        tz = ang[:, 2 * LANES :]
        weighted = jnp.concatenate(
            [(sums[:, k * glen : (k + 1) * glen] * tz).astype(bf16) for k in range(6)], axis=1
        )
        res = dot_nt(rep, weighted)
        for c in range(n_col):
            owner = i * n_col + c
            far_send[owner] = res[:, c * TB : (c + 1) * TB]

            @pl.when(owner == me)
            def _():
                far_recv[me] = res[:, c * TB : (c + 1) * TB]

            @pl.when(owner != me)
            def _():
                far_copy(i, c).start()

        return carry

    def y_copy(r, c, par):
        p = r * n_col + c
        return remote(
            y_send.at[par, c], y_recv.at[par, me], y_ss.at[par, p], y_rs.at[par, me], r, c
        )

    def y_arrive(r, c, par):
        p = r * n_col + c
        remote(
            y_send.at[par, 0], y_recv.at[par, p], y_ss.at[par, p], y_rs.at[par, p], r, c
        ).wait_recv()

    each(lambda r, c: e_copy(r, c).start())

    def degree_step(m, carry):
        par = lax.rem(m, 2)

        def apply(s, sums):
            tc = jnp.maximum(tiles_ref[1, s], 0)
            w = cur[tc]
            w = jnp.concatenate([w, jnp.zeros((6, 3 * TB), f32)], axis=0).astype(bf16)
            return pick(dot_nt(w, kmat[s])[0:2], sums, s)

        sums = lax.fori_loop(
            0, slots, apply, tuple(jnp.zeros((2, 3 * TB), f32) for _ in range(n_col)),
            unroll=slots <= 4,
        )
        own = jnp.zeros((2, 3 * TB), f32)
        for i in range(n_col):
            y_send[par, i] = sums[i]
            own = own + sums[i] * jnp.where(me_c == i, 1.0, 0.0).astype(f32)
        y_recv[par, me] = own
        each(lambda r, c: y_copy(r, c, par).start())

        @pl.when(m == 0)
        def _():
            prepare_table()

        lax.fori_loop(m * n_row // DEGREES, (m + 1) * n_row // DEGREES, far_chunk, 0)

        @pl.when(m == 0)
        def _():
            def e_arrive(r, c):
                p = r * n_col + c
                remote(e_send, e_recv.at[p], e_ss.at[p], e_rs.at[p], r, c).wait_recv()

            each(e_arrive)
            top = jnp.zeros((n_col, 3 * TB), f32)
            for r in range(n_row):
                total = e_recv[r * n_col]
                for c in range(1, n_col):
                    total = total + e_recv[r * n_col + c]
                top = jnp.maximum(top, total)
            largest = jnp.max(jnp.max(top, axis=1, keepdims=True), axis=0, keepdims=True)
            scale[...] = jnp.broadcast_to(1.0 / jnp.sqrt(largest + 1e-06), scale.shape)

        each(lambda r, c: y_arrive(r, c, par))
        each(lambda r, c: y_copy(r, c, par).wait_send())
        first = jnp.where(m == 0, 1.0, 0.0).astype(f32)
        coef = jnp.where(
            m == 0, cheb_coef[1],
            jnp.where(m == 1, cheb_coef[2], jnp.where(m == 2, cheb_coef[3], cheb_coef[4])),
        ).astype(f32)
        sc = jnp.concatenate([scale[0:2, :]] * 3, axis=1)

        def advance(r, carry):
            total = y_recv[par, r * n_col]
            for c in range(1, n_col):
                total = total + y_recv[par, r * n_col + c]
            now = sc * total
            following = jnp.where(m == 0, now, 2.0 * now - prev[r])
            prev[r] = cur[r]
            cur[r] = following
            return carry

        lax.fori_loop(0, n_row, advance, 0)
        acc[...] = acc[...] + coef * cur[me_r]
        return carry

    prev[...] = jnp.zeros_like(prev)
    lax.fori_loop(0, DEGREES, degree_step, 0)

    each_row(lambda r: b_col_copy(r).wait_send())
    each_col(lambda c: b_row_copy(c).wait_send())
    each(lambda r, c: a_copy(r, c).wait_send())
    each(lambda r, c: e_copy(r, c).wait_send())

    def far_arrive(r, c):
        p = r * n_col + c
        remote(
            far_send.at[p], far_recv.at[p], far_ss.at[p], far_rs.at[p], r, c
        ).wait_recv()

    each(far_arrive)
    each(lambda r, c: far_copy(r, c).wait_send())
    far = lax.fori_loop(
        1, nd, lambda p, t: t + far_recv[p], far_recv[0]
    )
    near = acc[...]
    for a in range(3):
        out_ref[a] = near[:, a * TB : (a + 1) * TB] + far[2 * a : 2 * a + 2, :]


def spread_device(noise_field, offsets, tile_list, send_cells, bead_slot, spectral):
    n_row = lax.axis_size("row")
    n_col = lax.axis_size("col")
    nd = n_row * n_col
    xs, ys, glen = spectral.shape[3:]
    slots = tile_list.shape[3]
    cap = send_cells.shape[2]
    cr = cap * nd // LANES
    xy = xs * ys
    kq = max(LANES, nd * cr)
    beads = n_col * TB
    a_rows = -(-(1 + cr) // 4) * 4
    chunks = 4 if xy % 256 == 0 else 1
    dims = (n_row, n_col, slots, xs, ys, glen, cap)
    vmem = pl.BlockSpec(memory_space=pltpu.VMEM)
    dma = pltpu.SemaphoreType.DMA
    wide = 3 * TB
    return pl.pallas_call(
        functools.partial(kernel, dims),
        out_shape=jax.ShapeDtypeStruct(noise_field.shape, f32),
        in_specs=[pl.BlockSpec(memory_space=pltpu.SMEM), vmem, vmem, vmem, vmem,
                  pl.BlockSpec(memory_space=pl.ANY)],
        out_specs=vmem,
        scratch_shapes=[
            pltpu.VMEM((12, xy, glen), f32),
            pltpu.VMEM((6 * (xy // chunks), 2 * glen), bf16),
            pltpu.VMEM((2 * xy, 6 * glen), bf16),
            pltpu.VMEM((beads, 2 * xy), bf16),
            pltpu.VMEM((beads, 3 * LANES), f32),
            pltpu.VMEM((3 * LANES, 3 * LANES), bf16),
            pltpu.VMEM((kq, LANES), f32),
            pltpu.VMEM((kq, 3 * LANES), bf16),
            pltpu.VMEM((slots, wide, wide), bf16),
            pltpu.VMEM((a_rows, LANES), f32),
            pltpu.VMEM((nd, a_rows, LANES), f32),
            pltpu.VMEM((4, wide), f32),
            pltpu.VMEM((n_col, 4, wide), f32),
            pltpu.VMEM((n_row, 4, wide), f32),
            pltpu.VMEM((n_col, wide), f32),
            pltpu.VMEM((nd, n_col, wide), f32),
            pltpu.VMEM((2, n_col, 2, wide), f32),
            pltpu.VMEM((2, nd, 2, wide), f32),
            pltpu.VMEM((nd, 8, TB), f32),
            pltpu.VMEM((nd, 8, TB), f32),
            pltpu.VMEM((n_row, 2, wide), f32),
            pltpu.VMEM((n_row, 2, wide), f32),
            pltpu.VMEM((2, wide), f32),
            pltpu.VMEM((8, LANES), f32),
            dma((chunks,)),
            dma((nd,)), dma((nd,)),
            dma((n_row + n_col,)), dma((n_row + n_col,)),
            dma((nd,)), dma((nd,)),
            dma((2, nd)), dma((2, nd)),
            dma((nd,)), dma((nd,)),
        ],
        compiler_params=pltpu.CompilerParams(
            collective_id=0, has_side_effects=True, vmem_limit_bytes=56 * 1024 * 1024
        ),
    )(
        tile_list.reshape(2, slots),
        noise_field,
        offsets,
        bead_slot.reshape(1, TB),
        send_cells.reshape(cap, nd),
        spectral.reshape(12, xy, glen),
    )


HALF = PERIOD // 2
FLAT = PERIOD * PERIOD
GROUPS = HALF
MODES = PERIOD**3
PAIRS = ((0, 0), (1, 1), (2, 2), (0, 1), (0, 2), (1, 2))


def lattice_spectrum():
    code = np.arange(PERIOD**3)
    site = np.stack([code // FLAT, code // PERIOD % PERIOD, code % PERIOD])
    disp = (site + PERIOD // 2) % PERIOD - PERIOD // 2
    d = disp.astype(np.float32)
    squares = d[0] * d[0] + d[1] * d[1] + d[2] * d[2]
    scale_sq = np.float32(kernel_range * kernel_range)
    envelope = np.exp(squares * np.float32(-0.5 / scale_sq)) / scale_sq
    table = np.zeros((3, 3, PERIOD**3))
    for a, b in PAIRS:
        element = d[a] * d[b]
        if a == b:
            element = element - squares / np.float32(3.0)
        table[a, b] = (envelope * element).astype(ml_dtypes.bfloat16).astype(np.float64)
        table[b, a] = table[a, b]
    energy = (table * table).sum(axis=1)
    ends = [(x, y) for y in (0, HALF) for x in range(HALF)]
    middle = [(x, y) for y in range(1, HALF) for x in range(PERIOD)]
    turned = [(HALF if x == 0 else x, y) for x, y in ends]
    modes = []
    for part, lead in enumerate((ends, turned)):
        modes += [(x, y, z, part) for z in (0, HALF) for x, y in lead + middle]
    for z in range(1, HALF):
        modes += [(n % PERIOD, n // PERIOD, z, p) for p in range(2) for n in range(FLAT)]
    wave = np.array(modes)
    angle = 2.0 * np.pi / PERIOD * ((wave[:, :3] @ site) % PERIOD)
    alone = (wave[:, :3] % HALF == 0).all(axis=1)
    weight = np.where(alone, 1.0, 2.0) / PERIOD**3
    turn = np.where(wave[:, 3] == 0, 1.0, -1.0)
    rows = [weight * (np.cos(angle) @ table[p]) for p in PAIRS]
    rows += [-turn * weight * (np.sin(angle) @ table[p]) for p in PAIRS[3:]]
    rows += [weight * (np.cos(angle) @ energy[a]) for a in range(3)]
    rows += [np.zeros(MODES)] * (-len(rows) % 8)
    return np.stack(rows).astype(np.float32)


def shared_kernel(
    dims,
    tiles_hbm, noise_hbm, off_hbm, slot_hbm, cells_hbm, spectrum_hbm, spec_hbm,
    out_ref,
    tiles_ref, noise_ref, off_ref, slot_ref, cells_ref,
    spec, pre, hat, phase_a, phase_b, phi, modes, wide, cheb_a, cheb_b, mixer, lattice,
    msg_f, msg, inbox, table, offs, spectrum, last,
    far_send, far_recv,
    load_sem, spec_sem, spectrum_sem, m_ss, m_rs, far_ss, far_rs,
):
    n_row, n_col, slots, xs, ys, glen, cap = dims
    nd = n_row * n_col
    xy = xs * ys
    per_row = LANES // nd
    cr = cap // per_row
    cells_at = 10
    tile_at = cells_at + 2 * cr
    beads = nd * TB
    me_r = lax.axis_index("row")
    me_c = lax.axis_index("col")
    me = me_r * n_col + me_c
    chunks = spec_sem.shape[0]
    part = xy // chunks
    nb = 2 * nd
    rows_t = 3 * nb
    rows_e = rows_t + nd

    def spec_copy(i):
        rows = pl.ds(i * part, part)
        return pltpu.make_async_copy(
            spec_hbm.at[:, rows, :], spec.at[:, rows, :], spec_sem.at[i]
        )

    loads = [
        pltpu.make_async_copy(src, dst, load_sem.at[k])
        for k, (src, dst) in enumerate((
            (cells_hbm, cells_ref), (tiles_hbm, tiles_ref), (noise_hbm, noise_ref),
            (off_hbm, off_ref), (slot_hbm, slot_ref),
        ))
    ]

    peers = sorted(
        [(i, j) for i in range(n_row) for j in range(n_col)], key=lambda t: (-t[1], -t[0])
    )
    others = peers[:-1]

    def place(i, j):
        return jnp.bitwise_xor(me_r, i), jnp.bitwise_xor(me_c, j)

    barrier = pltpu.get_barrier_semaphore()
    for i, j in others:
        r, c = place(i, j)
        pl.semaphore_signal(
            barrier, inc=1, device_id={"row": r, "col": c},
            device_id_type=pl.DeviceIdType.MESH,
        )
    for load in loads:
        load.start()
    for i in range(chunks):
        spec_copy(i).start()
    spectrum_copy = pltpu.make_async_copy(spectrum_hbm, spectrum, spectrum_sem)
    spectrum_copy.start()

    def remote(src, dst, ss, rs, r, c):
        return pltpu.make_async_remote_copy(
            src_ref=src, dst_ref=dst, send_sem=ss, recv_sem=rs,
            device_id={"row": r, "col": c}, device_id_type=pl.DeviceIdType.MESH,
        )

    for load in loads:
        load.wait()
    for a in range(3):
        msg_f[2 * a : 2 * a + 2, :] = noise_ref[a]
    msg_f[6:9, :] = off_ref[...].astype(f32)
    msg_f[9:10, :] = slot_ref[...].astype(f32)
    spread = over(iota((nd, LANES), 1), per_row) == iota((nd, LANES), 0)
    spread = spread.astype(f32).astype(bf16)
    keep = (iota((cap, LANES), 1) & (per_row - 1)) == (iota((cap, LANES), 0) & (per_row - 1))
    cells = cells_ref[...]
    for h, half_cell in enumerate((over(cells, 512), (cells & 511) - 256)):
        out = dot(half_cell.astype(f32).astype(bf16), spread)
        out = jnp.sum(jnp.where(keep, out, 0.0).reshape(cr, per_row, LANES), axis=1)
        msg_f[cells_at + h * cr : cells_at + (h + 1) * cr, :] = out
    lane_row = iota((1, LANES), 1)
    row_list = jnp.zeros((1, LANES), jnp.int32)
    col_list = jnp.zeros((1, LANES), jnp.int32)
    for s in range(slots):
        here = lane_row == me * slots + s
        tr, tc = tiles_ref[0, s], tiles_ref[1, s]
        row_list = jnp.where(
            here & (jnp.full((1, LANES), tr) >= 0), me_r * n_col + tr + 1, row_list
        )
        col_list = jnp.where(here, tc * n_col + me_c + 1, col_list)
    msg_f[tile_at : tile_at + 1, :] = row_list.astype(f32)
    msg_f[tile_at + 1 : tile_at + 2, :] = col_list.astype(f32)
    if tile_at + 2 < msg_f.shape[0]:
        msg_f[tile_at + 2 :, :] = jnp.zeros((msg_f.shape[0] - tile_at - 2, LANES), f32)
    msg[...] = msg_f[...].astype(bf16)
    inbox[me] = msg_f[...].astype(bf16)

    pl.semaphore_wait(barrier, nd - 1)

    def msg_copy(i, j):
        r, c = place(i, j)
        p = i * n_col + j
        return remote(msg, inbox.at[me], m_ss.at[p], m_rs.at[me], r, c)

    def msg_arrive(i, j):
        r, c = place(i, j)
        p = r * n_col + c
        remote(msg, inbox.at[p], m_ss.at[0], m_rs.at[p], r, c).wait_recv()

    for i, j in others:
        msg_copy(i, j).start()

    gj = iota((2 * glen, 2 * glen), 0)
    gi = iota((2 * glen, 2 * glen), 1)
    zi, zj = gi & (glen - 1), gj & (glen - 1)
    in_im, out_im = gi >= glen, gj >= glen
    half = glen // 2
    same = zi == zj
    mirror = (zi + zj == glen) & (zi != zj)
    even = zj <= half
    plain = in_im == out_im
    fold = jnp.where(
        even,
        jnp.where(plain & (same | mirror), 1.0, 0.0),
        jnp.where(
            plain,
            0.0,
            jnp.where(same, 1.0, 0.0) - jnp.where(mirror, 1.0, 0.0),
        )
        * jnp.where(out_im, -1.0, 1.0),
    ).astype(bf16)

    width_sq = (glen / 8.0) ** 2
    front = math.sqrt(1.5) / (2.0 * math.pi * width_sq) ** 0.75

    def signed(n):
        return jnp.where(n < half, n, n - glen).astype(f32)

    ky = signed(me_c * ys + iota((ys, glen), 0))
    kz = signed(iota((ys, glen), 1))
    kyz_sq = ky * ky + kz * kz

    def hat_block(i, first):
        kx = signed(me_r * xs + i)
        q = kx * kx + kyz_sq
        amp = jnp.where(q > 0, front * jnp.exp(q * (-0.25 / width_sq)), 0.0)
        damp = amp / jnp.maximum(q, 1.0)
        rows = pl.ds(pl.multiple_of(i * ys, ys), ys)
        at = pl.multiple_of((i - first) * ys, ys)
        waves = (kx, ky, kz)
        for v in range(2):
            for p in range(2):
                s = [spec[(p * 3 + a) * 2 + v, rows, :] for a in range(3)]
                along = (kx * s[0] + ky * s[1] + kz * s[2]) * damp
                for a in range(3):
                    pre[pl.ds((a * 2 + v) * part + at, ys), p * glen : (p + 1) * glen] = (
                        amp * s[a] - waves[a] * along
                    ).astype(bf16)
        return first

    per = part // ys
    for i in range(chunks):
        spec_copy(i).wait()
        lax.fori_loop(i * per, (i + 1) * per, hat_block, i * per)
        for k in range(6):
            folded = dot_nt(fold, pre[k * part : (k + 1) * part, :]).astype(bf16)
            for p in range(2):
                hat[
                    k * glen : (k + 1) * glen, p * xy + i * part : p * xy + (i + 1) * part
                ] = folded[p * glen : (p + 1) * glen, :]

    spectrum_copy.wait()
    for i, j in others[::-1]:
        msg_arrive(i, j)

    row_list = jnp.zeros((1, LANES), f32)
    col_list = jnp.zeros((1, LANES), f32)
    slot_rows = nb // 2 * cr
    for o in range(nd):
        got = inbox[o].astype(f32)
        row_list = row_list + got[tile_at : tile_at + 1]
        col_list = col_list + got[tile_at + 1 : tile_at + 2]
        for h in range(2):
            table[h, o * cr : (o + 1) * cr, :] = got[
                cells_at + h * cr : cells_at + (h + 1) * cr
            ]
        offs[:, o * TB : (o + 1) * TB] = got[6:9]
        for a in range(3):
            cheb_a[a, o] = got[2 * a : 2 * a + 2]
    tables = []
    for h in range(2):
        tables.append(jnp.transpose(table[h])[:, :slot_rows])
    for h in range(2):
        table[2 + h, :, :slot_rows] = tables[h]

    line = iota((nb + nd, LANES), 0)
    target = jnp.where(line < nb, over(line, 2), line - nb) + 1
    to = (target.astype(f32) == row_list).astype(f32).astype(bf16)
    source = iota((LANES, LANES), 0) + 1
    frm = (source.astype(f32) == col_list).astype(f32).astype(bf16)
    joined = dot_nt(to, frm)
    odd = (iota((nb, TB), 0) & 1) == 1

    def fill(o, a, values):
        lanes = slice(o * TB, (o + 1) * TB)
        spread = jnp.where(odd, values[1:2], values[0:1])
        wide[a * nb : (a + 1) * nb, lanes] = (mixer[0:nb, lanes] * spread).astype(bf16)

    for o in range(nd):
        lanes = slice(o * TB, (o + 1) * TB)
        mixer[:, lanes] = jnp.broadcast_to(joined[:, o : o + 1], (nb + nd, TB))
        wide[rows_t:rows_e, lanes] = mixer[nb:, lanes].astype(bf16)
        for a in range(3):
            fill(o, a, cheb_a[a, o])

    def build_phi(o):
        lanes = slice(o * TB, (o + 1) * TB)
        q = iota((PERIOD, TB), 0).astype(f32) * (1.0 / PERIOD)
        co, si = [], []
        for a in range(3):
            turn = q * offs[a : a + 1, lanes]
            co.append(cos_turn(turn))
            si.append(cos_turn(turn - 0.25))
        flat_c, flat_s = [], []
        for y in range(PERIOD):
            cy, sy = co[1][y : y + 1], si[1][y : y + 1]
            flat_c.append(cy * co[0] - sy * si[0])
            flat_s.append(sy * co[0] + cy * si[0])
        line = iota((PERIOD, TB), 0)

        def ends(first, second):
            return jnp.where(line < HALF, first, pltpu.roll(second, HALF, 0))

        sides = [
            jnp.where(line == 0, pltpu.roll(flat_c[y], HALF, 0), flat_s[y]) for y in (0, HALF)
        ]
        real = jnp.concatenate([ends(flat_c[0], flat_c[HALF])] + flat_c[1:HALF], axis=0)
        imag = jnp.concatenate([ends(*sides)] + flat_s[1:HALF], axis=0)
        flip = co[2][HALF : HALF + 1]
        blocks = [jnp.concatenate([real, real * flip, imag, imag * flip], axis=0)]
        flat_c = jnp.concatenate(flat_c, axis=0)
        flat_s = jnp.concatenate(flat_s, axis=0)
        for z in range(1, HALF):
            cz, sz = co[2][z : z + 1], si[2][z : z + 1]
            blocks.append(
                jnp.concatenate([flat_c * cz - flat_s * sz, flat_s * cz + flat_c * sz], axis=0)
            )
        for g, block in enumerate(blocks):
            at = g * 2 * FLAT
            phi[at : at + 2 * FLAT, lanes] = block.astype(bf16)
            modes[lanes, at : at + 2 * FLAT] = jnp.transpose(block).astype(bf16)

    y_slab, z_slab = glen // n_row, glen // n_col
    scaled = 1.0 / glen

    def locate(r, c):
        o = r * n_col + c
        code = inbox[o].astype(f32)[9:10].astype(jnp.int32)
        slot = over(code, nd)
        holder = code & (nd - 1)
        row_at = holder * cr + over(slot, per_row)
        hot = (iota((slot_rows, TB), 0) == row_at).astype(f32).astype(bf16)
        at = pl.ds(pl.multiple_of(o * per_row, per_row), per_row)
        lists = jnp.concatenate(
            [table[2, at, :slot_rows], table[3, at, :slot_rows]], axis=0
        ).astype(bf16)
        found = dot(lists, hot)
        mine = iota((per_row, TB), 0) == (slot & (per_row - 1))
        high = jnp.sum(jnp.where(mine, found[:per_row], 0.0), axis=0, keepdims=True)
        low = jnp.sum(jnp.where(mine, found[per_row:], 0.0), axis=0, keepdims=True)
        cell = high.astype(jnp.int32) * 512 + low.astype(jnp.int32) + 256
        pos_x = over(cell, y_slab * z_slab)
        pos_y = over(holder, n_col) * y_slab + (over(cell, z_slab) & (y_slab - 1))
        pos_z = (holder & (n_col - 1)) * z_slab + (cell & (z_slab - 1))
        return [p.astype(f32) * scaled for p in (pos_x, pos_y, pos_z)]

    kx_col = (me_r * xs + iota((xs, 2 * TB), 0)).astype(f32)
    ky_col = (me_c * ys + iota((ys, 2 * TB), 0)).astype(f32)
    kz_col = iota((glen, 2 * TB), 0)

    def build_phase(pair, phase):
        spots = [locate(*place(i, j)) for i, j in pair]
        px, py, pz = (
            jnp.concatenate([spots[0][t], spots[1][t]], axis=1) for t in range(3)
        )
        turn = kx_col * px
        cx, nx = cos_turn(turn), cos_turn(turn + 0.25)
        turn = ky_col * py
        cy, ny = cos_turn(turn), cos_turn(turn + 0.25)
        cx, nx, cy, ny = (t.astype(bf16) for t in (cx, nx, cy, ny))
        for i in range(xs):
            a, b = cx[i : i + 1], nx[i : i + 1]
            phase[i * ys : (i + 1) * ys, :] = (a * cy - b * ny).astype(bf16)
            phase[xy + i * ys : xy + (i + 1) * ys, :] = (b * cy + a * ny).astype(bf16)
        return cos_turn(kz_col.astype(f32) * pz + jnp.where(kz_col > half, 0.25, 0.0))

    def far_copy(i, j):
        r, c = place(i, j)
        p = r * n_col + c
        q = i * n_col + j
        return remote(far_send.at[q], far_recv.at[me], far_ss.at[q], far_rs.at[me], r, c)

    def far_sums(pair, phase, tz):
        sums = dot(hat[...], phase[...])
        for k in range(6):
            line = jnp.sum(sums[k * glen : (k + 1) * glen] * tz, axis=0, keepdims=True)
            for t, (i, j) in enumerate(pair):
                half_line = line[:, t * TB : (t + 1) * TB]
                if i + j:
                    far_send[i * n_col + j, k : k + 1, :] = half_line
                else:
                    far_recv[me, k : k + 1, :] = half_line

    def far_start(some):
        for i, j in some:
            if i + j:
                far_copy(i, j).start()

    near = [cheb_coef[0] * noise_ref[a] for a in range(3)]
    scales = []

    band = 2 * LANES
    bands = [slice(t, t + band) for t in range(0, MODES, band)]

    def to_modes(m):
        rows = rows_e if m == 0 else rows_t
        for lanes in bands:
            sums = dot(wide[0:rows, :], modes[:, lanes])
            turned = jnp.concatenate(
                [
                    pltpu.roll(sums[0:rows_t, g * LANES : (g + 1) * LANES], FLAT, 1)
                    for g in range(band // LANES)
                ],
                axis=1,
            )
            for a in range(3):
                total = spectrum[a : a + 1, lanes] * sums[a * nb : (a + 1) * nb]
                for b in range(3):
                    if a != b:
                        e = PAIRS.index((min(a, b), max(a, b)))
                        total = total + spectrum[e : e + 1, lanes] * sums[b * nb : (b + 1) * nb]
                        total = total + (
                            spectrum[e + 3 : e + 4, lanes] * turned[b * nb : (b + 1) * nb]
                        )
                lattice[a * nb : (a + 1) * nb, lanes] = total.astype(bf16)
            if m == 0:
                for a in range(3):
                    total = spectrum[9 + a : 10 + a, lanes] * sums[rows_t:rows_e]
                    high = total.astype(bf16)
                    at = rows_t + a * nd
                    lattice[at : at + nd, lanes] = high
                    lattice[at + 3 * nd : at + 4 * nd, lanes] = (
                        total - high.astype(f32)
                    ).astype(bf16)

    def to_beads(m):
        if m == 0:
            out = dot(lattice[...], phi[...])
            energy = out[rows_t : rows_t + 3 * nd] + out[rows_t + 3 * nd :]
            top = jnp.zeros((3 * nd, TB), f32)
            owner = iota((3 * nd, TB), 0) & (nd - 1)
            for o in range(nd):
                top = jnp.maximum(
                    top, jnp.where(owner == o, energy[:, o * TB : (o + 1) * TB], 0.0)
                )
            top = jnp.max(jnp.max(top, axis=1, keepdims=True), axis=0, keepdims=True)
            scales.append(jnp.broadcast_to(1.0 / jnp.sqrt(top + 1e-06), (2, TB)))
        elif m < DEGREES - 1:
            out = dot(lattice[0:rows_t, :], phi[...])
        scale = scales[0]
        before = cheb_b if m % 2 == 0 else cheb_a
        if m < DEGREES - 1:
            for o in range(nd):
                for a in range(3):
                    at = a * nb + 2 * o
                    got = scale * out[at : at + 2, o * TB : (o + 1) * TB]
                    if m > 0:
                        got = 2.0 * got - before[a, o]
                    before[a, o] = got
                    fill(o, a, got)
            for a in range(3):
                near[a] = near[a] + cheb_coef[m + 1] * before[a, me]
        else:
            last[...] = dot(
                lattice[0:rows_t, :], phi[:, pl.ds(pl.multiple_of(me * TB, TB), TB)]
            )
            for a in range(3):
                got = 2.0 * (scale * last[pl.ds(a * nb + 2 * me, 2), :])
                near[a] = near[a] + cheb_coef[m + 1] * (got - before[a, me])

    stages = [
        functools.partial(stage, m)
        for m in range(DEGREES) for stage in (to_modes, to_beads)
    ]
    pairs = [peers[t : t + 2] for t in range(0, nd, 2)]
    phases = (phase_a, phase_b)
    built = -(-3 * len(pairs) // 8)
    sends = (len(pairs) - 3, len(pairs) - 1)
    held = []
    tz = build_phase(pairs[0], phase_a)
    for n, pair in enumerate(pairs):
        nxt = None
        if n + 1 < len(pairs):
            nxt = build_phase(pairs[n + 1], phases[(n + 1) % 2])
        if n >= built and False:
            stages.pop(0)()
        far_sums(pair, phases[n % 2], tz)
        tz = nxt
        held += pair
        if n in sends:
            far_start(held)
            held = []
        if n < built:
            for o in range(n * nd // built, (n + 1) * nd // built):
                build_phi(o)
    for stage in stages:
        stage()

    for i, j in others:
        msg_copy(i, j).wait_send()

    def far_arrive(i, j):
        r, c = place(i, j)
        p = r * n_col + c
        remote(far_send.at[0], far_recv.at[p], far_ss.at[0], far_rs.at[p], r, c).wait_recv()

    for i, j in others:
        far_arrive(i, j)
    for i, j in others:
        far_copy(i, j).wait_send()
    far = far_recv[0]
    for p in range(1, nd):
        far = far + far_recv[p]
    for a in range(3):
        out_ref[a] = near[a] + far[2 * a : 2 * a + 2, :]


def shared_device(noise_field, offsets, tile_list, send_cells, bead_slot, spectral):
    n_row = lax.axis_size("row")
    n_col = lax.axis_size("col")
    nd = n_row * n_col
    xs, ys, glen = spectral.shape[3:]
    slots = tile_list.shape[3]
    cap = send_cells.shape[2]
    xy = xs * ys
    cr = cap * nd // LANES
    msg_rows = -(-(12 + 2 * cr) // 16) * 16
    chunks = 4 if xy % 256 == 0 else 1
    dims = (n_row, n_col, slots, xs, ys, glen, cap)
    vmem = pl.BlockSpec(memory_space=pltpu.VMEM)
    hbm = pl.BlockSpec(memory_space=pl.ANY)
    dma = pltpu.SemaphoreType.DMA
    rows_t = 6 * nd
    spectrum = lattice_spectrum()
    return pl.pallas_call(
        functools.partial(shared_kernel, dims),
        out_shape=pltpu.VMEM(noise_field.shape, f32),
        in_specs=[hbm] * 7,
        out_specs=vmem,
        scratch_shapes=[
            pltpu.SMEM((2, slots), jnp.int32),
            pltpu.VMEM(noise_field.shape, f32),
            pltpu.VMEM(offsets.shape, jnp.int32),
            pltpu.VMEM((1, TB), jnp.int32),
            pltpu.VMEM((cap, nd), jnp.int32),
            pltpu.VMEM((12, xy, glen), f32),
            pltpu.VMEM((6 * (xy // chunks), 2 * glen), bf16),
            pltpu.VMEM((6 * glen, 2 * xy), bf16),
            pltpu.VMEM((2 * xy, 2 * TB), bf16),
            pltpu.VMEM((2 * xy, 2 * TB), bf16),
            pltpu.VMEM((MODES, nd * TB), bf16),
            pltpu.VMEM((nd * TB, MODES), bf16),
            pltpu.VMEM((rows_t + nd, nd * TB), bf16),
            pltpu.VMEM((3, nd, 2, TB), f32),
            pltpu.VMEM((3, nd, 2, TB), f32),
            pltpu.VMEM((3 * nd, nd * TB), f32),
            pltpu.VMEM((rows_t + 6 * nd, MODES), bf16),
            pltpu.VMEM((msg_rows, LANES), f32),
            pltpu.VMEM((msg_rows, LANES), bf16),
            pltpu.VMEM((nd, msg_rows, LANES), bf16),
            pltpu.VMEM((4, LANES, LANES), f32),
            pltpu.VMEM((3, nd * TB), f32),
            pltpu.VMEM(spectrum.shape, f32),
            pltpu.VMEM((rows_t, TB), f32),
            pltpu.VMEM((nd, 8, TB), f32),
            pltpu.VMEM((nd, 8, TB), f32),
            dma((5,)), dma((chunks,)), dma,
            dma((nd,)), dma((nd,)),
            dma((nd,)), dma((nd,)),
        ],
        compiler_params=pltpu.CompilerParams(
            collective_id=1, has_side_effects=True, vmem_limit_bytes=56 * 1024 * 1024
        ),
    )(
        tile_list.reshape(2, slots),
        noise_field,
        offsets,
        bead_slot.reshape(1, TB),
        send_cells.reshape(cap, nd),
        jnp.asarray(spectrum),
        spectral.reshape(12, xy, glen),
    )


def power_of_two(n):
    return n & (n - 1) == 0


def per_device(noise_field, offsets, tile_list, send_cells, bead_slot, spectral):
    n_row = lax.axis_size("row")
    n_col = lax.axis_size("col")
    nd = n_row * n_col
    xs, ys, glen = spectral.shape[3:]
    cap = send_cells.shape[2]
    fits = (
        8 <= nd <= 16
        and power_of_two(n_row)
        and power_of_two(n_col)
        and power_of_two(glen)
        and nd * tile_list.shape[3] <= LANES
        and cap % (LANES // nd) == 0
        and cap * nd <= 256
        and glen * (glen // n_row) * (glen // n_col) <= 1 << 17
        and ys % 16 == 0
    )
    run = shared_device if fits else spread_device
    return run(noise_field, offsets, tile_list, send_cells, bead_slot, spectral)


def solution(mesh):
    return jax.shard_map(
        per_device,
        mesh=mesh,
        in_specs=(
            P(None, None, ("groups", "row", "col")),
            P(None, ("groups", "row", "col")),
            P(("groups", "row"), "col", None, None),
            P(("groups", "row"), "col", None, None),
            P(("groups", "row", "col")),
            P(None, None, None, ("groups", "row"), "col", None),
        ),
        out_specs=P(None, None, ("groups", "row", "col")),
        check_vma=False,
    )
```
